256 devices in a mesh: sec: 4 (over z_lo, core), lat: 16 (over x, y), col: 4 (over z_hi).
Axes of the slice: x: 4, y: 4, z: 8 (z_hi: 4, z_lo: 2; z = z_hi * 2 + z_lo), core: 2. Of those that a mesh axis runs over, the one named last changes fastest.
Arguments:
- state: float32 [1, 4, 28, 192, 384], P(None, 'sec', None, 'lat', 'col'), may hold values from -6 to 6
- forcing: float32 [1, 4, 28, 192, 384], P(None, 'sec', None, 'lat', 'col'), may hold values from -4 to 4
- crm_moisture: bfloat16 [1, 32, 28, 64, 4, 288], P(None, None, None, ('sec', 'lat'), 'col'), may hold values from -6 to 6
- cloud_order: int32 [4, 16, 1152], P('col', 'lat'), may hold values from 0 to 1151, each once within a row
- wave_table: int32 [128], replicated, may hold values from 0 to 127, each once
Outputs:
- state_out: float32 [1, 4, 28, 192, 384], P(None, 'sec', None, 'lat', 'col')
- spectral: float32 [4, 1, 28, 128, 2, 128], P('sec', None, 'col', 'lat')
The draws below stay inside these ranges and needn't reach their ends.
Inputs may be any that keep to these rules, and one draw needn't show every extreme that they name: `cloud_order`: every row lists each of the 1152 columns of a band block once. `wave_table`: each wavenumber stands in exactly one slot.
All inputs are finite; a program needn't handle non-finite values.
Results may differ from the reference program's by a relative error of at most 0.0003.
Values sent between devices are 32-bit elements; how exact they have to be, the bound alone decides.
No kernel may reach another device: no remote copies, remote signals or barrier semaphores. Data moves between devices by JAX's collectives and lax.ppermute only.
A program may use at most 64 MiB of HBM per device.

```python
import math
import jax
import jax.numpy as jnp
from jax import lax

NLON = 384
NLAT = 192
L = 28
F = 4
MMAX = 128
NCRM = 32
NSUB = 4
ENS = 1
LON_BLOCK = 96
BLOCK_COLS = 1152
TARGETS = 64
PER_TARGET = 18
RUN_COLS = 288
N_LAT = 16
N_COL = 4


def block_levels(stream_key, dims, shards, least, top_value):
    def one(dim, blocks):
        draws = jax.random.uniform(jax.random.fold_in(jax.random.fold_in(stream_key, 6), dim), (blocks,), jnp.float32, least / len(shards), top_value / len(shards))
        return jnp.repeat(jnp.exp(draws), dims[dim] // blocks).reshape((-1,) + (1,) * (len(dims) - dim - 1))

    level = one(*shards[0])
    for cut in shards[1:]:
        level = level * one(*cut)
    return level


def normal_values(rng, dims, width, reach, shards=(), held_as=jnp.bfloat16):
    factor_of = block_levels(rng, dims, shards, -0.22, 0.18) if shards else 1.0
    values = jax.random.normal(rng, dims, jnp.float32) * width * factor_of
    return jnp.minimum(jnp.maximum(values, -reach), reach).astype(held_as)


def setup_inputs(seed: int = 0) -> dict:
    splits = jax.random.split(jax.random.key(seed), 6)
    state = normal_values(splits[0], (ENS, F, L, NLAT, NLON), 1.0, 6.0, ((1, 4), (3, 16), (4, 4)), jnp.float32)
    forcing = normal_values(splits[1], (ENS, F, L, NLAT, NLON), 0.5, 4.0, ((1, 4), (3, 16), (4, 4)), jnp.float32)
    crm_moisture = normal_values(splits[2], (ENS, NCRM, L, TARGETS, N_COL, RUN_COLS), 1.0, 6.0, ((3, 64), (4, 4)))
    cloud_order = jax.vmap(lambda own: jax.random.permutation(own, BLOCK_COLS))(jax.random.split(splits[3], N_COL * N_LAT)).reshape((N_COL, N_LAT, BLOCK_COLS)).astype(jnp.int32)
    wave_table = jax.random.permutation(splits[4], MMAX).astype(jnp.int32)
    return dict(state=state, forcing=forcing, crm_moisture=crm_moisture, cloud_order=cloud_order, wave_table=wave_table)


COURANT_SCALE = 0.4
CONDENSE = 0.5

def transport(values, courant, mixing):
    forward = jnp.roll(values, -1, axis=0)
    behind = jnp.roll(values, 1, axis=0)
    return -0.5 * courant * (forward - behind) + mixing * (forward - 2.0 * values + behind)

def cloud_model(vertical_state_stack, forcing, vapour_mass_fraction):
    wind_u = vertical_state_stack[0]
    wind_v = vertical_state_stack[1]
    atmospheric_warmth = vertical_state_stack[2]
    humidity = vertical_state_stack[3]
    courant = COURANT_SCALE * jnp.tanh(wind_u)
    mixing = 0.2 + 0.5 * jnp.abs(courant)
    convective_warming_rate = jnp.broadcast_to(atmospheric_warmth, vapour_mass_fraction.shape)
    crm_water = humidity + vapour_mass_fraction
    start_water = crm_water
    ground_precipitation = jnp.zeros_like(atmospheric_warmth)
    for substep in range(NSUB):
        heat_move = transport(convective_warming_rate, courant, mixing)
        water_move = transport(crm_water, courant, mixing)
        condensed = CONDENSE * jnp.maximum(crm_water - convective_warming_rate, 0.0)
        convective_warming_rate = convective_warming_rate + heat_move + condensed + forcing[2] / NSUB
        crm_water = crm_water + water_move - condensed + forcing[3] / NSUB
        ground_precipitation = ground_precipitation + lax.optimization_barrier(jnp.mean(condensed, axis=0))
    ground_precipitation = ground_precipitation / NSUB
    zonal_velocity_rate = -ground_precipitation * wind_u + forcing[0]
    meridional_velocity_rate = -ground_precipitation * wind_v + forcing[1]
    warming_rate_change = lax.optimization_barrier(jnp.mean(convective_warming_rate, axis=0)) - atmospheric_warmth
    vapour_rate_change = lax.optimization_barrier(jnp.mean(crm_water - start_water, axis=0))
    return jnp.stack((zonal_velocity_rate, meridional_velocity_rate, warming_rate_change, vapour_rate_change))

def trig_table(longitudes, wave_numbers):
    phase = (longitudes[:, None] * wave_numbers[None, :] % NLON).astype(jnp.float32) * (2.0 * math.pi / NLON)
    return jnp.stack((jnp.cos(phase), jnp.sin(phase)), axis=1) / math.sqrt(NLON)

def legendre_table(orders):
    colatitude = (jnp.arange(NLAT, dtype=jnp.int32).astype(jnp.float32) + 0.5) * (math.pi / NLAT)
    cosine = jnp.cos(colatitude)[None, :]
    sine_lat = jnp.sin(colatitude)
    order_col = orders.astype(jnp.float32)[:, None]
    log_diag = 0.5 * (lax.lgamma(order_col + 1.5) - lax.lgamma(jnp.float32(1.5)) - lax.lgamma(order_col + 1.0))
    log_diag = log_diag + order_col * jnp.log(sine_lat)[None, :] - 0.5 * math.log(2.0)
    diagonal = jnp.exp(log_diag)
    empty = jnp.zeros_like(diagonal)

    def march_forward(carried, degree):
        previous, current = carried
        deg_float = degree.astype(jnp.float32)
        active = deg_float > order_col
        numerator = jnp.where(active, 4.0 * deg_float * deg_float - 1.0, 1.0)
        bottom = jnp.where(active, deg_float * deg_float - order_col * order_col, 1.0)
        lower_deg = deg_float - 1.0
        retreat = jnp.sqrt(jnp.maximum(lower_deg * lower_deg - order_col * order_col, 0.0) / (4.0 * lower_deg * lower_deg - 1.0))
        grown = jnp.sqrt(numerator / bottom) * (cosine * current - retreat * previous)
        fresh_row = jnp.where(active, grown, jnp.where(deg_float == order_col, diagonal, 0.0))
        return ((current, fresh_row), fresh_row)
    _, legendre_rows = lax.scan(march_forward, (empty, empty), jnp.arange(MMAX, dtype=jnp.int32), unroll=8)
    weights = sine_lat / math.sqrt(NLAT)
    return legendre_rows * weights[None, None, :]

def reference(state, forcing, crm_moisture, cloud_order, wave_table):
    updated = []
    for member in range(ENS):
        member_state = state[member]
        member_force = forcing[member]
        member_moist = crm_moisture[member]

        def per_group(col_group):
            lon_start = col_group * LON_BLOCK
            grid_block = lax.dynamic_slice_in_dim(member_state, lon_start, LON_BLOCK, 3).reshape(F, L, N_LAT, BLOCK_COLS)
            force_block = lax.dynamic_slice_in_dim(member_force, lon_start, LON_BLOCK, 3).reshape(F, L, N_LAT, BLOCK_COLS)
            col_order = lax.dynamic_index_in_dim(cloud_order, col_group, 0, keepdims=False)

            def to_slots(values):
                chosen = jnp.take_along_axis(values, jnp.broadcast_to(col_order[None, None], values.shape), axis=3)
                chosen = chosen.reshape(F, L, N_LAT, TARGETS, PER_TARGET).transpose(0, 1, 3, 2, 4)
                return chosen.reshape(F, L, TARGETS * RUN_COLS)
            vapour_mass_fraction = lax.dynamic_index_in_dim(member_moist, col_group, 3, keepdims=False)
            vapour_mass_fraction = vapour_mass_fraction.astype(jnp.float32).reshape(NCRM, L, TARGETS * RUN_COLS)
            tendencies = cloud_model(to_slots(grid_block), to_slots(force_block), vapour_mass_fraction)
            tendencies = tendencies.reshape(F, L, TARGETS, N_LAT, PER_TARGET).transpose(0, 1, 3, 2, 4)
            tendencies = tendencies.reshape(F, L, N_LAT, BLOCK_COLS)
            inverse = jnp.argsort(col_order, axis=1).astype(jnp.int32)
            restored = jnp.take_along_axis(tendencies, jnp.broadcast_to(inverse[None, None], tendencies.shape), axis=3)
            return restored.reshape(F, L, NLAT, LON_BLOCK)
        pieces = lax.map(per_group, jnp.arange(N_COL, dtype=jnp.int32))
        column_tend = pieces.transpose(1, 2, 3, 0, 4).reshape(F, L, NLAT, NLON)
        updated.append(member_state + column_tend)
    new_state = jnp.stack(updated)
    trig_rows = trig_table(jnp.arange(NLON, dtype=jnp.int32), wave_table)
    fourier = jnp.einsum('eflay,ycs->eflacs', new_state, trig_rows, precision=lax.Precision.HIGHEST)
    weighted = legendre_table(wave_table)
    spectral = jnp.einsum('eflacs,nsa->felscn', fourier, weighted, precision=lax.Precision.HIGHEST)
    return (new_state, spectral)
```

```python
import math

import jax
import jax.numpy as jnp
import numpy as np
from jax import lax
from jax.experimental import pallas as pl
from jax.experimental.pallas import tpu as pltpu
from jax.sharding import PartitionSpec as P

NLON = 384
NLAT = 192
MMAX = 128
NSUB = 4
NCRM = 32
LEVELS = 28
BAND = 12
LONS = 96
COLS = BAND * LONS
ROWS = LEVELS * BAND
TARGETS = 64
PER = 18
NL = 16
NS = 4
NC = 4
RUNS = NL * PER
LEV_OWN = LEVELS // NC
SLOTS_OWN = MMAX // NL

F32 = jnp.float32
BF16 = jnp.bfloat16
VMEM = pl.BlockSpec(memory_space=pltpu.VMEM)
SMEM = pl.BlockSpec(memory_space=pltpu.SMEM)


def split2(x):
    hi = x.astype(BF16)
    lo = (x - hi.astype(F32)).astype(BF16)
    return hi, lo


def params(mib=24):
    return pltpu.CompilerParams(vmem_limit_bytes=mib << 20)


def lanes_of(shape):
    return lax.broadcasted_iota(jnp.int32, shape, 1)


def fill_one_hot(order_ref, hot_ref):
    order = order_ref[...]
    step = 96
    for c in range(0, COLS, step):
        ids = lax.broadcasted_iota(jnp.int32, (step, COLS), 0) + c
        hot_ref[c : c + step, :] = jnp.where(ids == order, 1.0, 0.0).astype(BF16)


def pack_kernel(state_ref, force_ref, order_ref, out_ref, hot_ref, cols_ref):
    fill_one_hot(order_ref, hot_ref)
    for ref, base in ((state_ref, 0), (force_ref, LEVELS)):
        rows = ref[...].reshape(LEVELS, BAND, LONS)
        for b in range(BAND):
            cols_ref[base : base + LEVELS, b * LONS : (b + 1) * LONS] = rows[:, b, :]
    hi, lo = split2(cols_ref[...])
    both = jnp.concatenate((hi, lo), axis=0)
    got = jnp.dot(both, hot_ref[...], preferred_element_type=F32)
    got = got[: 2 * LEVELS] + got[2 * LEVELS :]
    lane = lanes_of((8, 128))
    groups = 2 * LEVELS // 8
    for t in range(TARGETS):
        v, off = divmod(t * PER, 128)
        tile = None
        for q in range(groups):
            src = got[q * 8 : q * 8 + 8, v * 128 : v * 128 + 128]
            if off + PER > 128:
                nxt = got[q * 8 : q * 8 + 8, v * 128 + 128 : v * 128 + 256]
                src = jnp.where(lane < off, nxt, src)
            shift = (q * PER - off) % 128
            if shift:
                src = pltpu.roll(src, shift, 1)
            tile = src if tile is None else jnp.where(lane >= q * PER, src, tile)
        out_ref[t] = tile


def gather_lanes(tile_of, q_list, first, count, width, store):
    lane = lanes_of((8, 128))
    for q in q_list:
        for v in range(pl.cdiv(width, 128)):
            acc = None
            for i in range(count):
                start = i * PER - v * 128
                if start >= 128 or start + PER <= 0:
                    continue
                src = tile_of(first + i)
                shift = (i * PER - q * PER) % 128
                if shift:
                    src = pltpu.roll(src, shift, 1)
                acc = src if acc is None else jnp.where(lane >= start, src, acc)
            store(q, v, acc)


def cloud_kernel(got_ref, moist_ref, out_ref, wind_ref, diff_ref, left_ref, right_ref, rain_ref):
    def store_wind(q, v, x):
        wind_ref[q * 8 : q * 8 + 8, v * 128 : v * 128 + 128] = x

    def store_diff(q, v, x):
        diff_ref[q * 8 : q * 8 + 8, v * 128 : v * 128 + 128] = x

    gather_lanes(lambda i: got_ref[i], range(4), 0, NL, RUNS, store_wind)
    cache = {}

    def diff(i):
        if i not in cache:
            cache[i] = got_ref[3 * NL + i] - got_ref[2 * NL + i]
        return cache[i]

    gather_lanes(diff, range(7), 0, NL, RUNS, store_diff)
    courant = 0.4 * jnp.tanh(wind_ref[...])
    mixing = 0.2 + 0.5 * jnp.abs(courant)
    left_ref[...] = mixing - 0.5 * courant
    right_ref[...] = mixing + 0.5 * courant
    rain_ref[...] = jnp.zeros_like(rain_ref)

    def level(k, carry):
        row = (pl.ds(k, 1), slice(0, RUNS))
        gap = diff_ref[row] + moist_ref[k].astype(F32)
        push = diff_ref[pl.ds(k + LEVELS, 1), 0:RUNS] * (1.0 / NSUB)
        ahead = left_ref[row]
        behind = right_ref[row]
        both = ahead + behind
        wet = jnp.maximum(gap, 0.0)
        for _ in range(NSUB - 1):
            up = pltpu.roll(gap, NCRM - 1, 0)
            down = pltpu.roll(gap, 1, 0)
            gap = (jnp.minimum(gap, 0.0) - both * gap) + (ahead * up + behind * down) + push
            wet = wet + jnp.maximum(gap, 0.0)
        rain_ref[pl.ds(k, 1), 0:RUNS] = jnp.sum(wet, axis=0, keepdims=True) * (0.5 / NCRM)
        return carry

    lax.fori_loop(0, LEVELS, level, 0)
    lane = lanes_of((8, 128))
    for i in range(NL):
        v, off = divmod(i * PER, 128)
        tile = None
        for q in range(4):
            src = rain_ref[q * 8 : q * 8 + 8, v * 128 : v * 128 + 128]
            if off + PER > 128:
                nxt = rain_ref[q * 8 : q * 8 + 8, v * 128 + 128 : v * 128 + 256]
                src = jnp.where(lane < off, nxt, src)
            shift = (q * PER - off) % 128
            if shift:
                src = pltpu.roll(src, shift, 1)
            tile = src if tile is None else jnp.where(lane >= q * PER, src, tile)
        for s in range(NS):
            out_ref[s * NL + i] = tile


def update_kernel(got_ref, order_ref, state_ref, force_ref, coef_ref, out_ref, hot_ref, slots_ref, rain_ref):
    fill_one_hot(order_ref, hot_ref)

    def store(q, v, x):
        slots_ref[q * 8 : q * 8 + 8, v * 128 : v * 128 + 128] = x

    gather_lanes(lambda i: got_ref[i], range(4), 0, TARGETS, COLS, store)
    hi, lo = split2(slots_ref[...])
    both = jnp.concatenate((hi, lo), axis=0)
    back = lax.dot_general(both, hot_ref[...], (((1,), (1,)), ((), ())), preferred_element_type=F32)
    back = back[:32] + back[32:]
    for b in range(BAND):
        rain_ref[:, b, :] = back[:LEVELS, b * LONS : (b + 1) * LONS]
    add = coef_ref[0]
    scale = coef_ref[1]
    rain = rain_ref[...].reshape(ROWS, 1, LONS)
    now = state_ref[...]
    out_ref[...] = now + (force_ref[...] + rain * (add + scale * now))


def trig_rows(wave_ref, hi_ref, lo_ref):
    orders = jnp.broadcast_to(wave_ref[...].astype(F32), (MMAX, MMAX)).T
    for v in range(NLON // 128):
        y = lax.broadcasted_iota(jnp.int32, (MMAX, 128), 1).astype(F32) + float(v * 128)
        product = y * orders
        phase = product - NLON * jnp.floor((product + 0.5) * (1.0 / NLON))
        turn = jnp.floor((phase + 48.5) * (1.0 / 96.0))
        x = (phase - 96.0 * turn) * (2.0 * math.pi / NLON)
        z = x * x
        sin = x * (1.0 + z * (-1.0 / 6 + z * (1.0 / 120 + z * (-1.0 / 5040 + z * (1.0 / 362880)))))
        cos = 1.0 + z * (-0.5 + z * (1.0 / 24 + z * (-1.0 / 720 + z * (1.0 / 40320))))
        odd = (turn == 1.0) | (turn == 3.0)
        cos_out = jnp.where(odd, sin, cos)
        sin_out = jnp.where(odd, cos, sin)
        cos_out = jnp.where((turn == 1.0) | (turn == 2.0), -cos_out, cos_out)
        sin_out = jnp.where((turn == 2.0) | (turn == 3.0), -sin_out, sin_out)
        norm = 1.0 / math.sqrt(NLON)
        both = jnp.concatenate(
            (cos_out.reshape(NL, 1, 8, 128), sin_out.reshape(NL, 1, 8, 128)), axis=1
        ).reshape(2 * MMAX, 128)
        hi, lo = split2(both * norm)
        hi_ref[:, v * 128 : v * 128 + 128] = hi
        lo_ref[:, v * 128 : v * 128 + 128] = lo


def table_kernel(wave_ref, own_ref, start_ref, geom_ref, hi_ref, lo_ref, poly_ref):
    trig_rows(wave_ref, hi_ref, lo_ref)
    sub = lax.broadcasted_iota(jnp.int32, (SLOTS_OWN, 128), 0)
    order = jnp.zeros((SLOTS_OWN, 128), F32)
    head = jnp.zeros((SLOTS_OWN, 128), F32)
    for s in range(SLOTS_OWN):
        m = own_ref[s]
        order = jnp.where(sub == s, m.astype(F32), order)
        head = jnp.where(sub == s, start_ref[m], head)
    degree = lax.broadcasted_iota(jnp.int32, (SLOTS_OWN, 128), 1).astype(F32)
    active = degree > order
    numer = jnp.where(active, 4.0 * degree * degree - 1.0, 0.0)
    denom = jnp.where(active, degree * degree - order * order, 1.0)
    grow = jnp.sqrt(numer / denom)
    lower = degree - 1.0
    retreat = jnp.sqrt(
        jnp.maximum(lower * lower - order * order, 0.0) / (4.0 * lower * lower - 1.0)
    )
    retreat = grow * retreat
    begin = jnp.where(degree == order, 1.0, 0.0)
    cosine = geom_ref[0:1, :]
    log_sine = geom_ref[1:2, :]
    weight = geom_ref[2:3, :]
    diagonal = jnp.exp(head[:, 0:1] + order[:, 0:1] * log_sine) * weight
    cosine = jnp.broadcast_to(cosine, (SLOTS_OWN, 256))
    previous = jnp.zeros((SLOTS_OWN, 256), F32)
    current = previous
    for n in range(MMAX):
        fresh = (grow[:, n : n + 1] * cosine) * current + (
            begin[:, n : n + 1] * diagonal - retreat[:, n : n + 1] * previous
        )
        poly_ref[0, n * 8 : n * 8 + 8, :] = fresh[:, :128]
        poly_ref[1, n * 8 : n * 8 + 8, :] = fresh[:, 128:]
        previous, current = current, fresh


def fourier_kernel(got_ref, hi_ref, lo_ref, out_ref, lon_ref):
    width = LEV_OWN * BAND
    rows = got_ref[...].reshape(NC, width, LONS)
    for j in range(NC):
        lon_ref[:, j * LONS : (j + 1) * LONS] = rows[j]
    hi, lo = split2(lon_ref[...])
    dims = (((1,), (1,)), ((), ()))
    out = lax.dot_general(hi_ref[...], hi, dims, preferred_element_type=F32)
    out = out + lax.dot_general(hi_ref[...], lo, dims, preferred_element_type=F32)
    out = out + lax.dot_general(lo_ref[...], hi, dims, preferred_element_type=F32)
    out_ref[...] = out.reshape(NL, 16, width)


def legendre_kernel(got_ref, poly_ref, out_ref, band_ref):
    band_ref[1] = jnp.zeros_like(band_ref[1])
    for k in range(LEV_OWN):
        for i in range(NL):
            h, at = divmod(i * BAND, 128)
            first = min(BAND, 128 - at)
            row = slice(k * 16, k * 16 + 16)
            piece = got_ref[i, :, k * BAND : (k + 1) * BAND]
            band_ref[h, row, at : at + first] = piece[:, :first]
            if first < BAND:
                band_ref[h + 1, row, 0 : BAND - first] = piece[:, first:]
    dims = (((1,), (1,)), ((), ()))
    for s in range(SLOTS_OWN):
        out = None
        for h in range(2):
            hi, lo = split2(band_ref[h, pl.ds(s, 2 * LEV_OWN, stride=8), :])
            whi, wlo = split2(poly_ref[h, pl.ds(s, MMAX, stride=8), :])
            part = lax.dot_general(hi, whi, dims, preferred_element_type=F32)
            part = part + lax.dot_general(hi, wlo, dims, preferred_element_type=F32)
            part = part + lax.dot_general(lo, whi, dims, preferred_element_type=F32)
            out = part if out is None else out + part
        out_ref[:, s, :, :] = out.reshape(LEV_OWN, 2, MMAX)


def diagonal_start():
    return np.array(
        [
            0.5 * (math.lgamma(m + 1.5) - math.lgamma(1.5) - math.lgamma(m + 1.0)) - 0.5 * math.log(2.0)
            for m in range(MMAX)
        ],
        np.float32,
    )


def geometry():
    theta = (np.arange(NLAT) + 0.5) * (math.pi / NLAT)
    sine = np.sin(theta)
    rows = np.stack((np.cos(theta), np.log(sine), sine / math.sqrt(NLAT))).astype(np.float32)
    return np.pad(rows, ((0, 0), (0, 256 - NLAT)))


def call(kernel, out, n_in, scratch=(), specs=None):
    return pl.pallas_call(
        kernel,
        out_shape=out,
        in_specs=specs or [VMEM] * n_in,
        out_specs=jax.tree.map(lambda _: VMEM, out),
        scratch_shapes=list(scratch),
        compiler_params=params(),
    )


def shards(state, forcing, crm_moisture, cloud_order, wave_table):
    shape = jax.ShapeDtypeStruct
    state = state.transpose(0, 2, 3, 1, 4).reshape(ROWS, 1, LONS)
    forcing = forcing.transpose(0, 2, 3, 1, 4).reshape(ROWS, 1, LONS)
    moist = crm_moisture.transpose(0, 2, 3, 4, 1, 5).reshape(LEVELS, NCRM, RUNS)
    order = cloud_order.reshape(1, COLS)
    waves = wave_table.reshape(1, MMAX)
    sec = lax.axis_index("sec")
    lat = lax.axis_index("lat")
    own = lax.dynamic_slice_in_dim(wave_table, lat * SLOTS_OWN, SLOTS_OWN)
    coef = jnp.stack(
        (
            jnp.where(sec == 2, 1.0, jnp.where(sec == 3, -1.0, 0.0)),
            jnp.where(sec < 2, -1.0 / NSUB, 0.0),
        )
    ).astype(F32)

    outgoing = call(
        pack_kernel,
        shape((TARGETS, 8, 128), F32),
        3,
        [pltpu.VMEM((COLS, COLS), BF16), pltpu.VMEM((2 * LEVELS, COLS), F32)],
    )(state, forcing, order)
    arrived = lax.all_to_all(outgoing, ("sec", "lat"), split_axis=0, concat_axis=0, tiled=True)
    trig_hi, trig_lo, poly = call(
        table_kernel,
        (
            shape((2 * MMAX, NLON), BF16),
            shape((2 * MMAX, NLON), BF16),
            shape((2, MMAX * SLOTS_OWN, 128), F32),
        ),
        4,
        specs=[VMEM, SMEM, SMEM, VMEM],
    )(waves, own, jnp.asarray(diagonal_start()), jnp.asarray(geometry()))
    rain = call(
        cloud_kernel,
        shape((TARGETS, 8, 128), F32),
        2,
        [
            pltpu.VMEM((32, 384), F32),
            pltpu.VMEM((56, 384), F32),
            pltpu.VMEM((32, 384), F32),
            pltpu.VMEM((32, 384), F32),
            pltpu.VMEM((32, 384), F32),
        ],
    )(arrived, moist)
    returned = lax.all_to_all(rain, ("sec", "lat"), split_axis=0, concat_axis=0, tiled=True)
    updated = call(
        update_kernel,
        shape((ROWS, 1, LONS), F32),
        5,
        [
            pltpu.VMEM((COLS, COLS), BF16),
            pltpu.VMEM((32, COLS), F32),
            pltpu.VMEM((LEVELS, BAND, LONS), F32),
        ],
        specs=[VMEM, VMEM, VMEM, VMEM, SMEM],
    )(returned, order, state, forcing, coef)
    all_lons = lax.all_to_all(updated, "col", split_axis=0, concat_axis=0, tiled=True)
    fourier = call(
        fourier_kernel,
        shape((NL, 16, LEV_OWN * BAND), F32),
        3,
        [pltpu.VMEM((LEV_OWN * BAND, NLON), F32)],
    )(all_lons, trig_hi, trig_lo)
    bands = lax.all_to_all(fourier, "lat", split_axis=0, concat_axis=0, tiled=True)
    spectral = call(
        legendre_kernel,
        shape((LEV_OWN, SLOTS_OWN, 2, MMAX), F32),
        2,
        [pltpu.VMEM((2, LEV_OWN * 16, 128), F32)],
    )(bands, poly)
    new_state = updated.reshape(1, LEVELS, BAND, 1, LONS).transpose(0, 3, 1, 2, 4)
    return new_state, spectral[None, None]


def solution(mesh):
    placed = (
        P(None, "sec", None, "lat", "col"),
        P(None, "sec", None, "lat", "col"),
        P(None, None, None, ("sec", "lat"), "col", None),
        P("col", "lat", None),
        P(),
    )
    return jax.shard_map(
        shards,
        mesh=mesh,
        in_specs=placed,
        out_specs=(P(None, "sec", None, "lat", "col"), P("sec", None, "col", "lat", None, None)),
        check_vma=False,
    )
```

```python
import math

import jax
import jax.numpy as jnp
import numpy as np
from jax import lax
from jax.experimental import pallas as pl
from jax.experimental.pallas import tpu as pltpu
from jax.sharding import PartitionSpec as P

NLON = 384
NLAT = 192
MMAX = 128
NSUB = 4
NCRM = 32
LEVELS = 28
BAND = 12
LONS = 96
COLS = BAND * LONS
ROWS = LEVELS * BAND
TARGETS = 64
PER = 18
NL = 16
NS = 4
NC = 4
RUNS = NL * PER
HALF = 4 * PER
LEV_OWN = LEVELS // NC
SLOTS_OWN = MMAX // NL

F32 = jnp.float32
BF16 = jnp.bfloat16
VMEM = pl.BlockSpec(memory_space=pltpu.VMEM)
HBM = pl.BlockSpec(memory_space=pltpu.HBM)


def split2(x):
    hi = x.astype(BF16)
    lo = (x - hi.astype(F32)).astype(BF16)
    return hi, lo


def params(mib=24):
    return pltpu.CompilerParams(vmem_limit_bytes=mib << 20)


def lanes_of(shape):
    return lax.broadcasted_iota(jnp.int32, shape, 1)


def fill_one_hot(order_ref, hot_ref):
    order = order_ref[...]
    step = 96
    for c in range(0, COLS, step):
        ids = lax.broadcasted_iota(jnp.int32, (step, COLS), 0) + c
        hot_ref[c : c + step, :] = jnp.where(ids == order, 1.0, 0.0).astype(BF16)


def trig_rows(orders, hi_ref, lo_ref):
    first = (lax.axis_index("col") * LONS).astype(F32)
    y = lax.broadcasted_iota(jnp.int32, (MMAX, 128), 1).astype(F32) + first
    product = y * orders
    phase = product - NLON * jnp.floor((product + 0.5) * (1.0 / NLON))
    turn = jnp.floor((phase + 48.5) * (1.0 / 96.0))
    x = (phase - 96.0 * turn) * (2.0 * math.pi / NLON)
    z = x * x
    sin = x * (1.0 + z * (-1.0 / 6 + z * (1.0 / 120 + z * (-1.0 / 5040 + z * (1.0 / 362880)))))
    cos = 1.0 + z * (-0.5 + z * (1.0 / 24 + z * (-1.0 / 720 + z * (1.0 / 40320))))
    odd = (turn == 1.0) | (turn == 3.0)
    cos_out = jnp.where(odd, sin, cos)
    sin_out = jnp.where(odd, cos, sin)
    cos_out = jnp.where((turn == 1.0) | (turn == 2.0), -cos_out, cos_out)
    sin_out = jnp.where((turn == 2.0) | (turn == 3.0), -sin_out, sin_out)
    norm = 1.0 / math.sqrt(NLON)
    both = jnp.concatenate(
        (cos_out.reshape(NL, 1, 8, 128), sin_out.reshape(NL, 1, 8, 128)), axis=1
    ).reshape(2 * MMAX, 128)
    hi, lo = split2(both * norm)
    hi_ref[...] = hi
    lo_ref[...] = lo


def legendre_rows(order, geom_ref, poly_ref):
    lane = lanes_of((SLOTS_OWN, 128)).astype(F32)
    head = jnp.sum(jnp.where(lane == order, geom_ref[3:4, 0:128], 0.0), axis=1, keepdims=True)
    degree = lax.broadcasted_iota(jnp.int32, (SLOTS_OWN, 128), 1).astype(F32)
    active = degree > order
    numer = jnp.where(active, 4.0 * degree * degree - 1.0, 0.0)
    denom = jnp.where(active, degree * degree - order * order, 1.0)
    grow = jnp.sqrt(numer / denom)
    lower = degree - 1.0
    retreat = jnp.sqrt(
        jnp.maximum(lower * lower - order * order, 0.0) / (4.0 * lower * lower - 1.0)
    )
    retreat = grow * retreat
    begin = jnp.where(degree == order, 1.0, 0.0)
    diagonal = jnp.exp(head + order[:, 0:1] * geom_ref[1:2, :]) * geom_ref[2:3, :]
    cosine = jnp.broadcast_to(geom_ref[0:1, :], (SLOTS_OWN, 256))
    previous = jnp.zeros((SLOTS_OWN, 256), F32)
    current = previous
    for n in range(MMAX):
        fresh = (grow[:, n : n + 1] * cosine) * current + (
            begin[:, n : n + 1] * diagonal - retreat[:, n : n + 1] * previous
        )
        poly_ref[0, n * 8 : n * 8 + 8, :] = fresh[:, :128]
        poly_ref[1, n * 8 : n * 8 + 8, :] = fresh[:, 128:]
        previous, current = current, fresh


def pack_kernel(
    state_hbm,
    force_hbm,
    order_hbm,
    wave_hbm,
    geom_hbm,
    moist_hbm,
    out_ref,
    hot_ref,
    cols_ref,
    hi_ref,
    lo_ref,
    poly_ref,
    moist_ref,
    state_ref,
    force_ref,
    order_ref,
    wave_ref,
    geom_ref,
    orders_ref,
    sems,
):
    loads = [
        pltpu.make_async_copy(src, dst, sems.at[n])
        for n, (src, dst) in enumerate(
            (
                (wave_hbm, wave_ref),
                (geom_hbm, geom_ref),
                (order_hbm, order_ref),
                (state_hbm, state_ref),
                (force_hbm, force_ref),
                (moist_hbm, moist_ref),
            )
        )
    ]
    for load in loads:
        load.start()
    loads[0].wait()
    orders = jnp.broadcast_to(wave_ref[...].astype(F32), (MMAX, MMAX)).T
    orders_ref[...] = orders
    trig_rows(orders, hi_ref, lo_ref)
    loads[1].wait()
    first = pl.multiple_of(lax.axis_index("lat") * SLOTS_OWN, SLOTS_OWN)
    legendre_rows(orders_ref[pl.ds(first, SLOTS_OWN), :], geom_ref, poly_ref)
    loads[2].wait()
    fill_one_hot(order_ref, hot_ref)
    loads[3].wait()
    loads[4].wait()
    for ref, base in ((state_ref, 0), (force_ref, LEVELS)):
        rows = ref[...].reshape(LEVELS, BAND, LONS)
        for b in range(BAND):
            cols_ref[base : base + LEVELS, b * LONS : (b + 1) * LONS] = rows[:, b, :]
    hi, lo = split2(cols_ref[...])
    both = jnp.concatenate((hi, lo), axis=0)
    got = jnp.dot(both, hot_ref[...], preferred_element_type=F32)
    got = got[: 2 * LEVELS] + got[2 * LEVELS :]
    lane = lanes_of((8, 128))
    groups = 2 * LEVELS // 8
    for t in range(TARGETS):
        v, off = divmod(t * PER, 128)
        tile = None
        for q in range(groups):
            src = got[q * 8 : q * 8 + 8, v * 128 : v * 128 + 128]
            if off + PER > 128:
                nxt = got[q * 8 : q * 8 + 8, v * 128 + 128 : v * 128 + 256]
                src = jnp.where(lane < off, nxt, src)
            shift = (q * PER - off) % 128
            if shift:
                src = pltpu.roll(src, shift, 1)
            tile = src if tile is None else jnp.where(lane >= q * PER, src, tile)
        out_ref[t] = tile
    loads[5].wait()


def gather_lanes(tile_of, q_list, first, count, width, store):
    lane = lanes_of((8, 128))
    for q in q_list:
        for v in range(pl.cdiv(width, 128)):
            acc = None
            for i in range(count):
                start = i * PER - v * 128
                if start >= 128 or start + PER <= 0:
                    continue
                src = tile_of(first + i)
                shift = (i * PER - q * PER) % 128
                if shift:
                    src = pltpu.roll(src, shift, 1)
                acc = src if acc is None else jnp.where(lane >= start, src, acc)
            store(q, v, acc)


def cloud_kernel(got_ref, moist_ref, out_ref, wind_ref, diff_ref, left_ref, right_ref, rain_ref):
    def store_wind(q, v, x):
        wind_ref[q * 8 : q * 8 + 8, v * 128 : v * 128 + 128] = x

    def store_diff(q, v, x):
        diff_ref[q * 8 : q * 8 + 8, v * 128 : v * 128 + 128] = x

    gather_lanes(lambda i: got_ref[i], range(4), 0, NL, RUNS, store_wind)
    cache = {}

    def diff(i):
        if i not in cache:
            cache[i] = got_ref[3 * NL + i] - got_ref[2 * NL + i]
        return cache[i]

    gather_lanes(diff, range(7), 0, NL, RUNS, store_diff)
    courant = 0.4 * jnp.tanh(wind_ref[...])
    mixing = 0.2 + 0.5 * jnp.abs(courant)
    left_ref[...] = mixing - 0.5 * courant
    right_ref[...] = mixing + 0.5 * courant
    rain_ref[...] = jnp.zeros_like(rain_ref)

    def level(k, carry):
        row = (pl.ds(k, 1), slice(0, RUNS))
        gap = diff_ref[row] + moist_ref[k].astype(F32)
        push = diff_ref[pl.ds(k + LEVELS, 1), 0:RUNS] * (1.0 / NSUB)
        ahead = left_ref[row]
        behind = right_ref[row]
        both = ahead + behind
        wet = jnp.maximum(gap, 0.0)
        for _ in range(NSUB - 1):
            up = pltpu.roll(gap, NCRM - 1, 0)
            down = pltpu.roll(gap, 1, 0)
            gap = (jnp.minimum(gap, 0.0) - both * gap) + (ahead * up + behind * down) + push
            wet = wet + jnp.maximum(gap, 0.0)
        rain_ref[pl.ds(k, 1), 0:RUNS] = jnp.sum(wet, axis=0, keepdims=True) * (0.5 / NCRM)
        return carry

    lax.fori_loop(0, LEVELS, level, 0)
    lane = lanes_of((8, 128))
    for i in range(NL):
        v, off = divmod(i * PER, 128)
        tile = None
        for q in range(4):
            src = rain_ref[q * 8 : q * 8 + 8, v * 128 : v * 128 + 128]
            if off + PER > 128:
                nxt = rain_ref[q * 8 : q * 8 + 8, v * 128 + 128 : v * 128 + 256]
                src = jnp.where(lane < off, nxt, src)
            shift = (q * PER - off) % 128
            if shift:
                src = pltpu.roll(src, shift, 1)
            tile = src if tile is None else jnp.where(lane >= q * PER, src, tile)
        low = tile[0:4]
        high = pltpu.roll(tile, HALF, 1)[4:8]
        tile = jnp.where(lane[0:4] < HALF, low, high)
        for s in range(NS):
            out_ref[s * NL + i] = tile


def update_kernel(got_ref, hot_ref, cols_ref, hi_ref, lo_ref, out_ref, four_ref, slots_ref, rows_ref):
    def store(q, v, x):
        slots_ref[q * 8 : q * 8 + 8, v * 128 : v * 128 + 128] = x

    cache = {}

    def tile_of(t):
        if t not in cache:
            tile = got_ref[t]
            cache[t] = jnp.concatenate((tile, pltpu.roll(tile, 128 - HALF, 1)), axis=0)
        return cache[t]

    gather_lanes(tile_of, range(4), 0, TARGETS, COLS, store)
    hi, lo = split2(slots_ref[...])
    both = jnp.concatenate((hi, lo), axis=0)
    back = lax.dot_general(both, hot_ref[...], (((1,), (1,)), ((), ())), preferred_element_type=F32)
    rain = back[:LEVELS] + back[32 : 32 + LEVELS]
    sec = lax.axis_index("sec")
    add = jnp.where(sec == 2, 1.0, jnp.where(sec == 3, -1.0, 0.0)).astype(F32)
    scale = jnp.where(sec < 2, -1.0 / NSUB, 0.0).astype(F32)
    now = cols_ref[0:LEVELS]
    now = now + (cols_ref[LEVELS : 2 * LEVELS] + rain * (add + scale * now))
    blank = jnp.zeros((LEVELS, 128 - LONS), F32)
    for b in range(BAND):
        piece = jnp.concatenate((now[:, b * LONS : (b + 1) * LONS], blank), axis=1)
        rows_ref[pl.ds(b, LEVELS, stride=BAND), :] = piece
    rows = rows_ref[...]
    out_ref[...] = rows[:, :LONS].reshape(ROWS, 1, LONS)
    xhi, xlo = split2(rows)
    dims = (((1,), (1,)), ((), ()))
    out = lax.dot_general(hi_ref[...], xhi, dims, preferred_element_type=F32)
    out = out + lax.dot_general(hi_ref[...], xlo, dims, preferred_element_type=F32)
    out = out + lax.dot_general(lo_ref[...], xhi, dims, preferred_element_type=F32)
    width = LEV_OWN * BAND
    for j in range(NC):
        part = out[:, j * width : (j + 1) * width].reshape(NL, 16, width)
        for i in range(NL):
            four_ref[i * NC + j] = part[i]


def legendre_kernel(got_ref, poly_ref, out_ref, band_ref):
    band_ref[1] = jnp.zeros_like(band_ref[1])
    bands = [
        (got_ref[i * NC] + got_ref[i * NC + 1]) + (got_ref[i * NC + 2] + got_ref[i * NC + 3])
        for i in range(NL)
    ]
    for k in range(LEV_OWN):
        for i in range(NL):
            h, at = divmod(i * BAND, 128)
            first = min(BAND, 128 - at)
            row = slice(k * 16, k * 16 + 16)
            piece = bands[i][:, k * BAND : (k + 1) * BAND]
            band_ref[h, row, at : at + first] = piece[:, :first]
            if first < BAND:
                band_ref[h + 1, row, 0 : BAND - first] = piece[:, first:]
    dims = (((1,), (1,)), ((), ()))
    for s in range(SLOTS_OWN):
        out = None
        for h in range(2):
            hi, lo = split2(band_ref[h, pl.ds(s, 2 * LEV_OWN, stride=8), :])
            whi, wlo = split2(poly_ref[h, pl.ds(s, MMAX, stride=8), :])
            part = lax.dot_general(hi, whi, dims, preferred_element_type=F32)
            part = part + lax.dot_general(hi, wlo, dims, preferred_element_type=F32)
            part = part + lax.dot_general(lo, whi, dims, preferred_element_type=F32)
            out = part if out is None else out + part
        out_ref[:, s, :, :] = out.reshape(LEV_OWN, 2, MMAX)


def geometry():
    theta = (np.arange(NLAT) + 0.5) * (math.pi / NLAT)
    sine = np.sin(theta)
    rows = np.zeros((4, 256))
    rows[0, :NLAT] = np.cos(theta)
    rows[1, :NLAT] = np.log(sine)
    rows[2, :NLAT] = sine / math.sqrt(NLAT)
    for m in range(MMAX):
        logs = math.lgamma(m + 1.5) - math.lgamma(1.5) - math.lgamma(m + 1.0)
        rows[3, m] = 0.5 * logs - 0.5 * math.log(2.0)
    return rows.astype(np.float32)


def call(kernel, out, specs, scratch=()):
    return pl.pallas_call(
        kernel,
        out_shape=out,
        in_specs=specs,
        out_specs=jax.tree.map(lambda _: VMEM, out),
        scratch_shapes=list(scratch),
        compiler_params=params(),
    )


def stay(x):
    return pltpu.with_memory_space_constraint(x, pltpu.HBM)


def shards(state, forcing, crm_moisture, cloud_order, wave_table):
    shape = jax.ShapeDtypeStruct
    state = state.transpose(0, 2, 3, 1, 4).reshape(ROWS, 1, LONS)
    forcing = forcing.transpose(0, 2, 3, 1, 4).reshape(ROWS, 1, LONS)
    moist = crm_moisture.transpose(0, 2, 3, 4, 1, 5).reshape(LEVELS, NCRM, RUNS)
    order = cloud_order.reshape(1, COLS)
    waves = wave_table.reshape(1, MMAX)
    outgoing, hot, cols, trig_hi, trig_lo, poly, moist = call(
        pack_kernel,
        (
            shape((TARGETS, 8, 128), F32),
            shape((COLS, COLS), BF16),
            shape((2 * LEVELS, COLS), F32),
            shape((2 * MMAX, 128), BF16),
            shape((2 * MMAX, 128), BF16),
            shape((2, MMAX * SLOTS_OWN, 128), F32),
            shape((LEVELS, NCRM, RUNS), BF16),
        ),
        [HBM] * 6,
        [
            pltpu.VMEM((ROWS, 1, LONS), F32),
            pltpu.VMEM((ROWS, 1, LONS), F32),
            pltpu.VMEM((1, COLS), jnp.int32),
            pltpu.VMEM((1, MMAX), jnp.int32),
            pltpu.VMEM((4, 256), F32),
            pltpu.VMEM((MMAX, 128), F32),
            pltpu.SemaphoreType.DMA((6,)),
        ],
    )(*(stay(x) for x in (state, forcing, order, waves, jnp.asarray(geometry()), moist)))
    arrived = lax.all_to_all(outgoing, ("sec", "lat"), split_axis=0, concat_axis=0, tiled=True)
    rain = call(
        cloud_kernel,
        shape((TARGETS, 4, 128), F32),
        [VMEM, VMEM],
        [
            pltpu.VMEM((32, 384), F32),
            pltpu.VMEM((56, 384), F32),
            pltpu.VMEM((32, 384), F32),
            pltpu.VMEM((32, 384), F32),
            pltpu.VMEM((32, 384), F32),
        ],
    )(arrived, moist)
    returned = lax.all_to_all(rain, ("sec", "lat"), split_axis=0, concat_axis=0, tiled=True)
    updated, fourier = call(
        update_kernel,
        (shape((ROWS, 1, LONS), F32), shape((NL * NC, 16, LEV_OWN * BAND), F32)),
        [VMEM] * 5,
        [pltpu.VMEM((32, COLS), F32), pltpu.VMEM((ROWS, 128), F32)],
    )(returned, hot, cols, trig_hi, trig_lo)
    bands = lax.all_to_all(fourier, ("lat", "col"), split_axis=0, concat_axis=0, tiled=True)
    spectral = call(
        legendre_kernel,
        shape((LEV_OWN, SLOTS_OWN, 2, MMAX), F32),
        [VMEM] * 2,
        [pltpu.VMEM((2, LEV_OWN * 16, 128), F32)],
    )(bands, poly)
    new_state = updated.reshape(1, LEVELS, BAND, 1, LONS).transpose(0, 3, 1, 2, 4)
    return new_state, spectral[None, None]


def solution(mesh):
    placed = (
        P(None, "sec", None, "lat", "col"),
        P(None, "sec", None, "lat", "col"),
        P(None, None, None, ("sec", "lat"), "col", None),
        P("col", "lat", None),
        P(),
    )
    return jax.shard_map(
        shards,
        mesh=mesh,
        in_specs=placed,
        out_specs=(P(None, "sec", None, "lat", "col"), P("sec", None, "col", "lat", None, None)),
        check_vma=False,
    )
```

```python
import math

import jax
import jax.numpy as jnp
import numpy as np
from jax import lax
from jax.experimental import pallas as pl
from jax.experimental.pallas import tpu as pltpu
from jax.sharding import PartitionSpec as P

NLON = 384
NLAT = 192
MMAX = 128
NSUB = 4
NCRM = 32
LEVELS = 28
BAND = 12
LONS = 96
COLS = BAND * LONS
ROWS = LEVELS * BAND
TARGETS = 64
PER = 18
NL = 16
NS = 4
NC = 4
RUNS = NL * PER
HALF = 4 * PER
LEV_OWN = LEVELS // NC
SLOTS_OWN = MMAX // NL

F32 = jnp.float32
BF16 = jnp.bfloat16
VMEM = pl.BlockSpec(memory_space=pltpu.VMEM)
HBM = pl.BlockSpec(memory_space=pltpu.HBM)


def split2(x):
    hi = x.astype(BF16)
    lo = (x - hi.astype(F32)).astype(BF16)
    return hi, lo


def params(mib=16):
    return pltpu.CompilerParams(vmem_limit_bytes=mib << 20)


def lanes_of(shape):
    return lax.broadcasted_iota(jnp.int32, shape, 1)


def fill_one_hot(order_ref, hot_ref):
    order = order_ref[...]
    step = 96
    for c in range(0, COLS, step):
        ids = lax.broadcasted_iota(jnp.int32, (step, COLS), 0) + c
        hot_ref[c : c + step, :] = jnp.where(ids == order, 1.0, 0.0).astype(BF16)


def trig_rows(orders, trig_ref):
    first = (lax.axis_index("col") * LONS).astype(F32)
    y = lax.broadcasted_iota(jnp.int32, (MMAX, 128), 1).astype(F32) + first
    product = y * orders
    phase = product - NLON * jnp.floor((product + 0.5) * (1.0 / NLON))
    turn = jnp.floor((phase + 48.5) * (1.0 / 96.0))
    x = (phase - 96.0 * turn) * (2.0 * math.pi / NLON)
    z = x * x
    sin = x * (1.0 + z * (-1.0 / 6 + z * (1.0 / 120 + z * (-1.0 / 5040 + z * (1.0 / 362880)))))
    cos = 1.0 + z * (-0.5 + z * (1.0 / 24 + z * (-1.0 / 720 + z * (1.0 / 40320))))
    odd = (turn == 1.0) | (turn == 3.0)
    cos_out = jnp.where(odd, sin, cos)
    sin_out = jnp.where(odd, cos, sin)
    cos_out = jnp.where((turn == 1.0) | (turn == 2.0), -cos_out, cos_out)
    sin_out = jnp.where((turn == 2.0) | (turn == 3.0), -sin_out, sin_out)
    norm = 1.0 / math.sqrt(NLON)
    halves = [
        part.reshape(NL, 2, 4, 128)[:, h].reshape(NL * 4, 128)
        for part in (cos_out * norm, sin_out * norm)
        for h in range(2)
    ]
    hi, lo = split2(jnp.concatenate(halves, axis=0))
    trig_ref[:, 0:128] = hi
    trig_ref[:, 128:256] = hi
    trig_ref[:, 256:384] = lo


def legendre_rows(order, geom_ref, poly_ref, weight_ref):
    lane = lanes_of((SLOTS_OWN, 128)).astype(F32)
    head = jnp.sum(jnp.where(lane == order, geom_ref[3:4, 0:128], 0.0), axis=1, keepdims=True)
    degree = lax.broadcasted_iota(jnp.int32, (SLOTS_OWN, 128), 1).astype(F32)
    active = degree > order
    numer = jnp.where(active, 4.0 * degree * degree - 1.0, 0.0)
    denom = jnp.where(active, degree * degree - order * order, 1.0)
    grow = jnp.sqrt(numer / denom)
    lower = degree - 1.0
    retreat = jnp.sqrt(
        jnp.maximum(lower * lower - order * order, 0.0) / (4.0 * lower * lower - 1.0)
    )
    retreat = grow * retreat
    begin = jnp.where(degree == order, 1.0, 0.0)
    diagonal = jnp.exp(head + order[:, 0:1] * geom_ref[1:2, :]) * geom_ref[2:3, :]
    cosine = jnp.broadcast_to(geom_ref[0:1, :], (SLOTS_OWN, 256))
    previous = jnp.zeros((SLOTS_OWN, 256), F32)
    current = previous
    for n in range(MMAX):
        fresh = (grow[:, n : n + 1] * cosine) * current + (
            begin[:, n : n + 1] * diagonal - retreat[:, n : n + 1] * previous
        )
        poly_ref[0, n * 8 : n * 8 + 8, :] = fresh[:, :128]
        poly_ref[1, n * 8 : n * 8 + 8, :] = fresh[:, 128:]
        previous, current = current, fresh
    for s in range(SLOTS_OWN):
        for h in range(2):
            hi, lo = split2(poly_ref[h, pl.ds(s, MMAX, stride=8), :])
            for part, block in ((hi, 0), (lo, 2), (hi, 4)):
                at = (block + h) * 128
                weight_ref[s, :, at : at + 128] = part


def table_kernel(
    wave_hbm,
    geom_hbm,
    moist_hbm,
    trig_ref,
    weight_ref,
    water_hbm,
    wave_ref,
    geom_ref,
    moist_ref,
    poly_ref,
    orders_ref,
    level_ref,
    water_ref,
    sems,
):
    pairs = ((wave_hbm, wave_ref), (geom_hbm, geom_ref), (moist_hbm, moist_ref))
    loads = [pltpu.make_async_copy(src, dst, sems.at[n]) for n, (src, dst) in enumerate(pairs)]
    for load in loads:
        load.start()
    loads[2].wait()
    blank = jnp.zeros((NCRM, 384 - RUNS), F32)
    for k in range(LEVELS):
        level = jnp.concatenate((moist_ref[k].astype(F32), blank), axis=1)
        for v in range(3):
            level_ref[k, v] = level[:, v * 128 : v * 128 + 128]
        for v in range(3):
            for n in range(4):
                water_ref[k, v, n] = level_ref[k, v, pl.ds(n, 8, stride=4), :]
    save = pltpu.make_async_copy(water_ref, water_hbm, sems.at[3])
    save.start()
    loads[0].wait()
    loads[1].wait()
    orders = jnp.broadcast_to(wave_ref[...].astype(F32), (MMAX, MMAX)).T
    orders_ref[...] = orders
    trig_rows(orders, trig_ref)
    first = pl.multiple_of(lax.axis_index("lat") * SLOTS_OWN, SLOTS_OWN)
    legendre_rows(orders_ref[pl.ds(first, SLOTS_OWN), :], geom_ref, poly_ref, weight_ref)
    save.wait()


def pack_kernel(
    state_hbm, force_hbm, order_hbm, out_ref, hot_ref, cols_ref, state_ref, force_ref, order_ref, sems
):
    pairs = ((order_hbm, order_ref), (state_hbm, state_ref), (force_hbm, force_ref))
    loads = [pltpu.make_async_copy(src, dst, sems.at[n]) for n, (src, dst) in enumerate(pairs)]
    for load in loads:
        load.start()
    loads[0].wait()
    fill_one_hot(order_ref, hot_ref)
    loads[1].wait()
    loads[2].wait()
    for ref, base in ((state_ref, 0), (force_ref, LEVELS)):
        rows = ref[...].reshape(LEVELS, BAND, LONS)
        for b in range(BAND):
            cols_ref[base : base + LEVELS, b * LONS : (b + 1) * LONS] = rows[:, b, :]
    hi, lo = split2(cols_ref[...])
    both = jnp.concatenate((hi, lo), axis=0)
    got = jnp.dot(both, hot_ref[...], preferred_element_type=F32)
    got = got[: 2 * LEVELS] + got[2 * LEVELS :]
    lane = lanes_of((8, 128))
    groups = 2 * LEVELS // 8
    for t in range(TARGETS):
        v, off = divmod(t * PER, 128)
        tile = None
        for q in range(groups):
            src = got[q * 8 : q * 8 + 8, v * 128 : v * 128 + 128]
            if off + PER > 128:
                nxt = got[q * 8 : q * 8 + 8, v * 128 + 128 : v * 128 + 256]
                src = jnp.where(lane < off, nxt, src)
            shift = (q * PER - off) % 128
            if shift:
                src = pltpu.roll(src, shift, 1)
            tile = src if tile is None else jnp.where(lane >= q * PER, src, tile)
        out_ref[t] = tile


def gather_lanes(tile_of, q_list, first, count, width, store):
    lane = lanes_of((8, 128))
    for q in q_list:
        for v in range(pl.cdiv(width, 128)):
            acc = None
            for i in range(count):
                start = i * PER - v * 128
                if start >= 128 or start + PER <= 0:
                    continue
                src = tile_of(first + i)
                shift = (i * PER - q * PER) % 128
                if shift:
                    src = pltpu.roll(src, shift, 1)
                acc = src if acc is None else jnp.where(lane >= start, src, acc)
            store(q, v, acc)


def cloud_kernel(
    got_ref, water_hbm, out_ref, wind_ref, diff_ref, left_ref, right_ref, rain_ref, water_ref, sem
):
    load = pltpu.make_async_copy(water_hbm, water_ref, sem)
    load.start()

    def store_wind(q, v, x):
        wind_ref[v, q * 8 : q * 8 + 8, :] = x

    def store_diff(q, v, x):
        diff_ref[v, q * 8 : q * 8 + 8, :] = x

    gather_lanes(lambda i: got_ref[i], range(4), 0, NL, RUNS, store_wind)
    cache = {}

    def diff(i):
        if i not in cache:
            cache[i] = got_ref[3 * NL + i] - got_ref[2 * NL + i]
        return cache[i]

    gather_lanes(diff, range(7), 0, NL, RUNS, store_diff)
    courant = 0.4 * jnp.tanh(wind_ref[...])
    mixing = 0.2 + 0.5 * jnp.abs(courant)
    left_ref[...] = mixing - 0.5 * courant
    right_ref[...] = mixing + 0.5 * courant
    rain_ref[...] = jnp.zeros_like(rain_ref)

    def level(k, carry):
        for v in range(3):

            def row(ref, at):
                return jnp.broadcast_to(ref[v, pl.ds(at, 1), :], (8, 128))

            start = row(diff_ref, k)
            push = row(diff_ref, k + LEVELS) * (1.0 / NSUB)
            ahead = row(left_ref, k)
            behind = row(right_ref, k)
            keep = 1.0 - (ahead + behind)
            gap = [start + water_ref[k, v, n] for n in range(4)]
            wet = [jnp.maximum(g, 0.0) for g in gap]
            total = (wet[0] + wet[1]) + (wet[2] + wet[3])
            for _ in range(NSUB - 1):
                up = gap[1:] + [pltpu.roll(gap[0], 7, 0)]
                down = [pltpu.roll(gap[3], 1, 0)] + gap[:3]
                gap = [
                    ((keep * gap[n] - wet[n]) + push) + (ahead * up[n] + behind * down[n])
                    for n in range(4)
                ]
                wet = [jnp.maximum(g, 0.0) for g in gap]
                total = total + ((wet[0] + wet[1]) + (wet[2] + wet[3]))
            rain_ref[v, pl.ds(k, 1), :] = jnp.sum(total, axis=0, keepdims=True) * (0.5 / NCRM)
        return carry

    load.wait()
    lax.fori_loop(0, LEVELS, level, 0, unroll=2)
    lane = lanes_of((8, 128))
    for i in range(NL):
        v, off = divmod(i * PER, 128)
        tile = None
        for q in range(4):
            src = rain_ref[v, q * 8 : q * 8 + 8, :]
            if off + PER > 128:
                nxt = rain_ref[v + 1, q * 8 : q * 8 + 8, :]
                src = jnp.where(lane < off, nxt, src)
            shift = (q * PER - off) % 128
            if shift:
                src = pltpu.roll(src, shift, 1)
            tile = src if tile is None else jnp.where(lane >= q * PER, src, tile)
        low = tile[0:4]
        high = pltpu.roll(tile, HALF, 1)[4:8]
        tile = jnp.where(lane[0:4] < HALF, low, high)
        for s in range(NS):
            out_ref[s * NL + i] = tile


def update_kernel(got_ref, hot_ref, cols_ref, trig_ref, out_ref, four_ref, slots_ref, rows_ref):
    def store(q, v, x):
        slots_ref[q * 8 : q * 8 + 8, v * 128 : v * 128 + 128] = x

    cache = {}

    def tile_of(t):
        if t not in cache:
            tile = got_ref[t]
            cache[t] = jnp.concatenate((tile, pltpu.roll(tile, 128 - HALF, 1)), axis=0)
        return cache[t]

    gather_lanes(tile_of, range(4), 0, TARGETS, COLS, store)
    hi, lo = split2(slots_ref[...])
    both = jnp.concatenate((hi, lo), axis=0)
    back = lax.dot_general(both, hot_ref[...], (((1,), (1,)), ((), ())), preferred_element_type=F32)
    rain = back[:LEVELS] + back[32 : 32 + LEVELS]
    sec = lax.axis_index("sec")
    add = jnp.where(sec == 2, 1.0, jnp.where(sec == 3, -1.0, 0.0)).astype(F32)
    scale = jnp.where(sec < 2, -1.0 / NSUB, 0.0).astype(F32)
    now = cols_ref[0:LEVELS]
    now = now + (cols_ref[LEVELS : 2 * LEVELS] + rain * (add + scale * now))
    blank = jnp.zeros((LEVELS, 128 - LONS), F32)
    for b in range(BAND):
        piece = jnp.concatenate((now[:, b * LONS : (b + 1) * LONS], blank), axis=1)
        rows_ref[pl.ds(b, LEVELS, stride=BAND), :] = piece
    rows = rows_ref[...]
    out_ref[...] = rows[:, :LONS].reshape(ROWS, 1, LONS)
    hi, lo = split2(rows)
    dims = (((1,), (1,)), ((), ()))
    parts = jnp.concatenate((hi, lo, hi), axis=1)
    out = lax.dot_general(trig_ref[...], parts, dims, preferred_element_type=F32)
    width = LEV_OWN * BAND
    blank = jnp.zeros((NL * 4, 384 - 4 * width), F32)
    for j in range(NC):
        pieces = [out[g * 64 : g * 64 + 64, j * width : (j + 1) * width] for g in range(4)]
        four_ref[:, j] = jnp.concatenate(pieces + [blank], axis=1).reshape(NL, 4, 384)


def legendre_kernel(got_ref, weight_ref, out_ref, band_ref):
    width = LEV_OWN * BAND
    band_ref[1] = jnp.zeros_like(band_ref[1])
    for i in range(NL):
        part = (got_ref[i, 0] + got_ref[i, 1]) + (got_ref[i, 2] + got_ref[i, 3])
        bands = jnp.concatenate([part[:, g * width : (g + 1) * width] for g in range(4)], axis=0)
        h, at = divmod(i * BAND, 128)
        first = min(BAND, 128 - at)
        for k in range(LEV_OWN):
            row = slice(k * 16, k * 16 + 16)
            piece = bands[:, k * BAND : (k + 1) * BAND]
            band_ref[h, row, at : at + first] = piece[:, :first]
            if first < BAND:
                band_ref[h + 1, row, 0 : BAND - first] = piece[:, first:]
    dims = (((1,), (1,)), ((), ()))
    for s in range(SLOTS_OWN):
        rows = [band_ref[h, pl.ds(s, 2 * LEV_OWN, stride=8), :] for h in range(2)]
        hi, lo = split2(jnp.concatenate(rows, axis=1))
        parts = jnp.concatenate((hi, hi, lo), axis=1)
        out = lax.dot_general(parts, weight_ref[s], dims, preferred_element_type=F32)
        out_ref[:, s, :, :] = out.reshape(LEV_OWN, 2, MMAX)


def geometry():
    theta = (np.arange(NLAT) + 0.5) * (math.pi / NLAT)
    sine = np.sin(theta)
    rows = np.zeros((4, 256))
    rows[0, :NLAT] = np.cos(theta)
    rows[1, :NLAT] = np.log(sine)
    rows[2, :NLAT] = sine / math.sqrt(NLAT)
    for m in range(MMAX):
        logs = math.lgamma(m + 1.5) - math.lgamma(1.5) - math.lgamma(m + 1.0)
        rows[3, m] = 0.5 * logs - 0.5 * math.log(2.0)
    return rows.astype(np.float32)


def call(kernel, out, specs, scratch=(), out_specs=None):
    return pl.pallas_call(
        kernel,
        out_shape=out,
        in_specs=specs,
        out_specs=out_specs or jax.tree.map(lambda _: VMEM, out),
        scratch_shapes=list(scratch),
        compiler_params=params(),
    )


def stay(x):
    return pltpu.with_memory_space_constraint(x, pltpu.HBM)


def shards(state, forcing, crm_moisture, cloud_order, wave_table):
    shape = jax.ShapeDtypeStruct
    state = state.transpose(0, 2, 3, 1, 4).reshape(ROWS, 1, LONS)
    forcing = forcing.transpose(0, 2, 3, 1, 4).reshape(ROWS, 1, LONS)
    moist = crm_moisture.transpose(0, 2, 3, 4, 1, 5).reshape(LEVELS, NCRM, RUNS)
    order = cloud_order.reshape(1, COLS)
    waves = wave_table.reshape(1, MMAX)
    outgoing, hot, cols = call(
        pack_kernel,
        (
            shape((TARGETS, 8, 128), F32),
            shape((COLS, COLS), BF16),
            shape((2 * LEVELS, COLS), F32),
        ),
        [HBM] * 3,
        [
            pltpu.VMEM((ROWS, 1, LONS), F32),
            pltpu.VMEM((ROWS, 1, LONS), F32),
            pltpu.VMEM((1, COLS), jnp.int32),
            pltpu.SemaphoreType.DMA((3,)),
        ],
    )(*(stay(x) for x in (state, forcing, order)))
    outgoing, waves = lax.optimization_barrier((outgoing, waves))
    arrived = lax.all_to_all(outgoing, ("sec", "lat"), split_axis=0, concat_axis=0, tiled=True)
    trig, weights, water = call(
        table_kernel,
        (
            shape((2 * MMAX, 384), BF16),
            shape((SLOTS_OWN, MMAX, 768), BF16),
            shape((LEVELS, 3, 4, 8, 128), F32),
        ),
        [HBM] * 3,
        [
            pltpu.VMEM((1, MMAX), jnp.int32),
            pltpu.VMEM((4, 256), F32),
            pltpu.VMEM((LEVELS, NCRM, RUNS), BF16),
            pltpu.VMEM((2, MMAX * SLOTS_OWN, 128), F32),
            pltpu.VMEM((MMAX, 128), F32),
            pltpu.VMEM((LEVELS, 3, NCRM, 128), F32),
            pltpu.VMEM((LEVELS, 3, 4, 8, 128), F32),
            pltpu.SemaphoreType.DMA((4,)),
        ],
        (VMEM, VMEM, HBM),
    )(*(stay(x) for x in (waves, jnp.asarray(geometry()), moist)))
    arrived, trig = lax.optimization_barrier((arrived, trig))
    rain = call(
        cloud_kernel,
        shape((TARGETS, 4, 128), F32),
        [VMEM, HBM],
        [
            pltpu.VMEM((3, 32, 128), F32),
            pltpu.VMEM((3, 56, 128), F32),
            pltpu.VMEM((3, 32, 128), F32),
            pltpu.VMEM((3, 32, 128), F32),
            pltpu.VMEM((3, 32, 128), F32),
            pltpu.VMEM((LEVELS, 3, 4, 8, 128), F32),
            pltpu.SemaphoreType.DMA,
        ],
    )(arrived, stay(water))
    returned = lax.all_to_all(rain, ("sec", "lat"), split_axis=0, concat_axis=0, tiled=True)
    updated, fourier = call(
        update_kernel,
        (shape((ROWS, 1, LONS), F32), shape((NL, NC, 4, 384), F32)),
        [VMEM] * 4,
        [pltpu.VMEM((32, COLS), F32), pltpu.VMEM((ROWS, 128), F32)],
    )(returned, hot, cols, trig)
    bands = lax.all_to_all(
        fourier.reshape(NL * NC, 4, 384), ("lat", "col"), split_axis=0, concat_axis=0, tiled=True
    )
    spectral = call(
        legendre_kernel,
        shape((LEV_OWN, SLOTS_OWN, 2, MMAX), F32),
        [VMEM] * 2,
        [pltpu.VMEM((2, LEV_OWN * 16, 128), F32)],
    )(bands.reshape(NL, NC, 4, 384), weights)
    new_state = updated.reshape(1, LEVELS, BAND, 1, LONS).transpose(0, 3, 1, 2, 4)
    return new_state, spectral[None, None]


def solution(mesh):
    placed = (
        P(None, "sec", None, "lat", "col"),
        P(None, "sec", None, "lat", "col"),
        P(None, None, None, ("sec", "lat"), "col", None),
        P("col", "lat", None),
        P(),
    )
    return jax.shard_map(
        shards,
        mesh=mesh,
        in_specs=placed,
        out_specs=(P(None, "sec", None, "lat", "col"), P("sec", None, "col", "lat", None, None)),
        check_vma=False,
    )
```

```python
import math

import jax
import jax.numpy as jnp
import numpy as np
from jax import lax
from jax.experimental import pallas as pl
from jax.experimental.pallas import tpu as pltpu
from jax.sharding import PartitionSpec as P

NLON = 384
NLAT = 192
MMAX = 128
NSUB = 4
NCRM = 32
LEVELS = 28
BAND = 12
LONS = 96
COLS = BAND * LONS
ROWS = LEVELS * BAND
TARGETS = 64
PER = 18
NL = 16
NS = 4
NC = 4
RUNS = NL * PER
HALF = 4 * PER
TAIL = RUNS - 256
LEV_OWN = LEVELS // NC
SLOTS_OWN = MMAX // NL

F32 = jnp.float32
BF16 = jnp.bfloat16
VMEM = pl.BlockSpec(memory_space=pltpu.VMEM)
HBM = pl.BlockSpec(memory_space=pltpu.HBM)


def split2(x):
    hi = x.astype(BF16)
    lo = (x - hi.astype(F32)).astype(BF16)
    return hi, lo


def params(mib=16):
    return pltpu.CompilerParams(vmem_limit_bytes=mib << 20)


def lanes_of(shape):
    return lax.broadcasted_iota(jnp.int32, shape, 1)


def fill_one_hot(order_ref, hot_ref):
    order = order_ref[...]
    step = 96
    for c in range(0, COLS, step):
        ids = lax.broadcasted_iota(jnp.int32, (step, COLS), 0) + c
        hot_ref[c : c + step, :] = jnp.where(ids == order, 1.0, 0.0).astype(BF16)


def trig_rows(orders, trig_ref):
    first = (lax.axis_index("col") * LONS).astype(F32)
    y = lax.broadcasted_iota(jnp.int32, (MMAX, 128), 1).astype(F32) + first
    product = y * orders
    phase = product - NLON * jnp.floor((product + 0.5) * (1.0 / NLON))
    turn = jnp.floor((phase + 48.5) * (1.0 / 96.0))
    x = (phase - 96.0 * turn) * (2.0 * math.pi / NLON)
    z = x * x
    sin = x * (1.0 + z * (-1.0 / 6 + z * (1.0 / 120 + z * (-1.0 / 5040 + z * (1.0 / 362880)))))
    cos = 1.0 + z * (-0.5 + z * (1.0 / 24 + z * (-1.0 / 720 + z * (1.0 / 40320))))
    odd = (turn == 1.0) | (turn == 3.0)
    cos_out = jnp.where(odd, sin, cos)
    sin_out = jnp.where(odd, cos, sin)
    cos_out = jnp.where((turn == 1.0) | (turn == 2.0), -cos_out, cos_out)
    sin_out = jnp.where((turn == 2.0) | (turn == 3.0), -sin_out, sin_out)
    norm = 1.0 / math.sqrt(NLON)
    halves = [
        part.reshape(NL, 2, 4, 128)[:, h].reshape(NL * 4, 128)
        for part in (cos_out * norm, sin_out * norm)
        for h in range(2)
    ]
    hi, lo = split2(jnp.concatenate(halves, axis=0))
    trig_ref[:, 0:128] = hi
    trig_ref[:, 128:256] = hi
    trig_ref[:, 256:384] = lo


def legendre_rows(order, geom_ref, poly_ref, weight_ref):
    lane = lanes_of((SLOTS_OWN, 128)).astype(F32)
    head = jnp.sum(jnp.where(lane == order, geom_ref[3:4, 0:128], 0.0), axis=1, keepdims=True)
    degree = lax.broadcasted_iota(jnp.int32, (SLOTS_OWN, 128), 1).astype(F32)
    active = degree > order
    numer = jnp.where(active, 4.0 * degree * degree - 1.0, 0.0)
    denom = jnp.where(active, degree * degree - order * order, 1.0)
    grow = jnp.sqrt(numer / denom)
    lower = degree - 1.0
    retreat = jnp.sqrt(
        jnp.maximum(lower * lower - order * order, 0.0) / (4.0 * lower * lower - 1.0)
    )
    retreat = grow * retreat
    begin = jnp.where(degree == order, 1.0, 0.0)
    diagonal = jnp.exp(head + order[:, 0:1] * geom_ref[1:2, :]) * geom_ref[2:3, :]
    cosine = jnp.broadcast_to(geom_ref[0:1, :], (SLOTS_OWN, 256))
    previous = jnp.zeros((SLOTS_OWN, 256), F32)
    current = previous
    for n in range(MMAX):
        fresh = (grow[:, n : n + 1] * cosine) * current + (
            begin[:, n : n + 1] * diagonal - retreat[:, n : n + 1] * previous
        )
        poly_ref[0, n * 8 : n * 8 + 8, :] = fresh[:, :128]
        poly_ref[1, n * 8 : n * 8 + 8, :] = fresh[:, 128:]
        previous, current = current, fresh
    for s in range(SLOTS_OWN):
        for h in range(2):
            hi, lo = split2(poly_ref[h, pl.ds(s, MMAX, stride=8), :])
            for part, block in ((hi, 0), (lo, 2), (hi, 4)):
                at = (block + h) * 128
                weight_ref[s, :, at : at + 128] = part


def arrange_moisture(moist_ref, level_ref, water_ref, tail_ref):
    lane = lanes_of((8, 128))
    blank = jnp.zeros((NCRM, 384 - RUNS), F32)
    for k in range(LEVELS):
        level = jnp.concatenate((moist_ref[k].astype(F32), blank), axis=1)
        for v in range(3):
            level_ref[k, v] = level[:, v * 128 : v * 128 + 128]
    for k in range(LEVELS):
        for v in range(2):
            for n in range(4):
                water_ref[k, v, n] = level_ref[k, v, pl.ds(n, 8, stride=4), :]
    for g in range(LEVELS // 4):
        for n in range(4):
            tile = level_ref[4 * g, 2, pl.ds(n, 8, stride=4), :]
            for kk in range(1, 4):
                more = pltpu.roll(level_ref[4 * g + kk, 2, pl.ds(n, 8, stride=4), :], kk * TAIL, 1)
                tile = jnp.where(lane >= kk * TAIL, more, tile)
            tail_ref[g, n] = tile


def pack_kernel(
    state_hbm,
    force_hbm,
    order_hbm,
    wave_hbm,
    geom_hbm,
    moist_hbm,
    out_ref,
    hot_ref,
    cols_ref,
    trig_ref,
    weight_ref,
    water_ref,
    tail_ref,
    state_ref,
    force_ref,
    order_ref,
    wave_ref,
    geom_ref,
    moist_ref,
    poly_ref,
    orders_ref,
    level_ref,
    sems,
):
    pairs = (
        (wave_hbm, wave_ref),
        (geom_hbm, geom_ref),
        (order_hbm, order_ref),
        (state_hbm, state_ref),
        (force_hbm, force_ref),
        (moist_hbm, moist_ref),
    )
    loads = [pltpu.make_async_copy(src, dst, sems.at[n]) for n, (src, dst) in enumerate(pairs)]
    for load in loads:
        load.start()
    for load in loads[:3]:
        load.wait()
    fill_one_hot(order_ref, hot_ref)
    orders = jnp.broadcast_to(wave_ref[...].astype(F32), (MMAX, MMAX)).T
    orders_ref[...] = orders
    trig_rows(orders, trig_ref)
    first = pl.multiple_of(lax.axis_index("lat") * SLOTS_OWN, SLOTS_OWN)
    legendre_rows(orders_ref[pl.ds(first, SLOTS_OWN), :], geom_ref, poly_ref, weight_ref)
    for load in loads[3:]:
        load.wait()
    arrange_moisture(moist_ref, level_ref, water_ref, tail_ref)
    for ref, base in ((state_ref, 0), (force_ref, LEVELS)):
        rows = ref[...].reshape(LEVELS, BAND, LONS)
        for b in range(BAND):
            cols_ref[base : base + LEVELS, b * LONS : (b + 1) * LONS] = rows[:, b, :]
    hi, lo = split2(cols_ref[...])
    both = jnp.concatenate((hi, lo), axis=0)
    got = jnp.dot(both, hot_ref[...], preferred_element_type=F32)
    got = got[: 2 * LEVELS] + got[2 * LEVELS :]
    lane = lanes_of((8, 128))
    groups = 2 * LEVELS // 8
    for t in range(TARGETS):
        v, off = divmod(t * PER, 128)
        tile = None
        for q in range(groups):
            src = got[q * 8 : q * 8 + 8, v * 128 : v * 128 + 128]
            if off + PER > 128:
                nxt = got[q * 8 : q * 8 + 8, v * 128 + 128 : v * 128 + 256]
                src = jnp.where(lane < off, nxt, src)
            shift = (q * PER - off) % 128
            if shift:
                src = pltpu.roll(src, shift, 1)
            tile = src if tile is None else jnp.where(lane >= q * PER, src, tile)
        out_ref[t] = tile


def gather_lanes(tile_of, q_list, first, count, width, store):
    lane = lanes_of((8, 128))
    for q in q_list:
        for v in range(pl.cdiv(width, 128)):
            acc = None
            for i in range(count):
                start = i * PER - v * 128
                if start >= 128 or start + PER <= 0:
                    continue
                src = tile_of(first + i)
                shift = (i * PER - q * PER) % 128
                if shift:
                    src = pltpu.roll(src, shift, 1)
                acc = src if acc is None else jnp.where(lane >= start, src, acc)
            store(q, v, acc)


def coefficients(wind):
    courant = 0.4 * jnp.tanh(wind)
    mixing = 0.2 + 0.5 * jnp.abs(courant)
    return mixing - 0.5 * courant, mixing + 0.5 * courant


def cloud_tile(start, push, ahead, behind, water):
    keep = 1.0 - (ahead + behind)
    gap = [start + w for w in water]
    wet = [jnp.maximum(g, 0.0) for g in gap]
    total = (wet[0] + wet[1]) + (wet[2] + wet[3])
    for _ in range(NSUB - 1):
        up = gap[1:] + [pltpu.roll(gap[0], 7, 0)]
        down = [pltpu.roll(gap[3], 1, 0)] + gap[:3]
        gap = [
            ((keep * gap[n] - wet[n]) + push) + (ahead * up[n] + behind * down[n]) for n in range(4)
        ]
        wet = [jnp.maximum(g, 0.0) for g in gap]
        total = total + ((wet[0] + wet[1]) + (wet[2] + wet[3]))
    return jnp.sum(total, axis=0, keepdims=True) * (0.5 / NCRM)


def cloud_kernel(
    got_ref,
    water_ref,
    tail_ref,
    out_ref,
    wind_ref,
    diff_ref,
    push_ref,
    left_ref,
    right_ref,
    rain_ref,
    last_ref,
):
    def store_wind(q, v, x):
        wind_ref[v, q * 8 : q * 8 + 8, :] = x

    def store_diff(q, v, x):
        diff_ref[v, q * 8 : q * 8 + 8, :] = x

    gather_lanes(lambda i: got_ref[i], range(4), 0, NL, RUNS, store_wind)
    cache = {}

    def diff(i):
        if i not in cache:
            cache[i] = got_ref[3 * NL + i] - got_ref[2 * NL + i]
        return cache[i]

    gather_lanes(diff, range(7), 0, NL, RUNS, store_diff)
    lane = lanes_of((8, 128))
    groups = LEVELS // 4

    def tails(ref, base):
        tile = ref[2, pl.ds(base, 8, stride=4), :]
        for kk in range(1, 4):
            more = pltpu.roll(ref[2, pl.ds(base + kk, 8, stride=4), :], kk * TAIL, 1)
            tile = jnp.where(lane >= kk * TAIL, more, tile)
        return tile

    wind_tail = tails(wind_ref, 0)
    diff_tail = tails(diff_ref, 0)
    push_tail = tails(diff_ref, LEVELS) * (1.0 / NSUB)
    for v in range(2):
        left_ref[v], right_ref[v] = coefficients(wind_ref[v])
        push_ref[v] = diff_ref[v, LEVELS : LEVELS + 32, :] * (1.0 / NSUB)
    last_ref[4] = jnp.zeros_like(diff_tail)
    last_ref[0] = diff_tail
    last_ref[1] = push_tail
    last_ref[2], last_ref[3] = coefficients(wind_tail)
    rain_ref[...] = jnp.zeros_like(rain_ref)

    def level(g, carry):
        for kk in range(4):
            k = 4 * g + kk
            for v in range(2):

                def row(ref):
                    return jnp.broadcast_to(ref[v, pl.ds(k, 1), :], (8, 128))

                rain_ref[v, pl.ds(k, 1), :] = cloud_tile(
                    row(diff_ref),
                    row(push_ref),
                    row(left_ref),
                    row(right_ref),
                    [water_ref[k, v, n] for n in range(4)],
                )
        rows = [jnp.broadcast_to(last_ref[c, pl.ds(g, 1), :], (8, 128)) for c in range(4)]
        last_ref[4, pl.ds(g, 1), :] = cloud_tile(*rows, [tail_ref[g, n] for n in range(4)])
        return carry

    lax.fori_loop(0, groups, level, 0)
    rain_tail = last_ref[4]
    for kk in range(4):
        piece = rain_tail if kk == 0 else pltpu.roll(rain_tail, 128 - kk * TAIL, 1)
        rain_ref[2, pl.ds(kk, 8, stride=4), :] = piece
    for i in range(NL):
        v, off = divmod(i * PER, 128)
        tile = None
        for q in range(4):
            src = rain_ref[v, q * 8 : q * 8 + 8, :]
            if off + PER > 128:
                nxt = rain_ref[v + 1, q * 8 : q * 8 + 8, :]
                src = jnp.where(lane < off, nxt, src)
            shift = (q * PER - off) % 128
            if shift:
                src = pltpu.roll(src, shift, 1)
            tile = src if tile is None else jnp.where(lane >= q * PER, src, tile)
        low = tile[0:4]
        high = pltpu.roll(tile, HALF, 1)[4:8]
        tile = jnp.where(lane[0:4] < HALF, low, high)
        for s in range(NS):
            out_ref[s * NL + i] = tile


def update_kernel(
    got_ref, hot_ref, cols_ref, trig_ref, out_hbm, four_ref, slots_ref, rows_ref, out_ref, sem
):
    def store(q, v, x):
        slots_ref[q * 8 : q * 8 + 8, v * 128 : v * 128 + 128] = x

    cache = {}

    def tile_of(t):
        if t not in cache:
            tile = got_ref[t]
            cache[t] = jnp.concatenate((tile, pltpu.roll(tile, 128 - HALF, 1)), axis=0)
        return cache[t]

    gather_lanes(tile_of, range(4), 0, TARGETS, COLS, store)
    hi, lo = split2(slots_ref[...])
    both = jnp.concatenate((hi, lo), axis=0)
    back = lax.dot_general(both, hot_ref[...], (((1,), (1,)), ((), ())), preferred_element_type=F32)
    rain = back[:LEVELS] + back[32 : 32 + LEVELS]
    sec = lax.axis_index("sec")
    add = jnp.where(sec == 2, 1.0, jnp.where(sec == 3, -1.0, 0.0)).astype(F32)
    scale = jnp.where(sec < 2, -1.0 / NSUB, 0.0).astype(F32)
    now = cols_ref[0:LEVELS]
    now = now + (cols_ref[LEVELS : 2 * LEVELS] + rain * (add + scale * now))
    blank = jnp.zeros((LEVELS, 128 - LONS), F32)
    for b in range(BAND):
        piece = jnp.concatenate((now[:, b * LONS : (b + 1) * LONS], blank), axis=1)
        rows_ref[pl.ds(b, LEVELS, stride=BAND), :] = piece
    rows = rows_ref[...]
    out_ref[...] = rows[:, :LONS].reshape(ROWS, 1, LONS)
    save = pltpu.make_async_copy(out_ref, out_hbm, sem)
    save.start()
    hi, lo = split2(rows)
    dims = (((1,), (1,)), ((), ()))
    parts = jnp.concatenate((hi, lo, hi), axis=1)
    out = lax.dot_general(trig_ref[...], parts, dims, preferred_element_type=F32)
    width = LEV_OWN * BAND
    blank = jnp.zeros((NL * 4, 384 - 4 * width), F32)
    for j in range(NC):
        pieces = [out[g * 64 : g * 64 + 64, j * width : (j + 1) * width] for g in range(4)]
        four_ref[:, j] = jnp.concatenate(pieces + [blank], axis=1).reshape(NL, 4, 384)
    save.wait()


def legendre_kernel(got_ref, weight_ref, out_hbm, band_ref, out_ref, sems):
    width = LEV_OWN * BAND
    band_ref[1] = jnp.zeros_like(band_ref[1])
    for i in range(NL):
        part = (got_ref[i, 0] + got_ref[i, 1]) + (got_ref[i, 2] + got_ref[i, 3])
        bands = jnp.concatenate([part[:, g * width : (g + 1) * width] for g in range(4)], axis=0)
        h, at = divmod(i * BAND, 128)
        first = min(BAND, 128 - at)
        for k in range(LEV_OWN):
            row = slice(k * 16, k * 16 + 16)
            piece = bands[:, k * BAND : (k + 1) * BAND]
            band_ref[h, row, at : at + first] = piece[:, :first]
            if first < BAND:
                band_ref[h + 1, row, 0 : BAND - first] = piece[:, first:]
    dims = (((1,), (1,)), ((), ()))
    saves = []
    for s in range(SLOTS_OWN):
        rows = [band_ref[h, pl.ds(s, 2 * LEV_OWN, stride=8), :] for h in range(2)]
        hi, lo = split2(jnp.concatenate(rows, axis=1))
        parts = jnp.concatenate((hi, hi, lo), axis=1)
        out = lax.dot_general(parts, weight_ref[s], dims, preferred_element_type=F32)
        out_ref[:, s, :, :] = out.reshape(LEV_OWN, 2, MMAX)
        if s % 4 == 3:
            part = pl.ds(s - 3, 4)
            save = pltpu.make_async_copy(out_ref.at[:, part], out_hbm.at[:, part], sems.at[s // 4])
            save.start()
            saves.append(save)
    for save in saves:
        save.wait()


def geometry():
    theta = (np.arange(NLAT) + 0.5) * (math.pi / NLAT)
    sine = np.sin(theta)
    rows = np.zeros((4, 256))
    rows[0, :NLAT] = np.cos(theta)
    rows[1, :NLAT] = np.log(sine)
    rows[2, :NLAT] = sine / math.sqrt(NLAT)
    for m in range(MMAX):
        logs = math.lgamma(m + 1.5) - math.lgamma(1.5) - math.lgamma(m + 1.0)
        rows[3, m] = 0.5 * logs - 0.5 * math.log(2.0)
    return rows.astype(np.float32)


def call(kernel, out, specs, scratch=(), out_specs=None):
    return pl.pallas_call(
        kernel,
        out_shape=out,
        in_specs=specs,
        out_specs=out_specs or jax.tree.map(lambda _: VMEM, out),
        scratch_shapes=list(scratch),
        compiler_params=params(),
    )


def stay(x):
    return pltpu.with_memory_space_constraint(x, pltpu.HBM)


def shards(state, forcing, crm_moisture, cloud_order, wave_table):
    shape = jax.ShapeDtypeStruct
    state = state.transpose(0, 2, 3, 1, 4).reshape(ROWS, 1, LONS)
    forcing = forcing.transpose(0, 2, 3, 1, 4).reshape(ROWS, 1, LONS)
    moist = crm_moisture.transpose(0, 2, 3, 4, 1, 5).reshape(LEVELS, NCRM, RUNS)
    order = cloud_order.reshape(1, COLS)
    waves = wave_table.reshape(1, MMAX)
    outgoing, hot, cols, trig, weights, water, tail = call(
        pack_kernel,
        (
            shape((TARGETS, 8, 128), F32),
            shape((COLS, COLS), BF16),
            shape((2 * LEVELS, COLS), F32),
            shape((2 * MMAX, 384), BF16),
            shape((SLOTS_OWN, MMAX, 768), BF16),
            shape((LEVELS, 2, 4, 8, 128), F32),
            shape((LEVELS // 4, 4, 8, 128), F32),
        ),
        [HBM] * 6,
        [
            pltpu.VMEM((ROWS, 1, LONS), F32),
            pltpu.VMEM((ROWS, 1, LONS), F32),
            pltpu.VMEM((1, COLS), jnp.int32),
            pltpu.VMEM((1, MMAX), jnp.int32),
            pltpu.VMEM((4, 256), F32),
            pltpu.VMEM((LEVELS, NCRM, RUNS), BF16),
            pltpu.VMEM((2, MMAX * SLOTS_OWN, 128), F32),
            pltpu.VMEM((MMAX, 128), F32),
            pltpu.VMEM((LEVELS, 3, NCRM, 128), F32),
            pltpu.SemaphoreType.DMA((6,)),
        ],
    )(*(stay(x) for x in (state, forcing, order, waves, jnp.asarray(geometry()), moist)))
    arrived = lax.all_to_all(outgoing, ("sec", "lat"), split_axis=0, concat_axis=0, tiled=True)
    rain = call(
        cloud_kernel,
        shape((TARGETS, 4, 128), F32),
        [VMEM] * 3,
        [
            pltpu.VMEM((3, 32, 128), F32),
            pltpu.VMEM((3, 64, 128), F32),
            pltpu.VMEM((2, 32, 128), F32),
            pltpu.VMEM((2, 32, 128), F32),
            pltpu.VMEM((2, 32, 128), F32),
            pltpu.VMEM((3, 32, 128), F32),
            pltpu.VMEM((5, 8, 128), F32),
        ],
    )(arrived, water, tail)
    returned = lax.all_to_all(rain, ("sec", "lat"), split_axis=0, concat_axis=0, tiled=True)
    updated, fourier = call(
        update_kernel,
        (shape((ROWS, 1, LONS), F32), shape((NL, NC, 4, 384), F32)),
        [VMEM] * 4,
        [
            pltpu.VMEM((32, COLS), F32),
            pltpu.VMEM((ROWS, 128), F32),
            pltpu.VMEM((ROWS, 1, LONS), F32),
            pltpu.SemaphoreType.DMA,
        ],
        (HBM, VMEM),
    )(returned, hot, cols, trig)
    bands = lax.all_to_all(
        fourier.reshape(NL * NC, 4, 384), ("lat", "col"), split_axis=0, concat_axis=0, tiled=True
    )
    spectral = call(
        legendre_kernel,
        shape((LEV_OWN, SLOTS_OWN, 2, MMAX), F32),
        [VMEM] * 2,
        [
            pltpu.VMEM((2, LEV_OWN * 16, 128), F32),
            pltpu.VMEM((LEV_OWN, SLOTS_OWN, 2, MMAX), F32),
            pltpu.SemaphoreType.DMA((2,)),
        ],
        HBM,
    )(bands.reshape(NL, NC, 4, 384), weights)
    new_state = updated.reshape(1, LEVELS, BAND, 1, LONS).transpose(0, 3, 1, 2, 4)
    return new_state, spectral[None, None]


def solution(mesh):
    placed = (
        P(None, "sec", None, "lat", "col"),
        P(None, "sec", None, "lat", "col"),
        P(None, None, None, ("sec", "lat"), "col", None),
        P("col", "lat", None),
        P(),
    )
    return jax.shard_map(
        shards,
        mesh=mesh,
        in_specs=placed,
        out_specs=(P(None, "sec", None, "lat", "col"), P("sec", None, "col", "lat", None, None)),
        check_vma=False,
    )
```

```python
import math

import jax
import jax.numpy as jnp
import numpy as np
from jax import lax
from jax.experimental import pallas as pl
from jax.experimental.pallas import tpu as pltpu
from jax.sharding import PartitionSpec as P

NLON = 384
NLAT = 192
MMAX = 128
NSUB = 4
NCRM = 32
LEVELS = 28
BAND = 12
LONS = 96
COLS = BAND * LONS
ROWS = LEVELS * BAND
TARGETS = 64
PER = 18
NL = 16
NS = 4
NC = 4
RUNS = NL * PER
HALF = 4 * PER
TAIL = RUNS - 256
LEV_OWN = LEVELS // NC
SLOTS_OWN = MMAX // NL

F32 = jnp.float32
BF16 = jnp.bfloat16
VMEM = pl.BlockSpec(memory_space=pltpu.VMEM)
HBM = pl.BlockSpec(memory_space=pltpu.HBM)


def split2(x):
    hi = x.astype(BF16)
    lo = (x - hi.astype(F32)).astype(BF16)
    return hi, lo


def params(mib=16):
    return pltpu.CompilerParams(vmem_limit_bytes=mib << 20)


def lanes_of(shape):
    return lax.broadcasted_iota(jnp.int32, shape, 1)


def fill_one_hot(order_ref, hot_ref):
    order = order_ref[...]
    step = 96
    for c in range(0, COLS, step):
        ids = lax.broadcasted_iota(jnp.int32, (step, COLS), 0) + c
        hot_ref[c : c + step, :] = jnp.where(ids == order, 1.0, 0.0).astype(BF16)


def trig_rows(orders, trig_ref):
    first = (lax.axis_index("col") * LONS).astype(F32)
    y = lax.broadcasted_iota(jnp.int32, (MMAX, 128), 1).astype(F32) + first
    product = y * orders
    phase = product - NLON * jnp.floor((product + 0.5) * (1.0 / NLON))
    turn = jnp.floor((phase + 48.5) * (1.0 / 96.0))
    x = (phase - 96.0 * turn) * (2.0 * math.pi / NLON)
    z = x * x
    sin = x * (1.0 + z * (-1.0 / 6 + z * (1.0 / 120 + z * (-1.0 / 5040 + z * (1.0 / 362880)))))
    cos = 1.0 + z * (-0.5 + z * (1.0 / 24 + z * (-1.0 / 720 + z * (1.0 / 40320))))
    odd = (turn == 1.0) | (turn == 3.0)
    cos_out = jnp.where(odd, sin, cos)
    sin_out = jnp.where(odd, cos, sin)
    cos_out = jnp.where((turn == 1.0) | (turn == 2.0), -cos_out, cos_out)
    sin_out = jnp.where((turn == 2.0) | (turn == 3.0), -sin_out, sin_out)
    norm = 1.0 / math.sqrt(NLON)
    halves = [
        part.reshape(NL, 2, 4, 128)[:, h].reshape(NL * 4, 128)
        for part in (cos_out * norm, sin_out * norm)
        for h in range(2)
    ]
    hi, lo = split2(jnp.concatenate(halves, axis=0))
    trig_ref[:, 0:128] = hi
    trig_ref[:, 128:256] = hi
    trig_ref[:, 256:384] = lo


def legendre_rows(order, geom_ref, poly_ref, weight_ref):
    lane = lanes_of((SLOTS_OWN, 128)).astype(F32)
    head = jnp.sum(jnp.where(lane == order, geom_ref[3:4, 0:128], 0.0), axis=1, keepdims=True)
    degree = lax.broadcasted_iota(jnp.int32, (SLOTS_OWN, 128), 1).astype(F32)
    active = degree > order
    numer = jnp.where(active, 4.0 * degree * degree - 1.0, 0.0)
    denom = jnp.where(active, degree * degree - order * order, 1.0)
    grow = jnp.sqrt(numer / denom)
    lower = degree - 1.0
    retreat = jnp.sqrt(
        jnp.maximum(lower * lower - order * order, 0.0) / (4.0 * lower * lower - 1.0)
    )
    retreat = grow * retreat
    begin = jnp.where(degree == order, 1.0, 0.0)
    diagonal = jnp.exp(head + order[:, 0:1] * geom_ref[1:2, :]) * geom_ref[2:3, :]
    cosine = jnp.broadcast_to(geom_ref[0:1, :], (SLOTS_OWN, 256))
    previous = jnp.zeros((SLOTS_OWN, 256), F32)
    current = previous
    for n in range(MMAX):
        fresh = (grow[:, n : n + 1] * cosine) * current + (
            begin[:, n : n + 1] * diagonal - retreat[:, n : n + 1] * previous
        )
        poly_ref[0, n * 8 : n * 8 + 8, :] = fresh[:, :128]
        poly_ref[1, n * 8 : n * 8 + 8, :] = fresh[:, 128:]
        previous, current = current, fresh
    for s in range(SLOTS_OWN):
        for h in range(2):
            hi, lo = split2(poly_ref[h, pl.ds(s, MMAX, stride=8), :])
            for part, block in ((hi, 0), (lo, 2)):
                at = (block + h) * 128
                weight_ref[s, :, at : at + 128] = part


def arrange_moisture(moist_ref, level_ref, water_ref, tail_ref):
    lane = lanes_of((8, 128))
    blank = jnp.zeros((NCRM, 384 - RUNS), F32)
    for k in range(LEVELS):
        level = jnp.concatenate((moist_ref[k].astype(F32), blank), axis=1)
        for v in range(3):
            level_ref[k, v] = level[:, v * 128 : v * 128 + 128]
    for k in range(LEVELS):
        for v in range(2):
            for n in range(4):
                water_ref[k, v, n] = level_ref[k, v, pl.ds(n, 8, stride=4), :]
    for g in range(LEVELS // 4):
        for n in range(4):
            tile = level_ref[4 * g, 2, pl.ds(n, 8, stride=4), :]
            for kk in range(1, 4):
                more = pltpu.roll(level_ref[4 * g + kk, 2, pl.ds(n, 8, stride=4), :], kk * TAIL, 1)
                tile = jnp.where(lane >= kk * TAIL, more, tile)
            tail_ref[g, n] = tile


def table_kernel(
    wave_hbm,
    geom_hbm,
    order_hbm,
    moist_hbm,
    trig_ref,
    weight_ref,
    water_ref,
    tail_ref,
    column_ref,
    wave_ref,
    geom_ref,
    order_ref,
    moist_ref,
    poly_ref,
    orders_ref,
    level_ref,
    sems,
):
    pairs = (
        (wave_hbm, wave_ref),
        (geom_hbm, geom_ref),
        (order_hbm, order_ref),
        (moist_hbm, moist_ref),
    )
    loads = [pltpu.make_async_copy(src, dst, sems.at[n]) for n, (src, dst) in enumerate(pairs)]
    for load in loads:
        load.start()
    for load in loads[:3]:
        load.wait()
    orders = jnp.broadcast_to(wave_ref[...].astype(F32), (MMAX, MMAX)).T
    orders_ref[...] = orders
    trig_rows(orders, trig_ref)
    first = pl.multiple_of(lax.axis_index("lat") * SLOTS_OWN, SLOTS_OWN)
    legendre_rows(orders_ref[pl.ds(first, SLOTS_OWN), :], geom_ref, poly_ref, weight_ref)
    order = order_ref[...].astype(F32)
    for v in range(COLS // 128):
        at = slice(v * 128, v * 128 + 128)
        column_ref[at, :] = jnp.broadcast_to(order[:, at], (128, 128)).T
    loads[3].wait()
    arrange_moisture(moist_ref, level_ref, water_ref, tail_ref)


def pack_kernel(
    state_hbm,
    force_hbm,
    order_hbm,
    out_hbm,
    cols_ref,
    state_ref,
    force_ref,
    order_ref,
    hot_ref,
    out_ref,
    sems,
):
    half = ROWS // 2
    pairs = [(order_hbm, order_ref)]
    for part in (pl.ds(0, half), pl.ds(half, half)):
        pairs.append((state_hbm.at[part], state_ref.at[part]))
        pairs.append((force_hbm.at[part], force_ref.at[part]))
    loads = [pltpu.make_async_copy(src, dst, sems.at[n]) for n, (src, dst) in enumerate(pairs)]
    for load in loads:
        load.start()
    loads[0].wait()
    fill_one_hot(order_ref, hot_ref)
    for load in loads[1:]:
        load.wait()
    for ref, base in ((state_ref, 0), (force_ref, LEVELS)):
        rows = ref[...].reshape(LEVELS, BAND, LONS)
        for b in range(BAND):
            cols_ref[base : base + LEVELS, b * LONS : (b + 1) * LONS] = rows[:, b, :]
    hi, lo = split2(cols_ref[...])
    both = jnp.concatenate((hi, lo), axis=0)
    got = jnp.dot(both, hot_ref[...], preferred_element_type=F32)
    got = got[: 2 * LEVELS] + got[2 * LEVELS :]
    lane = lanes_of((8, 128))
    groups = 2 * LEVELS // 8
    saves = []
    for t in range(TARGETS):
        v, off = divmod(t * PER, 128)
        tile = None
        for q in range(groups):
            src = got[q * 8 : q * 8 + 8, v * 128 : v * 128 + 128]
            if off + PER > 128:
                nxt = got[q * 8 : q * 8 + 8, v * 128 + 128 : v * 128 + 256]
                src = jnp.where(lane < off, nxt, src)
            shift = (q * PER - off) % 128
            if shift:
                src = pltpu.roll(src, shift, 1)
            tile = src if tile is None else jnp.where(lane >= q * PER, src, tile)
        out_ref[t] = tile
        if t % 16 == 15:
            part = pl.ds(t - 15, 16)
            save = pltpu.make_async_copy(out_ref.at[part], out_hbm.at[part], sems.at[5 + t // 16])
            save.start()
            saves.append(save)
    for save in saves:
        save.wait()


def gather_lanes(tile_of, q_list, first, count, width, store):
    lane = lanes_of((8, 128))
    for q in q_list:
        for v in range(pl.cdiv(width, 128)):
            acc = None
            for i in range(count):
                start = i * PER - v * 128
                if start >= 128 or start + PER <= 0:
                    continue
                src = tile_of(first + i)
                shift = (i * PER - q * PER) % 128
                if shift:
                    src = pltpu.roll(src, shift, 1)
                acc = src if acc is None else jnp.where(lane >= start, src, acc)
            store(q, v, acc)


def coefficients(wind):
    courant = 0.4 * jnp.tanh(wind)
    mixing = 0.2 + 0.5 * jnp.abs(courant)
    return mixing - 0.5 * courant, mixing + 0.5 * courant


def cloud_tile(start, push, ahead, behind, water):
    keep = 1.0 - (ahead + behind)
    gap = [start + w for w in water]
    wet = [jnp.maximum(g, 0.0) for g in gap]
    total = (wet[0] + wet[1]) + (wet[2] + wet[3])
    for _ in range(NSUB - 1):
        up = gap[1:] + [pltpu.roll(gap[0], 7, 0)]
        down = [pltpu.roll(gap[3], 1, 0)] + gap[:3]
        gap = [
            ((keep * gap[n] - wet[n]) + push) + (ahead * up[n] + behind * down[n]) for n in range(4)
        ]
        wet = [jnp.maximum(g, 0.0) for g in gap]
        total = total + ((wet[0] + wet[1]) + (wet[2] + wet[3]))
    return jnp.sum(total, axis=0, keepdims=True) * (0.5 / NCRM)


def cloud_kernel(
    got_ref,
    water_ref,
    tail_ref,
    out_ref,
    wind_ref,
    diff_ref,
    push_ref,
    left_ref,
    right_ref,
    rain_ref,
    last_ref,
):
    def store_wind(q, v, x):
        wind_ref[v, q * 8 : q * 8 + 8, :] = x

    def store_diff(q, v, x):
        diff_ref[v, q * 8 : q * 8 + 8, :] = x

    gather_lanes(lambda i: got_ref[i], range(4), 0, NL, RUNS, store_wind)
    cache = {}

    def diff(i):
        if i not in cache:
            cache[i] = got_ref[3 * NL + i] - got_ref[2 * NL + i]
        return cache[i]

    gather_lanes(diff, range(7), 0, NL, RUNS, store_diff)
    lane = lanes_of((8, 128))
    groups = LEVELS // 4

    def tails(ref, base):
        tile = ref[2, pl.ds(base, 8, stride=4), :]
        for kk in range(1, 4):
            more = pltpu.roll(ref[2, pl.ds(base + kk, 8, stride=4), :], kk * TAIL, 1)
            tile = jnp.where(lane >= kk * TAIL, more, tile)
        return tile

    wind_tail = tails(wind_ref, 0)
    diff_tail = tails(diff_ref, 0)
    push_tail = tails(diff_ref, LEVELS) * (1.0 / NSUB)
    for v in range(2):
        left_ref[v], right_ref[v] = coefficients(wind_ref[v])
        push_ref[v] = diff_ref[v, LEVELS : LEVELS + 32, :] * (1.0 / NSUB)
    last_ref[4] = jnp.zeros_like(diff_tail)
    last_ref[0] = diff_tail
    last_ref[1] = push_tail
    last_ref[2], last_ref[3] = coefficients(wind_tail)
    rain_ref[...] = jnp.zeros_like(rain_ref)

    def level(g, carry):
        for kk in range(4):
            k = 4 * g + kk
            for v in range(2):

                def row(ref):
                    return jnp.broadcast_to(ref[v, pl.ds(k, 1), :], (8, 128))

                rain_ref[v, pl.ds(k, 1), :] = cloud_tile(
                    row(diff_ref),
                    row(push_ref),
                    row(left_ref),
                    row(right_ref),
                    [water_ref[k, v, n] for n in range(4)],
                )
        rows = [jnp.broadcast_to(last_ref[c, pl.ds(g, 1), :], (8, 128)) for c in range(4)]
        last_ref[4, pl.ds(g, 1), :] = cloud_tile(*rows, [tail_ref[g, n] for n in range(4)])
        return carry

    lax.fori_loop(0, groups, level, 0)
    rain_tail = last_ref[4]
    for kk in range(4):
        piece = rain_tail if kk == 0 else pltpu.roll(rain_tail, 128 - kk * TAIL, 1)
        rain_ref[2, pl.ds(kk, 8, stride=4), :] = piece
    for i in range(NL):
        v, off = divmod(i * PER, 128)
        tile = None
        for q in range(4):
            src = rain_ref[v, q * 8 : q * 8 + 8, :]
            if off + PER > 128:
                nxt = rain_ref[v + 1, q * 8 : q * 8 + 8, :]
                src = jnp.where(lane < off, nxt, src)
            shift = (q * PER - off) % 128
            if shift:
                src = pltpu.roll(src, shift, 1)
            tile = src if tile is None else jnp.where(lane >= q * PER, src, tile)
        low = tile[0:4]
        high = pltpu.roll(tile, HALF, 1)[4:8]
        tile = jnp.where(lane[0:4] < HALF, low, high)
        for s in range(NS):
            out_ref[s * NL + i] = tile


def update_kernel(
    got_ref,
    column_ref,
    cols_ref,
    trig_ref,
    out_hbm,
    four_ref,
    slots_ref,
    rows_ref,
    out_ref,
    hot_ref,
    sem,
):
    lane = lanes_of((128, 128)).astype(F32)
    for v in range(COLS // 128):
        rows = slice(v * 128, v * 128 + 128)
        column = column_ref[rows, :]
        for c in range(COLS // 128):
            hot = jnp.where(lane + float(c * 128) == column, 1.0, 0.0)
            hot_ref[rows, c * 128 : c * 128 + 128] = hot.astype(BF16)

    def store(q, v, x):
        slots_ref[q * 8 : q * 8 + 8, v * 128 : v * 128 + 128] = x

    cache = {}

    def tile_of(t):
        if t not in cache:
            tile = got_ref[t]
            cache[t] = jnp.concatenate((tile, pltpu.roll(tile, 128 - HALF, 1)), axis=0)
        return cache[t]

    gather_lanes(tile_of, range(4), 0, TARGETS, COLS, store)
    hi, lo = split2(slots_ref[...])
    both = jnp.concatenate((hi, lo), axis=0)
    back = jnp.dot(both, hot_ref[...], preferred_element_type=F32)
    rain = back[:LEVELS] + back[32 : 32 + LEVELS]
    sec = lax.axis_index("sec")
    add = jnp.where(sec == 2, 1.0, jnp.where(sec == 3, -1.0, 0.0)).astype(F32)
    scale = jnp.where(sec < 2, -1.0 / NSUB, 0.0).astype(F32)
    now = cols_ref[0:LEVELS]
    now = now + (cols_ref[LEVELS : 2 * LEVELS] + rain * (add + scale * now))
    blank = jnp.zeros((LEVELS, 128 - LONS), F32)
    for b in range(BAND):
        piece = jnp.concatenate((now[:, b * LONS : (b + 1) * LONS], blank), axis=1)
        rows_ref[pl.ds(b, LEVELS, stride=BAND), :] = piece
    rows = rows_ref[...]
    out_ref[...] = rows[:, :LONS].reshape(ROWS, 1, LONS)
    save = pltpu.make_async_copy(out_ref, out_hbm, sem)
    save.start()
    hi, lo = split2(rows)
    dims = (((1,), (1,)), ((), ()))
    parts = jnp.concatenate((hi, lo, hi), axis=1)
    out = lax.dot_general(trig_ref[...], parts, dims, preferred_element_type=F32)
    width = LEV_OWN * BAND
    blank = jnp.zeros((NL * 4, 384 - 4 * width), F32)
    for j in range(NC):
        pieces = [out[g * 64 : g * 64 + 64, j * width : (j + 1) * width] for g in range(4)]
        four_ref[:, j] = jnp.concatenate(pieces + [blank], axis=1).reshape(NL, 4, 384)
    save.wait()


def legendre_kernel(got_ref, weight_ref, out_hbm, band_ref, out_ref, sems):
    width = LEV_OWN * BAND
    band_ref[1] = jnp.zeros_like(band_ref[1])
    for i in range(NL):
        part = (got_ref[i, 0] + got_ref[i, 1]) + (got_ref[i, 2] + got_ref[i, 3])
        bands = jnp.concatenate([part[:, g * width : (g + 1) * width] for g in range(4)], axis=0)
        h, at = divmod(i * BAND, 128)
        first = min(BAND, 128 - at)
        for k in range(LEV_OWN):
            row = slice(k * 16, k * 16 + 16)
            piece = bands[:, k * BAND : (k + 1) * BAND]
            band_ref[h, row, at : at + first] = piece[:, :first]
            if first < BAND:
                band_ref[h + 1, row, 0 : BAND - first] = piece[:, first:]
    dims = (((1,), (1,)), ((), ()))
    saves = []
    for s in range(SLOTS_OWN):
        rows = [band_ref[h, pl.ds(s, 2 * LEV_OWN, stride=8), :] for h in range(2)]
        hi, lo = split2(jnp.concatenate(rows, axis=1))
        parts = jnp.concatenate((hi, hi), axis=1)
        out = lax.dot_general(parts, weight_ref[s], dims, preferred_element_type=F32)
        out = out + lax.dot_general(lo, weight_ref[s, :, 0:256], dims, preferred_element_type=F32)
        out_ref[:, s, :, :] = out.reshape(LEV_OWN, 2, MMAX)
        if s % 4 == 3:
            part = pl.ds(s - 3, 4)
            save = pltpu.make_async_copy(out_ref.at[:, part], out_hbm.at[:, part], sems.at[s // 4])
            save.start()
            saves.append(save)
    for save in saves:
        save.wait()


def geometry():
    theta = (np.arange(NLAT) + 0.5) * (math.pi / NLAT)
    sine = np.sin(theta)
    rows = np.zeros((4, 256))
    rows[0, :NLAT] = np.cos(theta)
    rows[1, :NLAT] = np.log(sine)
    rows[2, :NLAT] = sine / math.sqrt(NLAT)
    for m in range(MMAX):
        logs = math.lgamma(m + 1.5) - math.lgamma(1.5) - math.lgamma(m + 1.0)
        rows[3, m] = 0.5 * logs - 0.5 * math.log(2.0)
    return rows.astype(np.float32)


def call(kernel, out, specs, scratch=(), out_specs=None):
    return pl.pallas_call(
        kernel,
        out_shape=out,
        in_specs=specs,
        out_specs=out_specs or jax.tree.map(lambda _: VMEM, out),
        scratch_shapes=list(scratch),
        compiler_params=params(),
    )


def stay(x):
    return pltpu.with_memory_space_constraint(x, pltpu.HBM)


def shards(state, forcing, crm_moisture, cloud_order, wave_table):
    shape = jax.ShapeDtypeStruct
    state = state.transpose(0, 2, 3, 1, 4).reshape(ROWS, 1, LONS)
    forcing = forcing.transpose(0, 2, 3, 1, 4).reshape(ROWS, 1, LONS)
    moist = crm_moisture.transpose(0, 2, 3, 4, 1, 5).reshape(LEVELS, NCRM, RUNS)
    order = cloud_order.reshape(1, COLS)
    waves = wave_table.reshape(1, MMAX)
    outgoing, cols = call(
        pack_kernel,
        (shape((TARGETS, 8, 128), F32), shape((2 * LEVELS, COLS), F32)),
        [HBM] * 3,
        [
            pltpu.VMEM((ROWS, 1, LONS), F32),
            pltpu.VMEM((ROWS, 1, LONS), F32),
            pltpu.VMEM((1, COLS), jnp.int32),
            pltpu.VMEM((COLS, COLS), BF16),
            pltpu.VMEM((TARGETS, 8, 128), F32),
            pltpu.SemaphoreType.DMA((9,)),
        ],
        (HBM, VMEM),
    )(*(stay(x) for x in (state, forcing, order)))
    outgoing, waves = lax.optimization_barrier((outgoing, waves))
    arrived = lax.all_to_all(outgoing, ("sec", "lat"), split_axis=0, concat_axis=0, tiled=True)
    trig, weights, water, tail, column = call(
        table_kernel,
        (
            shape((2 * MMAX, 384), BF16),
            shape((SLOTS_OWN, MMAX, 512), BF16),
            shape((LEVELS, 2, 4, 8, 128), F32),
            shape((LEVELS // 4, 4, 8, 128), F32),
            shape((COLS, 128), F32),
        ),
        [HBM] * 4,
        [
            pltpu.VMEM((1, MMAX), jnp.int32),
            pltpu.VMEM((4, 256), F32),
            pltpu.VMEM((1, COLS), jnp.int32),
            pltpu.VMEM((LEVELS, NCRM, RUNS), BF16),
            pltpu.VMEM((2, MMAX * SLOTS_OWN, 128), F32),
            pltpu.VMEM((MMAX, 128), F32),
            pltpu.VMEM((LEVELS, 3, NCRM, 128), F32),
            pltpu.SemaphoreType.DMA((4,)),
        ],
    )(*(stay(x) for x in (waves, jnp.asarray(geometry()), order, moist)))
    arrived, trig = lax.optimization_barrier((arrived, trig))
    rain = call(
        cloud_kernel,
        shape((TARGETS, 4, 128), F32),
        [VMEM] * 3,
        [
            pltpu.VMEM((3, 32, 128), F32),
            pltpu.VMEM((3, 64, 128), F32),
            pltpu.VMEM((2, 32, 128), F32),
            pltpu.VMEM((2, 32, 128), F32),
            pltpu.VMEM((2, 32, 128), F32),
            pltpu.VMEM((3, 32, 128), F32),
            pltpu.VMEM((5, 8, 128), F32),
        ],
    )(arrived, water, tail)
    returned = lax.all_to_all(rain, ("sec", "lat"), split_axis=0, concat_axis=0, tiled=True)
    updated, fourier = call(
        update_kernel,
        (shape((ROWS, 1, LONS), F32), shape((NL, NC, 4, 384), F32)),
        [VMEM] * 4,
        [
            pltpu.VMEM((32, COLS), F32),
            pltpu.VMEM((ROWS, 128), F32),
            pltpu.VMEM((ROWS, 1, LONS), F32),
            pltpu.VMEM((COLS, COLS), BF16),
            pltpu.SemaphoreType.DMA,
        ],
        (HBM, VMEM),
    )(returned, column, cols, trig)
    bands = lax.all_to_all(
        fourier.reshape(NL * NC, 4, 384), ("lat", "col"), split_axis=0, concat_axis=0, tiled=True
    )
    spectral = call(
        legendre_kernel,
        shape((LEV_OWN, SLOTS_OWN, 2, MMAX), F32),
        [VMEM] * 2,
        [
            pltpu.VMEM((2, LEV_OWN * 16, 128), F32),
            pltpu.VMEM((LEV_OWN, SLOTS_OWN, 2, MMAX), F32),
            pltpu.SemaphoreType.DMA((2,)),
        ],
        HBM,
    )(bands.reshape(NL, NC, 4, 384), weights)
    new_state = updated.reshape(1, LEVELS, BAND, 1, LONS).transpose(0, 3, 1, 2, 4)
    return new_state, spectral[None, None]


def solution(mesh):
    placed = (
        P(None, "sec", None, "lat", "col"),
        P(None, "sec", None, "lat", "col"),
        P(None, None, None, ("sec", "lat"), "col", None),
        P("col", "lat", None),
        P(),
    )
    return jax.shard_map(
        shards,
        mesh=mesh,
        in_specs=placed,
        out_specs=(P(None, "sec", None, "lat", "col"), P("sec", None, "col", "lat", None, None)),
        check_vma=False,
    )
```

```python
import math

import jax
import jax.numpy as jnp
import numpy as np
from jax import lax
from jax.experimental import pallas as pl
from jax.experimental.pallas import tpu as pltpu
from jax.sharding import PartitionSpec as P

NLON = 384
NLAT = 192
MMAX = 128
NSUB = 4
NCRM = 32
LEVELS = 28
BAND = 12
LONS = 96
COLS = BAND * LONS
WIDE = BAND * 128
ROWS = LEVELS * BAND
TARGETS = 64
PER = 18
NL = 16
NS = 4
NC = 4
RUNS = NL * PER
HALF = 4 * PER
TAIL = RUNS - 256
LEV_OWN = LEVELS // NC
SLOTS_OWN = MMAX // NL

F32 = jnp.float32
BF16 = jnp.bfloat16
VMEM = pl.BlockSpec(memory_space=pltpu.VMEM)
HBM = pl.BlockSpec(memory_space=pltpu.HBM)


def split2(x):
    hi = x.astype(BF16)
    lo = (x - hi.astype(F32)).astype(BF16)
    return hi, lo


def params(mib=16):
    return pltpu.CompilerParams(vmem_limit_bytes=mib << 20)


def lanes_of(shape):
    return lax.broadcasted_iota(jnp.int32, shape, 1)


def widened(order):
    order = order.astype(F32)
    return order + 32.0 * jnp.floor((order + 0.5) * (1.0 / LONS))


def fill_one_hot(order_ref, hot_ref):
    order = widened(order_ref[...]).astype(jnp.int32)
    step = 128
    for c in range(0, WIDE, step):
        ids = lax.broadcasted_iota(jnp.int32, (step, COLS), 0) + c
        hot_ref[c : c + step, :] = jnp.where(ids == order, 1.0, 0.0).astype(BF16)


def trig_rows(orders, trig_ref):
    first = (lax.axis_index("col") * LONS).astype(F32)
    y = lax.broadcasted_iota(jnp.int32, (MMAX, 128), 1).astype(F32) + first
    product = y * orders
    phase = product - NLON * jnp.floor((product + 0.5) * (1.0 / NLON))
    turn = jnp.floor((phase + 48.5) * (1.0 / 96.0))
    x = (phase - 96.0 * turn) * (2.0 * math.pi / NLON)
    z = x * x
    sin = x * (1.0 + z * (-1.0 / 6 + z * (1.0 / 120 + z * (-1.0 / 5040 + z * (1.0 / 362880)))))
    cos = 1.0 + z * (-0.5 + z * (1.0 / 24 + z * (-1.0 / 720 + z * (1.0 / 40320))))
    odd = (turn == 1.0) | (turn == 3.0)
    cos_out = jnp.where(odd, sin, cos)
    sin_out = jnp.where(odd, cos, sin)
    cos_out = jnp.where((turn == 1.0) | (turn == 2.0), -cos_out, cos_out)
    sin_out = jnp.where((turn == 2.0) | (turn == 3.0), -sin_out, sin_out)
    norm = 1.0 / math.sqrt(NLON)
    halves = [
        part.reshape(NL, 2, 4, 128)[:, h].reshape(NL * 4, 128)
        for part in (cos_out * norm, sin_out * norm)
        for h in range(2)
    ]
    hi, lo = split2(jnp.concatenate(halves, axis=0))
    trig_ref[:, 0:128] = hi
    trig_ref[:, 128:256] = hi
    trig_ref[:, 256:384] = lo


def legendre_rows(order, geom_ref, poly_ref, weight_ref):
    lane = lanes_of((SLOTS_OWN, 128)).astype(F32)
    head = jnp.sum(jnp.where(lane == order, geom_ref[3:4, 0:128], 0.0), axis=1, keepdims=True)
    degree = lax.broadcasted_iota(jnp.int32, (SLOTS_OWN, 128), 1).astype(F32)
    active = degree > order
    numer = jnp.where(active, 4.0 * degree * degree - 1.0, 0.0)
    denom = jnp.where(active, degree * degree - order * order, 1.0)
    grow = jnp.sqrt(numer / denom)
    lower = degree - 1.0
    retreat = jnp.sqrt(
        jnp.maximum(lower * lower - order * order, 0.0) / (4.0 * lower * lower - 1.0)
    )
    retreat = grow * retreat
    begin = jnp.where(degree == order, 1.0, 0.0)
    diagonal = jnp.exp(head + order[:, 0:1] * geom_ref[1:2, :]) * geom_ref[2:3, :]
    cosine = jnp.broadcast_to(geom_ref[0:1, :], (SLOTS_OWN, 256))
    previous = jnp.zeros((SLOTS_OWN, 256), F32)
    current = previous
    for n in range(MMAX):
        fresh = (grow[:, n : n + 1] * cosine) * current + (
            begin[:, n : n + 1] * diagonal - retreat[:, n : n + 1] * previous
        )
        poly_ref[0, n * 8 : n * 8 + 8, :] = fresh[:, :128]
        poly_ref[1, n * 8 : n * 8 + 8, :] = fresh[:, 128:]
        previous, current = current, fresh
    for s in range(SLOTS_OWN):
        for h in range(2):
            hi, lo = split2(poly_ref[h, pl.ds(s, MMAX, stride=8), :])
            size = min(128, NLAT - h * 128)
            for part, base in ((hi, 0), (lo, NLAT)):
                at = base + h * 128
                weight_ref[s, :, at : at + size] = part[:, :size]


def arrange_moisture(moist_ref, level_ref, water_ref, tail_ref):
    lane = lanes_of((8, 128))
    blank = jnp.zeros((NCRM, 384 - RUNS), F32)
    for k in range(LEVELS):
        level = jnp.concatenate((moist_ref[k].astype(F32), blank), axis=1)
        for v in range(3):
            level_ref[k, v] = level[:, v * 128 : v * 128 + 128]
    for k in range(LEVELS):
        for v in range(2):
            for n in range(4):
                water_ref[k, v, n] = level_ref[k, v, pl.ds(n, 8, stride=4), :]
    for g in range(LEVELS // 4):
        for n in range(4):
            tile = level_ref[4 * g, 2, pl.ds(n, 8, stride=4), :]
            for kk in range(1, 4):
                more = pltpu.roll(level_ref[4 * g + kk, 2, pl.ds(n, 8, stride=4), :], kk * TAIL, 1)
                tile = jnp.where(lane >= kk * TAIL, more, tile)
            tail_ref[g, n] = tile


def table_kernel(
    wave_hbm,
    geom_hbm,
    order_hbm,
    moist_hbm,
    trig_ref,
    weight_ref,
    water_ref,
    tail_ref,
    column_ref,
    wave_ref,
    geom_ref,
    order_ref,
    moist_ref,
    poly_ref,
    orders_ref,
    level_ref,
    sems,
):
    pairs = (
        (wave_hbm, wave_ref),
        (geom_hbm, geom_ref),
        (order_hbm, order_ref),
        (moist_hbm, moist_ref),
    )
    loads = [pltpu.make_async_copy(src, dst, sems.at[n]) for n, (src, dst) in enumerate(pairs)]
    for load in loads:
        load.start()
    for load in loads[:3]:
        load.wait()
    orders = jnp.broadcast_to(wave_ref[...].astype(F32), (MMAX, MMAX)).T
    orders_ref[...] = orders
    trig_rows(orders, trig_ref)
    first = pl.multiple_of(lax.axis_index("lat") * SLOTS_OWN, SLOTS_OWN)
    legendre_rows(orders_ref[pl.ds(first, SLOTS_OWN), :], geom_ref, poly_ref, weight_ref)
    order = widened(order_ref[...])
    for v in range(COLS // 128):
        at = slice(v * 128, v * 128 + 128)
        column_ref[at, :] = jnp.broadcast_to(order[:, at], (128, 128)).T
    loads[3].wait()
    arrange_moisture(moist_ref, level_ref, water_ref, tail_ref)


def pack_kernel(
    state_hbm,
    force_hbm,
    order_hbm,
    out_hbm,
    cols_ref,
    state_ref,
    force_ref,
    order_ref,
    hot_ref,
    out_ref,
    sems,
):
    pairs = ((order_hbm, order_ref), (state_hbm, state_ref), (force_hbm, force_ref))
    loads = [pltpu.make_async_copy(src, dst, sems.at[n]) for n, (src, dst) in enumerate(pairs)]
    for load in loads:
        load.start()
    loads[0].wait()
    fill_one_hot(order_ref, hot_ref)
    loads[1].wait()
    loads[2].wait()
    blank = jnp.zeros((LEVELS, 128 - LONS), F32)
    for ref, base in ((state_ref, 0), (force_ref, LEVELS)):
        rows = ref[...].reshape(LEVELS, BAND, LONS)
        for b in range(BAND):
            piece = jnp.concatenate((rows[:, b, :], blank), axis=1)
            cols_ref[base : base + LEVELS, b * 128 : (b + 1) * 128] = piece
    hi, lo = split2(cols_ref[...])
    both = jnp.concatenate((hi, lo), axis=0)
    got = jnp.dot(both, hot_ref[...], preferred_element_type=F32)
    got = got[: 2 * LEVELS] + got[2 * LEVELS :]
    lane = lanes_of((8, 128))
    groups = 2 * LEVELS // 8
    for t in range(TARGETS):
        v, off = divmod(t * PER, 128)
        tile = None
        for q in range(groups):
            src = got[q * 8 : q * 8 + 8, v * 128 : v * 128 + 128]
            if off + PER > 128:
                nxt = got[q * 8 : q * 8 + 8, v * 128 + 128 : v * 128 + 256]
                src = jnp.where(lane < off, nxt, src)
            shift = (q * PER - off) % 128
            if shift:
                src = pltpu.roll(src, shift, 1)
            tile = src if tile is None else jnp.where(lane >= q * PER, src, tile)
        out_ref[t] = tile
    save = pltpu.make_async_copy(out_ref, out_hbm, sems.at[3])
    save.start()
    save.wait()


def gather_lanes(tile_of, q_list, first, count, width, store):
    lane = lanes_of((8, 128))
    for q in q_list:
        for v in range(pl.cdiv(width, 128)):
            acc = None
            for i in range(count):
                start = i * PER - v * 128
                if start >= 128 or start + PER <= 0:
                    continue
                src = tile_of(first + i)
                shift = (i * PER - q * PER) % 128
                if shift:
                    src = pltpu.roll(src, shift, 1)
                acc = src if acc is None else jnp.where(lane >= start, src, acc)
            store(q, v, acc)


def coefficients(wind):
    courant = 0.4 * jnp.tanh(wind)
    mixing = 0.2 + 0.5 * jnp.abs(courant)
    return mixing - 0.5 * courant, mixing + 0.5 * courant


def cloud_tile(start, push, ahead, behind, water):
    keep = 1.0 - (ahead + behind)
    gap = [start + w for w in water]
    wet = [jnp.maximum(g, 0.0) for g in gap]
    total = (wet[0] + wet[1]) + (wet[2] + wet[3])
    for _ in range(NSUB - 1):
        up = gap[1:] + [pltpu.roll(gap[0], 7, 0)]
        down = [pltpu.roll(gap[3], 1, 0)] + gap[:3]
        gap = [
            ((keep * gap[n] - wet[n]) + push) + (ahead * up[n] + behind * down[n]) for n in range(4)
        ]
        wet = [jnp.maximum(g, 0.0) for g in gap]
        total = total + ((wet[0] + wet[1]) + (wet[2] + wet[3]))
    return jnp.sum(total, axis=0, keepdims=True) * (0.5 / NCRM)


def cloud_kernel(
    got_ref,
    water_ref,
    tail_ref,
    out_ref,
    wind_ref,
    diff_ref,
    push_ref,
    left_ref,
    right_ref,
    rain_ref,
    last_ref,
):
    def store_wind(q, v, x):
        wind_ref[v, q * 8 : q * 8 + 8, :] = x

    def store_diff(q, v, x):
        diff_ref[v, q * 8 : q * 8 + 8, :] = x

    gather_lanes(lambda i: got_ref[i], range(4), 0, NL, RUNS, store_wind)
    cache = {}

    def diff(i):
        if i not in cache:
            cache[i] = got_ref[3 * NL + i] - got_ref[2 * NL + i]
        return cache[i]

    gather_lanes(diff, range(7), 0, NL, RUNS, store_diff)
    lane = lanes_of((8, 128))
    groups = LEVELS // 4

    def tails(ref, base):
        tile = ref[2, pl.ds(base, 8, stride=4), :]
        for kk in range(1, 4):
            more = pltpu.roll(ref[2, pl.ds(base + kk, 8, stride=4), :], kk * TAIL, 1)
            tile = jnp.where(lane >= kk * TAIL, more, tile)
        return tile

    wind_tail = tails(wind_ref, 0)
    diff_tail = tails(diff_ref, 0)
    push_tail = tails(diff_ref, LEVELS) * (1.0 / NSUB)
    for v in range(2):
        left_ref[v], right_ref[v] = coefficients(wind_ref[v])
        push_ref[v] = diff_ref[v, LEVELS : LEVELS + 32, :] * (1.0 / NSUB)
    last_ref[4] = jnp.zeros_like(diff_tail)
    last_ref[0] = diff_tail
    last_ref[1] = push_tail
    last_ref[2], last_ref[3] = coefficients(wind_tail)
    rain_ref[...] = jnp.zeros_like(rain_ref)

    def level(g, carry):
        for kk in range(4):
            k = 4 * g + kk
            for v in range(2):

                def row(ref):
                    return jnp.broadcast_to(ref[v, pl.ds(k, 1), :], (8, 128))

                rain_ref[v, pl.ds(k, 1), :] = cloud_tile(
                    row(diff_ref),
                    row(push_ref),
                    row(left_ref),
                    row(right_ref),
                    [water_ref[k, v, n] for n in range(4)],
                )
        rows = [jnp.broadcast_to(last_ref[c, pl.ds(g, 1), :], (8, 128)) for c in range(4)]
        last_ref[4, pl.ds(g, 1), :] = cloud_tile(*rows, [tail_ref[g, n] for n in range(4)])
        return carry

    lax.fori_loop(0, groups, level, 0)
    rain_tail = last_ref[4]
    for kk in range(4):
        piece = rain_tail if kk == 0 else pltpu.roll(rain_tail, 128 - kk * TAIL, 1)
        rain_ref[2, pl.ds(kk, 8, stride=4), :] = piece
    for i in range(NL):
        v, off = divmod(i * PER, 128)
        tile = None
        for q in range(4):
            src = rain_ref[v, q * 8 : q * 8 + 8, :]
            if off + PER > 128:
                nxt = rain_ref[v + 1, q * 8 : q * 8 + 8, :]
                src = jnp.where(lane < off, nxt, src)
            shift = (q * PER - off) % 128
            if shift:
                src = pltpu.roll(src, shift, 1)
            tile = src if tile is None else jnp.where(lane >= q * PER, src, tile)
        low = tile[0:4]
        high = pltpu.roll(tile, HALF, 1)[4:8]
        tile = jnp.where(lane[0:4] < HALF, low, high)
        for s in range(NS):
            out_ref[s * NL + i] = tile


def update_kernel(
    got_ref,
    column_ref,
    cols_ref,
    trig_ref,
    out_ref,
    four_ref,
    slots_ref,
    rows_ref,
    hot_ref,
):
    lane = lanes_of((128, 128)).astype(F32)
    for v in range(COLS // 128):
        rows = slice(v * 128, v * 128 + 128)
        column = column_ref[rows, :]
        for c in range(WIDE // 128):
            hot = jnp.where(lane + float(c * 128) == column, 1.0, 0.0)
            hot_ref[rows, c * 128 : c * 128 + 128] = hot.astype(BF16)

    def store(q, v, x):
        slots_ref[q * 8 : q * 8 + 8, v * 128 : v * 128 + 128] = x

    cache = {}

    def tile_of(t):
        if t not in cache:
            tile = got_ref[t]
            cache[t] = jnp.concatenate((tile, pltpu.roll(tile, 128 - HALF, 1)), axis=0)
        return cache[t]

    gather_lanes(tile_of, range(4), 0, TARGETS, COLS, store)
    hi, lo = split2(slots_ref[...])
    both = jnp.concatenate((hi, lo), axis=0)
    back = jnp.dot(both, hot_ref[...], preferred_element_type=F32)
    rain = back[:LEVELS] + back[32 : 32 + LEVELS]
    sec = lax.axis_index("sec")
    add = jnp.where(sec == 2, 1.0, jnp.where(sec == 3, -1.0, 0.0)).astype(F32)
    scale = jnp.where(sec < 2, -1.0 / NSUB, 0.0).astype(F32)
    now = cols_ref[0:LEVELS]
    now = now + (cols_ref[LEVELS : 2 * LEVELS] + rain * (add + scale * now))
    for b in range(BAND):
        rows_ref[pl.ds(b, LEVELS, stride=BAND), :] = now[:, b * 128 : (b + 1) * 128]
    rows = rows_ref[...]
    out_ref[...] = rows[:, :LONS].reshape(ROWS, 1, LONS)
    hi, lo = split2(rows)
    dims = (((1,), (1,)), ((), ()))
    parts = jnp.concatenate((hi, lo, hi), axis=1)
    out = lax.dot_general(trig_ref[...], parts, dims, preferred_element_type=F32)
    width = LEV_OWN * BAND
    blank = jnp.zeros((NL * 4, 384 - 4 * width), F32)
    for j in range(NC):
        pieces = [out[g * 64 : g * 64 + 64, j * width : (j + 1) * width] for g in range(4)]
        four_ref[:, j] = jnp.concatenate(pieces + [blank], axis=1).reshape(NL, 4, 384)


def legendre_kernel(
    got_ref, weight_ref, state_ref, out_hbm, state_hbm, band_ref, out_ref, sems
):
    saves = [pltpu.make_async_copy(state_ref, state_hbm, sems.at[2])]
    saves[0].start()
    width = LEV_OWN * BAND
    band_ref[1] = jnp.zeros_like(band_ref[1])
    for i in range(NL):
        part = (got_ref[i, 0] + got_ref[i, 1]) + (got_ref[i, 2] + got_ref[i, 3])
        bands = jnp.concatenate([part[:, g * width : (g + 1) * width] for g in range(4)], axis=0)
        h, at = divmod(i * BAND, 128)
        first = min(BAND, 128 - at)
        for k in range(LEV_OWN):
            row = slice(k * 16, k * 16 + 16)
            piece = bands[:, k * BAND : (k + 1) * BAND]
            band_ref[h, row, at : at + first] = piece[:, :first]
            if first < BAND:
                band_ref[h + 1, row, 0 : BAND - first] = piece[:, first:]
    dims = (((1,), (1,)), ((), ()))
    for s in range(SLOTS_OWN):
        rows = [band_ref[h, pl.ds(s, 2 * LEV_OWN, stride=8), :] for h in range(2)]
        hi, lo = split2(jnp.concatenate(rows, axis=1)[:, :NLAT])
        parts = jnp.concatenate((hi, hi), axis=1)
        out = lax.dot_general(parts, weight_ref[s], dims, preferred_element_type=F32)
        out = out + lax.dot_general(lo, weight_ref[s, :, 0:NLAT], dims, preferred_element_type=F32)
        out_ref[:, s, :, :] = out.reshape(LEV_OWN, 2, MMAX)
        if s % 4 == 3:
            part = pl.ds(s - 3, 4)
            save = pltpu.make_async_copy(out_ref.at[:, part], out_hbm.at[:, part], sems.at[s // 4])
            save.start()
            saves.append(save)
    for save in saves:
        save.wait()


def geometry():
    theta = (np.arange(NLAT) + 0.5) * (math.pi / NLAT)
    sine = np.sin(theta)
    rows = np.zeros((4, 256))
    rows[0, :NLAT] = np.cos(theta)
    rows[1, :NLAT] = np.log(sine)
    rows[2, :NLAT] = sine / math.sqrt(NLAT)
    for m in range(MMAX):
        logs = math.lgamma(m + 1.5) - math.lgamma(1.5) - math.lgamma(m + 1.0)
        rows[3, m] = 0.5 * logs - 0.5 * math.log(2.0)
    return rows.astype(np.float32)


def call(kernel, out, specs, scratch=(), out_specs=None):
    return pl.pallas_call(
        kernel,
        out_shape=out,
        in_specs=specs,
        out_specs=out_specs or jax.tree.map(lambda _: VMEM, out),
        scratch_shapes=list(scratch),
        compiler_params=params(),
    )


def stay(x):
    return pltpu.with_memory_space_constraint(x, pltpu.HBM)


def shards(state, forcing, crm_moisture, cloud_order, wave_table):
    shape = jax.ShapeDtypeStruct
    state = state.transpose(0, 2, 3, 1, 4).reshape(ROWS, 1, LONS)
    forcing = forcing.transpose(0, 2, 3, 1, 4).reshape(ROWS, 1, LONS)
    moist = crm_moisture.transpose(0, 2, 3, 4, 1, 5).reshape(LEVELS, NCRM, RUNS)
    order = cloud_order.reshape(1, COLS)
    waves = wave_table.reshape(1, MMAX)
    outgoing, cols = call(
        pack_kernel,
        (shape((TARGETS, 8, 128), F32), shape((2 * LEVELS, WIDE), F32)),
        [HBM] * 3,
        [
            pltpu.VMEM((ROWS, 1, LONS), F32),
            pltpu.VMEM((ROWS, 1, LONS), F32),
            pltpu.VMEM((1, COLS), jnp.int32),
            pltpu.VMEM((WIDE, COLS), BF16),
            pltpu.VMEM((TARGETS, 8, 128), F32),
            pltpu.SemaphoreType.DMA((4,)),
        ],
        (HBM, VMEM),
    )(*(stay(x) for x in (state, forcing, order)))
    outgoing, waves = lax.optimization_barrier((outgoing, waves))
    arrived = lax.all_to_all(outgoing, ("sec", "lat"), split_axis=0, concat_axis=0, tiled=True)
    trig, weights, water, tail, column = call(
        table_kernel,
        (
            shape((2 * MMAX, 384), BF16),
            shape((SLOTS_OWN, MMAX, 2 * NLAT), BF16),
            shape((LEVELS, 2, 4, 8, 128), F32),
            shape((LEVELS // 4, 4, 8, 128), F32),
            shape((COLS, 128), F32),
        ),
        [HBM] * 4,
        [
            pltpu.VMEM((1, MMAX), jnp.int32),
            pltpu.VMEM((4, 256), F32),
            pltpu.VMEM((1, COLS), jnp.int32),
            pltpu.VMEM((LEVELS, NCRM, RUNS), BF16),
            pltpu.VMEM((2, MMAX * SLOTS_OWN, 128), F32),
            pltpu.VMEM((MMAX, 128), F32),
            pltpu.VMEM((LEVELS, 3, NCRM, 128), F32),
            pltpu.SemaphoreType.DMA((4,)),
        ],
    )(*(stay(x) for x in (waves, jnp.asarray(geometry()), order, moist)))
    arrived, trig = lax.optimization_barrier((arrived, trig))
    rain = call(
        cloud_kernel,
        shape((TARGETS, 4, 128), F32),
        [VMEM] * 3,
        [
            pltpu.VMEM((3, 32, 128), F32),
            pltpu.VMEM((3, 64, 128), F32),
            pltpu.VMEM((2, 32, 128), F32),
            pltpu.VMEM((2, 32, 128), F32),
            pltpu.VMEM((2, 32, 128), F32),
            pltpu.VMEM((3, 32, 128), F32),
            pltpu.VMEM((5, 8, 128), F32),
        ],
    )(arrived, water, tail)
    returned = lax.all_to_all(rain, ("sec", "lat"), split_axis=0, concat_axis=0, tiled=True)
    updated, fourier = call(
        update_kernel,
        (shape((ROWS, 1, LONS), F32), shape((NL, NC, 4, 384), F32)),
        [VMEM] * 4,
        [
            pltpu.VMEM((32, COLS), F32),
            pltpu.VMEM((ROWS, 128), F32),
            pltpu.VMEM((COLS, WIDE), BF16),
        ],
    )(returned, column, cols, trig)
    bands = lax.all_to_all(
        fourier.reshape(NL * NC, 4, 384), ("lat", "col"), split_axis=0, concat_axis=0, tiled=True
    )
    spectral, updated = call(
        legendre_kernel,
        (shape((LEV_OWN, SLOTS_OWN, 2, MMAX), F32), shape((ROWS, 1, LONS), F32)),
        [VMEM] * 3,
        [
            pltpu.VMEM((2, LEV_OWN * 16, 128), F32),
            pltpu.VMEM((LEV_OWN, SLOTS_OWN, 2, MMAX), F32),
            pltpu.SemaphoreType.DMA((3,)),
        ],
        (HBM, HBM),
    )(bands.reshape(NL, NC, 4, 384), weights, updated)
    new_state = updated.reshape(1, LEVELS, BAND, 1, LONS).transpose(0, 3, 1, 2, 4)
    return new_state, spectral[None, None]


def solution(mesh):
    placed = (
        P(None, "sec", None, "lat", "col"),
        P(None, "sec", None, "lat", "col"),
        P(None, None, None, ("sec", "lat"), "col", None),
        P("col", "lat", None),
        P(),
    )
    return jax.shard_map(
        shards,
        mesh=mesh,
        in_specs=placed,
        out_specs=(P(None, "sec", None, "lat", "col"), P("sec", None, "col", "lat", None, None)),
        check_vma=False,
    )
```

```python
import math

import jax
import jax.numpy as jnp
import numpy as np
from jax import lax
from jax.experimental import pallas as pl
from jax.experimental.pallas import tpu as pltpu
from jax.sharding import PartitionSpec as P

NLON = 384
NLAT = 192
MMAX = 128
NSUB = 4
NCRM = 32
LEVELS = 28
BAND = 12
LONS = 96
COLS = BAND * LONS
ROWS = LEVELS * BAND
TARGETS = 64
PER = 18
NL = 16
NS = 4
NC = 4
RUNS = NL * PER
HALF = 4 * PER
TAIL = RUNS - 256
LEV_OWN = LEVELS // NC
SLOTS_OWN = MMAX // NL

F32 = jnp.float32
BF16 = jnp.bfloat16
VMEM = pl.BlockSpec(memory_space=pltpu.VMEM)
HBM = pl.BlockSpec(memory_space=pltpu.HBM)


def split2(x):
    hi = x.astype(BF16)
    lo = (x - hi.astype(F32)).astype(BF16)
    return hi, lo


def params(mib=16):
    return pltpu.CompilerParams(vmem_limit_bytes=mib << 20)


def lanes_of(shape):
    return lax.broadcasted_iota(jnp.int32, shape, 1)


def fill_one_hot(order_ref, hot_ref):
    order = order_ref[...]
    step = 96
    for c in range(0, COLS, step):
        ids = lax.broadcasted_iota(jnp.int32, (step, COLS), 0) + c
        hot_ref[c : c + step, :] = jnp.where(ids == order, 1.0, 0.0).astype(BF16)


def trig_rows(orders, trig_ref):
    first = (lax.axis_index("col") * LONS).astype(F32)
    y = lax.broadcasted_iota(jnp.int32, (MMAX, 128), 1).astype(F32) + first
    product = y * orders
    phase = product - NLON * jnp.floor((product + 0.5) * (1.0 / NLON))
    turn = jnp.floor((phase + 48.5) * (1.0 / 96.0))
    x = (phase - 96.0 * turn) * (2.0 * math.pi / NLON)
    z = x * x
    sin = x * (1.0 + z * (-1.0 / 6 + z * (1.0 / 120 + z * (-1.0 / 5040 + z * (1.0 / 362880)))))
    cos = 1.0 + z * (-0.5 + z * (1.0 / 24 + z * (-1.0 / 720 + z * (1.0 / 40320))))
    odd = (turn == 1.0) | (turn == 3.0)
    cos_out = jnp.where(odd, sin, cos)
    sin_out = jnp.where(odd, cos, sin)
    cos_out = jnp.where((turn == 1.0) | (turn == 2.0), -cos_out, cos_out)
    sin_out = jnp.where((turn == 2.0) | (turn == 3.0), -sin_out, sin_out)
    norm = 1.0 / math.sqrt(NLON)
    halves = [
        part.reshape(NL, 2, 4, 128)[:, h].reshape(NL * 4, 128)
        for part in (cos_out * norm, sin_out * norm)
        for h in range(2)
    ]
    hi, lo = split2(jnp.concatenate(halves, axis=0))
    trig_ref[:, 0:128] = hi
    trig_ref[:, 128:256] = hi
    trig_ref[:, 256:384] = lo


def legendre_rows(order, geom_ref, poly_ref, weight_ref):
    lane = lanes_of((SLOTS_OWN, 128)).astype(F32)
    head = jnp.sum(jnp.where(lane == order, geom_ref[3:4, 0:128], 0.0), axis=1, keepdims=True)
    degree = lax.broadcasted_iota(jnp.int32, (SLOTS_OWN, 128), 1).astype(F32)
    active = degree > order
    numer = jnp.where(active, 4.0 * degree * degree - 1.0, 0.0)
    denom = jnp.where(active, degree * degree - order * order, 1.0)
    grow = jnp.sqrt(numer / denom)
    lower = degree - 1.0
    retreat = jnp.sqrt(
        jnp.maximum(lower * lower - order * order, 0.0) / (4.0 * lower * lower - 1.0)
    )
    retreat = grow * retreat
    begin = jnp.where(degree == order, 1.0, 0.0)
    diagonal = jnp.exp(head + order[:, 0:1] * geom_ref[1:2, :]) * geom_ref[2:3, :]
    cosine = jnp.broadcast_to(geom_ref[0:1, :], (SLOTS_OWN, 256))
    previous = jnp.zeros((SLOTS_OWN, 256), F32)
    current = previous
    for n in range(MMAX):
        fresh = (grow[:, n : n + 1] * cosine) * current + (
            begin[:, n : n + 1] * diagonal - retreat[:, n : n + 1] * previous
        )
        poly_ref[0, n * 8 : n * 8 + 8, :] = fresh[:, :128]
        poly_ref[1, n * 8 : n * 8 + 8, :] = fresh[:, 128:]
        previous, current = current, fresh
    for s in range(SLOTS_OWN):
        for h in range(2):
            hi, lo = split2(poly_ref[h, pl.ds(s, MMAX, stride=8), :])
            size = min(128, NLAT - h * 128)
            for part, base in ((hi, 0), (lo, NLAT)):
                at = base + h * 128
                weight_ref[s, :, at : at + size] = part[:, :size]


def arrange_moisture(moist_ref, level_ref, water_ref, tail_ref):
    lane = lanes_of((8, 128))
    blank = jnp.zeros((NCRM, 384 - RUNS), F32)
    for k in range(LEVELS):
        level = jnp.concatenate((moist_ref[k].astype(F32), blank), axis=1)
        for v in range(3):
            level_ref[k, v] = level[:, v * 128 : v * 128 + 128]
    for k in range(LEVELS):
        for v in range(2):
            for n in range(4):
                water_ref[k, v, n] = level_ref[k, v, pl.ds(n, 8, stride=4), :]
    for g in range(LEVELS // 4):
        for n in range(4):
            tile = level_ref[4 * g, 2, pl.ds(n, 8, stride=4), :]
            for kk in range(1, 4):
                more = pltpu.roll(level_ref[4 * g + kk, 2, pl.ds(n, 8, stride=4), :], kk * TAIL, 1)
                tile = jnp.where(lane >= kk * TAIL, more, tile)
            tail_ref[g, n] = tile


def table_kernel(
    wave_hbm,
    geom_hbm,
    order_hbm,
    moist_hbm,
    trig_ref,
    weight_ref,
    water_ref,
    tail_ref,
    column_ref,
    wave_ref,
    geom_ref,
    order_ref,
    moist_ref,
    poly_ref,
    orders_ref,
    level_ref,
    sems,
):
    pairs = (
        (wave_hbm, wave_ref),
        (geom_hbm, geom_ref),
        (order_hbm, order_ref),
        (moist_hbm, moist_ref),
    )
    loads = [pltpu.make_async_copy(src, dst, sems.at[n]) for n, (src, dst) in enumerate(pairs)]
    for load in loads:
        load.start()
    for load in loads[:3]:
        load.wait()
    orders = jnp.broadcast_to(wave_ref[...].astype(F32), (MMAX, MMAX)).T
    orders_ref[...] = orders
    trig_rows(orders, trig_ref)
    first = pl.multiple_of(lax.axis_index("lat") * SLOTS_OWN, SLOTS_OWN)
    legendre_rows(orders_ref[pl.ds(first, SLOTS_OWN), :], geom_ref, poly_ref, weight_ref)
    order = order_ref[...].astype(F32)
    for v in range(COLS // 128):
        at = slice(v * 128, v * 128 + 128)
        column_ref[at, :] = jnp.broadcast_to(order[:, at], (128, 128)).T
    loads[3].wait()
    arrange_moisture(moist_ref, level_ref, water_ref, tail_ref)


def pack_kernel(
    state_hbm,
    force_hbm,
    order_hbm,
    out_hbm,
    cols_ref,
    state_ref,
    force_ref,
    order_ref,
    hot_ref,
    out_ref,
    sems,
):
    pairs = ((order_hbm, order_ref), (state_hbm, state_ref), (force_hbm, force_ref))
    loads = [pltpu.make_async_copy(src, dst, sems.at[n]) for n, (src, dst) in enumerate(pairs)]
    for load in loads:
        load.start()
    loads[0].wait()
    fill_one_hot(order_ref, hot_ref)
    loads[1].wait()
    loads[2].wait()
    for ref, base in ((state_ref, 0), (force_ref, LEVELS)):
        rows = ref[...].reshape(LEVELS, BAND, LONS)
        for b in range(BAND):
            cols_ref[base : base + LEVELS, b * LONS : (b + 1) * LONS] = rows[:, b, :]
    hi, lo = split2(cols_ref[...])
    both = jnp.concatenate((hi, lo), axis=0)
    got = jnp.dot(both, hot_ref[...], preferred_element_type=F32)
    got = got[: 2 * LEVELS] + got[2 * LEVELS :]
    lane = lanes_of((8, 128))
    groups = 2 * LEVELS // 8
    for t in range(TARGETS):
        v, off = divmod(t * PER, 128)
        tile = None
        for q in range(groups):
            src = got[q * 8 : q * 8 + 8, v * 128 : v * 128 + 128]
            if off + PER > 128:
                nxt = got[q * 8 : q * 8 + 8, v * 128 + 128 : v * 128 + 256]
                src = jnp.where(lane < off, nxt, src)
            shift = (q * PER - off) % 128
            if shift:
                src = pltpu.roll(src, shift, 1)
            tile = src if tile is None else jnp.where(lane >= q * PER, src, tile)
        out_ref[t] = tile
    save = pltpu.make_async_copy(out_ref, out_hbm, sems.at[3])
    save.start()
    save.wait()


def gather_lanes(tile_of, q_list, first, count, width, store):
    lane = lanes_of((8, 128))
    for q in q_list:
        for v in range(pl.cdiv(width, 128)):
            acc = None
            for i in range(count):
                start = i * PER - v * 128
                if start >= 128 or start + PER <= 0:
                    continue
                src = tile_of(first + i)
                shift = (i * PER - q * PER) % 128
                if shift:
                    src = pltpu.roll(src, shift, 1)
                acc = src if acc is None else jnp.where(lane >= start, src, acc)
            store(q, v, acc)


def coefficients(wind):
    courant = 0.4 * jnp.tanh(wind)
    mixing = 0.2 + 0.5 * jnp.abs(courant)
    return mixing - 0.5 * courant, mixing + 0.5 * courant


def cloud_tile(start, push, ahead, behind, water):
    keep = 1.0 - (ahead + behind)
    gap = [start + w for w in water]
    wet = [jnp.maximum(g, 0.0) for g in gap]
    total = (wet[0] + wet[1]) + (wet[2] + wet[3])
    for _ in range(NSUB - 1):
        up = gap[1:] + [pltpu.roll(gap[0], 7, 0)]
        down = [pltpu.roll(gap[3], 1, 0)] + gap[:3]
        gap = [
            ((keep * gap[n] - wet[n]) + push) + (ahead * up[n] + behind * down[n]) for n in range(4)
        ]
        wet = [jnp.maximum(g, 0.0) for g in gap]
        total = total + ((wet[0] + wet[1]) + (wet[2] + wet[3]))
    return jnp.sum(total, axis=0, keepdims=True) * (0.5 / NCRM)


def cloud_kernel(
    got_ref,
    water_ref,
    tail_ref,
    out_ref,
    wind_ref,
    diff_ref,
    push_ref,
    left_ref,
    right_ref,
    rain_ref,
    last_ref,
):
    def store_wind(q, v, x):
        wind_ref[v, q * 8 : q * 8 + 8, :] = x

    def store_diff(q, v, x):
        diff_ref[v, q * 8 : q * 8 + 8, :] = x

    gather_lanes(lambda i: got_ref[i], range(4), 0, NL, RUNS, store_wind)
    cache = {}

    def diff(i):
        if i not in cache:
            cache[i] = got_ref[3 * NL + i] - got_ref[2 * NL + i]
        return cache[i]

    gather_lanes(diff, range(7), 0, NL, RUNS, store_diff)
    lane = lanes_of((8, 128))
    groups = LEVELS // 4

    def tails(ref, base):
        tile = ref[2, pl.ds(base, 8, stride=4), :]
        for kk in range(1, 4):
            more = pltpu.roll(ref[2, pl.ds(base + kk, 8, stride=4), :], kk * TAIL, 1)
            tile = jnp.where(lane >= kk * TAIL, more, tile)
        return tile

    wind_tail = tails(wind_ref, 0)
    diff_tail = tails(diff_ref, 0)
    push_tail = tails(diff_ref, LEVELS) * (1.0 / NSUB)
    for v in range(2):
        left_ref[v], right_ref[v] = coefficients(wind_ref[v])
        push_ref[v] = diff_ref[v, LEVELS : LEVELS + 32, :] * (1.0 / NSUB)
    last_ref[4] = jnp.zeros_like(diff_tail)
    last_ref[0] = diff_tail
    last_ref[1] = push_tail
    last_ref[2], last_ref[3] = coefficients(wind_tail)
    rain_ref[...] = jnp.zeros_like(rain_ref)

    def level(g, carry):
        for kk in range(4):
            k = 4 * g + kk
            for v in range(2):

                def row(ref):
                    return jnp.broadcast_to(ref[v, pl.ds(k, 1), :], (8, 128))

                rain_ref[v, pl.ds(k, 1), :] = cloud_tile(
                    row(diff_ref),
                    row(push_ref),
                    row(left_ref),
                    row(right_ref),
                    [water_ref[k, v, n] for n in range(4)],
                )
        rows = [jnp.broadcast_to(last_ref[c, pl.ds(g, 1), :], (8, 128)) for c in range(4)]
        last_ref[4, pl.ds(g, 1), :] = cloud_tile(*rows, [tail_ref[g, n] for n in range(4)])
        return carry

    lax.fori_loop(0, groups, level, 0)
    rain_tail = last_ref[4]
    for kk in range(4):
        piece = rain_tail if kk == 0 else pltpu.roll(rain_tail, 128 - kk * TAIL, 1)
        rain_ref[2, pl.ds(kk, 8, stride=4), :] = piece
    for i in range(NL):
        v, off = divmod(i * PER, 128)
        tile = None
        for q in range(4):
            src = rain_ref[v, q * 8 : q * 8 + 8, :]
            if off + PER > 128:
                nxt = rain_ref[v + 1, q * 8 : q * 8 + 8, :]
                src = jnp.where(lane < off, nxt, src)
            shift = (q * PER - off) % 128
            if shift:
                src = pltpu.roll(src, shift, 1)
            tile = src if tile is None else jnp.where(lane >= q * PER, src, tile)
        low = tile[0:4]
        high = pltpu.roll(tile, HALF, 1)[4:8]
        tile = jnp.where(lane[0:4] < HALF, low, high)
        for s in range(NS):
            out_ref[s * NL + i] = tile


def update_kernel(
    got_ref,
    column_ref,
    cols_ref,
    trig_ref,
    out_ref,
    four_ref,
    slots_ref,
    rows_ref,
    hot_ref,
):
    lane = lanes_of((128, 128)).astype(F32)
    for v in range(COLS // 128):
        rows = slice(v * 128, v * 128 + 128)
        column = column_ref[rows, :]
        for c in range(COLS // 128):
            hot = jnp.where(lane + float(c * 128) == column, 1.0, 0.0)
            hot_ref[rows, c * 128 : c * 128 + 128] = hot.astype(BF16)

    def store(q, v, x):
        slots_ref[q * 8 : q * 8 + 8, v * 128 : v * 128 + 128] = x

    cache = {}

    def tile_of(t):
        if t not in cache:
            tile = got_ref[t]
            cache[t] = jnp.concatenate((tile, pltpu.roll(tile, 128 - HALF, 1)), axis=0)
        return cache[t]

    gather_lanes(tile_of, range(4), 0, TARGETS, COLS, store)
    hi, lo = split2(slots_ref[...])
    both = jnp.concatenate((hi, lo), axis=0)
    back = jnp.dot(both, hot_ref[...], preferred_element_type=F32)
    rain = back[:LEVELS] + back[32 : 32 + LEVELS]
    sec = lax.axis_index("sec")
    add = jnp.where(sec == 2, 1.0, jnp.where(sec == 3, -1.0, 0.0)).astype(F32)
    scale = jnp.where(sec < 2, -1.0 / NSUB, 0.0).astype(F32)
    now = cols_ref[0:LEVELS]
    now = now + (cols_ref[LEVELS : 2 * LEVELS] + rain * (add + scale * now))
    blank = jnp.zeros((LEVELS, 128 - LONS), F32)
    for b in range(BAND):
        piece = jnp.concatenate((now[:, b * LONS : (b + 1) * LONS], blank), axis=1)
        rows_ref[pl.ds(b, LEVELS, stride=BAND), :] = piece
    rows = rows_ref[...]
    out_ref[...] = rows[:, :LONS].reshape(ROWS, 1, LONS)
    hi, lo = split2(rows)
    dims = (((1,), (1,)), ((), ()))
    parts = jnp.concatenate((hi, lo, hi), axis=1)
    out = lax.dot_general(trig_ref[...], parts, dims, preferred_element_type=F32)
    width = LEV_OWN * BAND
    blank = jnp.zeros((NL * 4, 384 - 4 * width), F32)
    for j in range(NC):
        pieces = [out[g * 64 : g * 64 + 64, j * width : (j + 1) * width] for g in range(4)]
        four_ref[:, j] = jnp.concatenate(pieces + [blank], axis=1).reshape(NL, 4, 384)


def legendre_kernel(
    got_ref, weight_ref, state_ref, out_hbm, state_hbm, band_ref, out_ref, sems
):
    saves = [pltpu.make_async_copy(state_ref, state_hbm, sems.at[2])]
    saves[0].start()
    width = LEV_OWN * BAND
    band_ref[1] = jnp.zeros_like(band_ref[1])
    for i in range(NL):
        part = (got_ref[i, 0] + got_ref[i, 1]) + (got_ref[i, 2] + got_ref[i, 3])
        bands = jnp.concatenate([part[:, g * width : (g + 1) * width] for g in range(4)], axis=0)
        h, at = divmod(i * BAND, 128)
        first = min(BAND, 128 - at)
        for k in range(LEV_OWN):
            row = slice(k * 16, k * 16 + 16)
            piece = bands[:, k * BAND : (k + 1) * BAND]
            band_ref[h, row, at : at + first] = piece[:, :first]
            if first < BAND:
                band_ref[h + 1, row, 0 : BAND - first] = piece[:, first:]
    dims = (((1,), (1,)), ((), ()))
    for s in range(SLOTS_OWN):
        rows = [band_ref[h, pl.ds(s, 2 * LEV_OWN, stride=8), :] for h in range(2)]
        hi, lo = split2(jnp.concatenate(rows, axis=1)[:, :NLAT])
        parts = jnp.concatenate((hi, hi), axis=1)
        out = lax.dot_general(parts, weight_ref[s], dims, preferred_element_type=F32)
        out = out + lax.dot_general(lo, weight_ref[s, :, 0:NLAT], dims, preferred_element_type=F32)
        out_ref[:, s, :, :] = out.reshape(LEV_OWN, 2, MMAX)
        if s % 4 == 3:
            part = pl.ds(s - 3, 4)
            save = pltpu.make_async_copy(out_ref.at[:, part], out_hbm.at[:, part], sems.at[s // 4])
            save.start()
            saves.append(save)
    for save in saves:
        save.wait()


def geometry():
    theta = (np.arange(NLAT) + 0.5) * (math.pi / NLAT)
    sine = np.sin(theta)
    rows = np.zeros((4, 256))
    rows[0, :NLAT] = np.cos(theta)
    rows[1, :NLAT] = np.log(sine)
    rows[2, :NLAT] = sine / math.sqrt(NLAT)
    for m in range(MMAX):
        logs = math.lgamma(m + 1.5) - math.lgamma(1.5) - math.lgamma(m + 1.0)
        rows[3, m] = 0.5 * logs - 0.5 * math.log(2.0)
    return rows.astype(np.float32)


def call(kernel, out, specs, scratch=(), out_specs=None):
    return pl.pallas_call(
        kernel,
        out_shape=out,
        in_specs=specs,
        out_specs=out_specs or jax.tree.map(lambda _: VMEM, out),
        scratch_shapes=list(scratch),
        compiler_params=params(),
    )


def stay(x):
    return pltpu.with_memory_space_constraint(x, pltpu.HBM)


def shards(state, forcing, crm_moisture, cloud_order, wave_table):
    shape = jax.ShapeDtypeStruct
    state = state.transpose(0, 2, 3, 1, 4).reshape(ROWS, 1, LONS)
    forcing = forcing.transpose(0, 2, 3, 1, 4).reshape(ROWS, 1, LONS)
    moist = crm_moisture.transpose(0, 2, 3, 4, 1, 5).reshape(LEVELS, NCRM, RUNS)
    order = cloud_order.reshape(1, COLS)
    waves = wave_table.reshape(1, MMAX)
    outgoing, cols = call(
        pack_kernel,
        (shape((TARGETS, 8, 128), F32), shape((2 * LEVELS, COLS), F32)),
        [HBM] * 3,
        [
            pltpu.VMEM((ROWS, 1, LONS), F32),
            pltpu.VMEM((ROWS, 1, LONS), F32),
            pltpu.VMEM((1, COLS), jnp.int32),
            pltpu.VMEM((COLS, COLS), BF16),
            pltpu.VMEM((TARGETS, 8, 128), F32),
            pltpu.SemaphoreType.DMA((4,)),
        ],
        (HBM, VMEM),
    )(*(stay(x) for x in (state, forcing, order)))
    outgoing, waves = lax.optimization_barrier((outgoing, waves))
    arrived = lax.all_to_all(outgoing, ("sec", "lat"), split_axis=0, concat_axis=0, tiled=True)
    trig, weights, water, tail, column = call(
        table_kernel,
        (
            shape((2 * MMAX, 384), BF16),
            shape((SLOTS_OWN, MMAX, 2 * NLAT), BF16),
            shape((LEVELS, 2, 4, 8, 128), F32),
            shape((LEVELS // 4, 4, 8, 128), F32),
            shape((COLS, 128), F32),
        ),
        [HBM] * 4,
        [
            pltpu.VMEM((1, MMAX), jnp.int32),
            pltpu.VMEM((4, 256), F32),
            pltpu.VMEM((1, COLS), jnp.int32),
            pltpu.VMEM((LEVELS, NCRM, RUNS), BF16),
            pltpu.VMEM((2, MMAX * SLOTS_OWN, 128), F32),
            pltpu.VMEM((MMAX, 128), F32),
            pltpu.VMEM((LEVELS, 3, NCRM, 128), F32),
            pltpu.SemaphoreType.DMA((4,)),
        ],
    )(*(stay(x) for x in (waves, jnp.asarray(geometry()), order, moist)))
    arrived, trig = lax.optimization_barrier((arrived, trig))
    rain = call(
        cloud_kernel,
        shape((TARGETS, 4, 128), F32),
        [VMEM] * 3,
        [
            pltpu.VMEM((3, 32, 128), F32),
            pltpu.VMEM((3, 64, 128), F32),
            pltpu.VMEM((2, 32, 128), F32),
            pltpu.VMEM((2, 32, 128), F32),
            pltpu.VMEM((2, 32, 128), F32),
            pltpu.VMEM((3, 32, 128), F32),
            pltpu.VMEM((5, 8, 128), F32),
        ],
    )(arrived, water, tail)
    returned = lax.all_to_all(rain, ("sec", "lat"), split_axis=0, concat_axis=0, tiled=True)
    updated, fourier = call(
        update_kernel,
        (shape((ROWS, 1, LONS), F32), shape((NL, NC, 4, 384), F32)),
        [VMEM] * 4,
        [
            pltpu.VMEM((32, COLS), F32),
            pltpu.VMEM((ROWS, 128), F32),
            pltpu.VMEM((COLS, COLS), BF16),
        ],
    )(returned, column, cols, trig)
    bands = lax.all_to_all(
        fourier.reshape(NL * NC, 4, 384), ("lat", "col"), split_axis=0, concat_axis=0, tiled=True
    )
    spectral, updated = call(
        legendre_kernel,
        (shape((LEV_OWN, SLOTS_OWN, 2, MMAX), F32), shape((ROWS, 1, LONS), F32)),
        [VMEM] * 3,
        [
            pltpu.VMEM((2, LEV_OWN * 16, 128), F32),
            pltpu.VMEM((LEV_OWN, SLOTS_OWN, 2, MMAX), F32),
            pltpu.SemaphoreType.DMA((3,)),
        ],
        (HBM, HBM),
    )(bands.reshape(NL, NC, 4, 384), weights, updated)
    new_state = updated.reshape(1, LEVELS, BAND, 1, LONS).transpose(0, 3, 1, 2, 4)
    return new_state, spectral[None, None]


def solution(mesh):
    placed = (
        P(None, "sec", None, "lat", "col"),
        P(None, "sec", None, "lat", "col"),
        P(None, None, None, ("sec", "lat"), "col", None),
        P("col", "lat", None),
        P(),
    )
    return jax.shard_map(
        shards,
        mesh=mesh,
        in_specs=placed,
        out_specs=(P(None, "sec", None, "lat", "col"), P("sec", None, "col", "lat", None, None)),
        check_vma=False,
    )
```

```python
import math

import jax
import jax.numpy as jnp
import numpy as np
from jax import lax
from jax.experimental import pallas as pl
from jax.experimental.pallas import tpu as pltpu
from jax.sharding import PartitionSpec as P

NLON = 384
NLAT = 192
MMAX = 128
NSUB = 4
NCRM = 32
LEVELS = 28
BAND = 12
LONS = 96
COLS = BAND * LONS
ROWS = LEVELS * BAND
TARGETS = 64
PER = 18
NL = 16
NS = 4
NC = 4
RUNS = NL * PER
HALF = 4 * PER
TAIL = RUNS - 256
LEV_OWN = LEVELS // NC
SLOTS_OWN = MMAX // NL

F32 = jnp.float32
BF16 = jnp.bfloat16
VMEM = pl.BlockSpec(memory_space=pltpu.VMEM)
HBM = pl.BlockSpec(memory_space=pltpu.HBM)


def split2(x):
    hi = x.astype(BF16)
    lo = (x - hi.astype(F32)).astype(BF16)
    return hi, lo


def params(mib=16):
    return pltpu.CompilerParams(vmem_limit_bytes=mib << 20)


def lanes_of(shape):
    return lax.broadcasted_iota(jnp.int32, shape, 1)


def fill_one_hot(order_ref, hot_ref):
    order = order_ref[...]
    step = 96
    for c in range(0, COLS, step):
        ids = lax.broadcasted_iota(jnp.int32, (step, COLS), 0) + c
        hot_ref[c : c + step, :] = jnp.where(ids == order, 1.0, 0.0).astype(BF16)


def trig_rows(orders, trig_ref):
    first = (lax.axis_index("col") * LONS).astype(F32)
    y = lax.broadcasted_iota(jnp.int32, (MMAX, 128), 1).astype(F32) + first
    product = y * orders
    phase = product - NLON * jnp.floor((product + 0.5) * (1.0 / NLON))
    turn = jnp.floor((phase + 48.5) * (1.0 / 96.0))
    x = (phase - 96.0 * turn) * (2.0 * math.pi / NLON)
    z = x * x
    sin = x * (1.0 + z * (-1.0 / 6 + z * (1.0 / 120 + z * (-1.0 / 5040 + z * (1.0 / 362880)))))
    cos = 1.0 + z * (-0.5 + z * (1.0 / 24 + z * (-1.0 / 720 + z * (1.0 / 40320))))
    odd = (turn == 1.0) | (turn == 3.0)
    cos_out = jnp.where(odd, sin, cos)
    sin_out = jnp.where(odd, cos, sin)
    cos_out = jnp.where((turn == 1.0) | (turn == 2.0), -cos_out, cos_out)
    sin_out = jnp.where((turn == 2.0) | (turn == 3.0), -sin_out, sin_out)
    norm = 1.0 / math.sqrt(NLON)
    halves = [
        part.reshape(NL, 2, 4, 128)[:, h].reshape(NL * 4, 128)
        for part in (cos_out * norm, sin_out * norm)
        for h in range(2)
    ]
    hi, lo = split2(jnp.concatenate(halves, axis=0))
    trig_ref[:, 0:128] = hi
    trig_ref[:, 128:256] = hi
    trig_ref[:, 256:384] = lo


def legendre_rows(order, geom_ref, poly_ref, weight_ref):
    lane = lanes_of((SLOTS_OWN, 128)).astype(F32)
    head = jnp.sum(jnp.where(lane == order, geom_ref[3:4, 0:128], 0.0), axis=1, keepdims=True)
    degree = lax.broadcasted_iota(jnp.int32, (SLOTS_OWN, 128), 1).astype(F32)
    active = degree > order
    numer = jnp.where(active, 4.0 * degree * degree - 1.0, 0.0)
    denom = jnp.where(active, degree * degree - order * order, 1.0)
    grow = jnp.sqrt(numer / denom)
    lower = degree - 1.0
    retreat = jnp.sqrt(
        jnp.maximum(lower * lower - order * order, 0.0) / (4.0 * lower * lower - 1.0)
    )
    retreat = grow * retreat
    begin = jnp.where(degree == order, 1.0, 0.0)
    diagonal = jnp.exp(head + order[:, 0:1] * geom_ref[1:2, :]) * geom_ref[2:3, :]
    cosine = jnp.broadcast_to(geom_ref[0:1, :], (SLOTS_OWN, 256))
    previous = jnp.zeros((SLOTS_OWN, 256), F32)
    current = previous
    for n in range(MMAX):
        fresh = (grow[:, n : n + 1] * cosine) * current + (
            begin[:, n : n + 1] * diagonal - retreat[:, n : n + 1] * previous
        )
        poly_ref[0, n * 8 : n * 8 + 8, :] = fresh[:, :128]
        poly_ref[1, n * 8 : n * 8 + 8, :] = fresh[:, 128:]
        previous, current = current, fresh
    for s in range(SLOTS_OWN):
        for h in range(2):
            hi, lo = split2(poly_ref[h, pl.ds(s, MMAX, stride=8), :])
            size = min(128, NLAT - h * 128)
            for part, base in ((hi, 0), (lo, NLAT)):
                at = base + h * 128
                weight_ref[s, :, at : at + size] = part[:, :size]


def arrange_moisture(moist_ref, level_ref, water_ref, tail_ref):
    lane = lanes_of((8, 128))
    blank = jnp.zeros((NCRM, 384 - RUNS), F32)
    for k in range(LEVELS):
        level = jnp.concatenate((moist_ref[k].astype(F32), blank), axis=1)
        for v in range(3):
            level_ref[k, v] = level[:, v * 128 : v * 128 + 128]
    for k in range(LEVELS):
        for v in range(2):
            for n in range(4):
                water_ref[k, v, n] = level_ref[k, v, pl.ds(n, 8, stride=4), :]
    for g in range(LEVELS // 4):
        for n in range(4):
            tile = level_ref[4 * g, 2, pl.ds(n, 8, stride=4), :]
            for kk in range(1, 4):
                more = pltpu.roll(level_ref[4 * g + kk, 2, pl.ds(n, 8, stride=4), :], kk * TAIL, 1)
                tile = jnp.where(lane >= kk * TAIL, more, tile)
            tail_ref[g, n] = tile


def table_kernel(
    wave_hbm,
    geom_hbm,
    order_hbm,
    moist_hbm,
    trig_ref,
    weight_ref,
    water_ref,
    tail_ref,
    column_ref,
    wave_ref,
    geom_ref,
    order_ref,
    moist_ref,
    poly_ref,
    orders_ref,
    level_ref,
    sems,
):
    pairs = (
        (wave_hbm, wave_ref),
        (geom_hbm, geom_ref),
        (order_hbm, order_ref),
        (moist_hbm, moist_ref),
    )
    loads = [pltpu.make_async_copy(src, dst, sems.at[n]) for n, (src, dst) in enumerate(pairs)]
    for load in loads:
        load.start()
    for load in loads[:3]:
        load.wait()
    orders = jnp.broadcast_to(wave_ref[...].astype(F32), (MMAX, MMAX)).T
    orders_ref[...] = orders
    trig_rows(orders, trig_ref)
    first = pl.multiple_of(lax.axis_index("lat") * SLOTS_OWN, SLOTS_OWN)
    legendre_rows(orders_ref[pl.ds(first, SLOTS_OWN), :], geom_ref, poly_ref, weight_ref)
    order = order_ref[...].astype(F32)
    for v in range(COLS // 128):
        at = slice(v * 128, v * 128 + 128)
        column_ref[at, :] = jnp.broadcast_to(order[:, at], (128, 128)).T
    loads[3].wait()
    arrange_moisture(moist_ref, level_ref, water_ref, tail_ref)


def pack_kernel(
    state_hbm,
    force_hbm,
    order_hbm,
    out_hbm,
    cols_ref,
    state_ref,
    force_ref,
    order_ref,
    hot_ref,
    out_ref,
    sems,
):
    pairs = ((order_hbm, order_ref), (state_hbm, state_ref), (force_hbm, force_ref))
    loads = [pltpu.make_async_copy(src, dst, sems.at[n]) for n, (src, dst) in enumerate(pairs)]
    for load in loads:
        load.start()
    loads[0].wait()
    fill_one_hot(order_ref, hot_ref)
    loads[1].wait()
    loads[2].wait()
    for ref, base in ((state_ref, 0), (force_ref, LEVELS)):
        rows = ref[...].reshape(LEVELS, BAND, LONS)
        for b in range(BAND):
            cols_ref[base : base + LEVELS, b * LONS : (b + 1) * LONS] = rows[:, b, :]
    hi, lo = split2(cols_ref[...])
    both = jnp.concatenate((hi, lo), axis=0)
    got = jnp.dot(both, hot_ref[...], preferred_element_type=F32)
    got = got[: 2 * LEVELS] + got[2 * LEVELS :]
    lane = lanes_of((8, 128))
    groups = 2 * LEVELS // 8
    for t in range(TARGETS):
        v, off = divmod(t * PER, 128)
        tile = None
        for q in range(groups):
            src = got[q * 8 : q * 8 + 8, v * 128 : v * 128 + 128]
            if off + PER > 128:
                nxt = got[q * 8 : q * 8 + 8, v * 128 + 128 : v * 128 + 256]
                src = jnp.where(lane < off, nxt, src)
            shift = (q * PER - off) % 128
            if shift:
                src = pltpu.roll(src, shift, 1)
            tile = src if tile is None else jnp.where(lane >= q * PER, src, tile)
        out_ref[t] = tile
    save = pltpu.make_async_copy(out_ref, out_hbm, sems.at[3])
    save.start()
    save.wait()


def gather_lanes(tile_of, q_list, first, count, width, store):
    lane = lanes_of((8, 128))
    for q in q_list:
        for v in range(pl.cdiv(width, 128)):
            acc = None
            for i in range(count):
                start = i * PER - v * 128
                if start >= 128 or start + PER <= 0:
                    continue
                src = tile_of(first + i)
                shift = (i * PER - q * PER) % 128
                if shift:
                    src = pltpu.roll(src, shift, 1)
                acc = src if acc is None else jnp.where(lane >= start, src, acc)
            store(q, v, acc)


def coefficients(wind):
    courant = 0.4 * jnp.tanh(wind)
    mixing = 0.2 + 0.5 * jnp.abs(courant)
    return mixing - 0.5 * courant, mixing + 0.5 * courant


def cloud_tile(start, push, ahead, behind, water):
    keep = 1.0 - (ahead + behind)
    gap = [start + w for w in water]
    wet = [jnp.maximum(g, 0.0) for g in gap]
    total = (wet[0] + wet[1]) + (wet[2] + wet[3])
    for _ in range(NSUB - 1):
        up = gap[1:] + [pltpu.roll(gap[0], 7, 0)]
        down = [pltpu.roll(gap[3], 1, 0)] + gap[:3]
        gap = [
            ((keep * gap[n] - wet[n]) + push) + (ahead * up[n] + behind * down[n]) for n in range(4)
        ]
        wet = [jnp.maximum(g, 0.0) for g in gap]
        total = total + ((wet[0] + wet[1]) + (wet[2] + wet[3]))
    return jnp.sum(total, axis=0, keepdims=True) * (0.5 / NCRM)


def cloud_kernel(
    got_ref,
    water_ref,
    tail_ref,
    out_ref,
    wind_ref,
    diff_ref,
    push_ref,
    left_ref,
    right_ref,
    rain_ref,
    last_ref,
):
    def store_wind(q, v, x):
        wind_ref[v, q * 8 : q * 8 + 8, :] = x

    def store_diff(q, v, x):
        diff_ref[v, q * 8 : q * 8 + 8, :] = x

    gather_lanes(lambda i: got_ref[i], range(4), 0, NL, RUNS, store_wind)
    cache = {}

    def diff(i):
        if i not in cache:
            cache[i] = got_ref[3 * NL + i] - got_ref[2 * NL + i]
        return cache[i]

    gather_lanes(diff, range(7), 0, NL, RUNS, store_diff)
    lane = lanes_of((8, 128))
    groups = LEVELS // 4

    def tails(ref, base):
        tile = ref[2, pl.ds(base, 8, stride=4), :]
        for kk in range(1, 4):
            more = pltpu.roll(ref[2, pl.ds(base + kk, 8, stride=4), :], kk * TAIL, 1)
            tile = jnp.where(lane >= kk * TAIL, more, tile)
        return tile

    wind_tail = tails(wind_ref, 0)
    diff_tail = tails(diff_ref, 0)
    push_tail = tails(diff_ref, LEVELS) * (1.0 / NSUB)
    for v in range(2):
        left_ref[v], right_ref[v] = coefficients(wind_ref[v])
        push_ref[v] = diff_ref[v, LEVELS : LEVELS + 32, :] * (1.0 / NSUB)
    last_ref[4] = jnp.zeros_like(diff_tail)
    last_ref[0] = diff_tail
    last_ref[1] = push_tail
    last_ref[2], last_ref[3] = coefficients(wind_tail)
    rain_ref[...] = jnp.zeros_like(rain_ref)

    def level(g, carry):
        for kk in range(4):
            k = 4 * g + kk
            for v in range(2):

                def row(ref):
                    return jnp.broadcast_to(ref[v, pl.ds(k, 1), :], (8, 128))

                rain_ref[v, pl.ds(k, 1), :] = cloud_tile(
                    row(diff_ref),
                    row(push_ref),
                    row(left_ref),
                    row(right_ref),
                    [water_ref[k, v, n] for n in range(4)],
                )
        rows = [jnp.broadcast_to(last_ref[c, pl.ds(g, 1), :], (8, 128)) for c in range(4)]
        last_ref[4, pl.ds(g, 1), :] = cloud_tile(*rows, [tail_ref[g, n] for n in range(4)])
        return carry

    lax.fori_loop(0, groups, level, 0)
    rain_tail = last_ref[4]
    for kk in range(4):
        piece = rain_tail if kk == 0 else pltpu.roll(rain_tail, 128 - kk * TAIL, 1)
        rain_ref[2, pl.ds(kk, 8, stride=4), :] = piece
    for i in range(NL):
        v, off = divmod(i * PER, 128)
        tile = None
        for q in range(4):
            src = rain_ref[v, q * 8 : q * 8 + 8, :]
            if off + PER > 128:
                nxt = rain_ref[v + 1, q * 8 : q * 8 + 8, :]
                src = jnp.where(lane < off, nxt, src)
            shift = (q * PER - off) % 128
            if shift:
                src = pltpu.roll(src, shift, 1)
            tile = src if tile is None else jnp.where(lane >= q * PER, src, tile)
        low = tile[0:4]
        high = pltpu.roll(tile, HALF, 1)[4:8]
        tile = jnp.where(lane[0:4] < HALF, low, high)
        for s in range(NS):
            out_ref[s * NL + i] = tile


def update_kernel(
    got_ref,
    column_ref,
    cols_ref,
    trig_ref,
    out_ref,
    four_ref,
    slots_ref,
    rows_ref,
    hot_ref,
):
    lane = lanes_of((128, 128)).astype(F32)
    for v in range(COLS // 128):
        rows = slice(v * 128, v * 128 + 128)
        column = column_ref[rows, :]
        for c in range(COLS // 128):
            hot = jnp.where(lane + float(c * 128) == column, 1.0, 0.0)
            hot_ref[rows, c * 128 : c * 128 + 128] = hot.astype(BF16)

    def store(q, v, x):
        slots_ref[q * 8 : q * 8 + 8, v * 128 : v * 128 + 128] = x

    cache = {}

    def tile_of(t):
        if t not in cache:
            tile = got_ref[t]
            cache[t] = jnp.concatenate((tile, pltpu.roll(tile, 128 - HALF, 1)), axis=0)
        return cache[t]

    gather_lanes(tile_of, range(4), 0, TARGETS, COLS, store)
    hi, lo = split2(slots_ref[...])
    both = jnp.concatenate((hi, lo), axis=0)
    back = jnp.dot(both, hot_ref[...], preferred_element_type=F32)
    rain = back[:LEVELS] + back[32 : 32 + LEVELS]
    sec = lax.axis_index("sec")
    add = jnp.where(sec == 2, 1.0, jnp.where(sec == 3, -1.0, 0.0)).astype(F32)
    scale = jnp.where(sec < 2, -1.0 / NSUB, 0.0).astype(F32)
    now = cols_ref[0:LEVELS]
    now = now + (cols_ref[LEVELS : 2 * LEVELS] + rain * (add + scale * now))
    blank = jnp.zeros((LEVELS, 128 - LONS), F32)
    for b in range(BAND):
        piece = jnp.concatenate((now[:, b * LONS : (b + 1) * LONS], blank), axis=1)
        rows_ref[pl.ds(b, LEVELS, stride=BAND), :] = piece
    rows = rows_ref[...]
    out_ref[...] = rows[:, :LONS].reshape(ROWS, 1, LONS)
    hi, lo = split2(rows)
    dims = (((1,), (1,)), ((), ()))
    parts = jnp.concatenate((hi, lo, hi), axis=1)
    out = lax.dot_general(trig_ref[...], parts, dims, preferred_element_type=F32)
    width = LEV_OWN * BAND
    blank = jnp.zeros((NL * 4, 384 - 4 * width), F32)
    for j in range(NC):
        pieces = [out[g * 64 : g * 64 + 64, j * width : (j + 1) * width] for g in range(4)]
        four_ref[j] = jnp.concatenate(pieces + [blank], axis=1).reshape(NL, 4, 384)


def legendre_kernel(
    got_ref, weight_ref, state_ref, out_hbm, state_hbm, band_ref, out_ref, sems
):
    saves = [pltpu.make_async_copy(state_ref, state_hbm, sems.at[2])]
    saves[0].start()
    width = LEV_OWN * BAND
    band_ref[1] = jnp.zeros_like(band_ref[1])
    for i in range(NL):
        part = (got_ref[0, i] + got_ref[1, i]) + (got_ref[2, i] + got_ref[3, i])
        bands = jnp.concatenate([part[:, g * width : (g + 1) * width] for g in range(4)], axis=0)
        h, at = divmod(i * BAND, 128)
        first = min(BAND, 128 - at)
        for k in range(LEV_OWN):
            row = slice(k * 16, k * 16 + 16)
            piece = bands[:, k * BAND : (k + 1) * BAND]
            band_ref[h, row, at : at + first] = piece[:, :first]
            if first < BAND:
                band_ref[h + 1, row, 0 : BAND - first] = piece[:, first:]
    dims = (((1,), (1,)), ((), ()))
    for s in range(SLOTS_OWN):
        rows = [band_ref[h, pl.ds(s, 2 * LEV_OWN, stride=8), :] for h in range(2)]
        hi, lo = split2(jnp.concatenate(rows, axis=1)[:, :NLAT])
        parts = jnp.concatenate((hi, hi), axis=1)
        out = lax.dot_general(parts, weight_ref[s], dims, preferred_element_type=F32)
        out = out + lax.dot_general(lo, weight_ref[s, :, 0:NLAT], dims, preferred_element_type=F32)
        out_ref[:, s, :, :] = out.reshape(LEV_OWN, 2, MMAX)
        if s % 4 == 3:
            part = pl.ds(s - 3, 4)
            save = pltpu.make_async_copy(out_ref.at[:, part], out_hbm.at[:, part], sems.at[s // 4])
            save.start()
            saves.append(save)
    for save in saves:
        save.wait()


def geometry():
    theta = (np.arange(NLAT) + 0.5) * (math.pi / NLAT)
    sine = np.sin(theta)
    rows = np.zeros((4, 256))
    rows[0, :NLAT] = np.cos(theta)
    rows[1, :NLAT] = np.log(sine)
    rows[2, :NLAT] = sine / math.sqrt(NLAT)
    for m in range(MMAX):
        logs = math.lgamma(m + 1.5) - math.lgamma(1.5) - math.lgamma(m + 1.0)
        rows[3, m] = 0.5 * logs - 0.5 * math.log(2.0)
    return rows.astype(np.float32)


def call(kernel, out, specs, scratch=(), out_specs=None):
    return pl.pallas_call(
        kernel,
        out_shape=out,
        in_specs=specs,
        out_specs=out_specs or jax.tree.map(lambda _: VMEM, out),
        scratch_shapes=list(scratch),
        compiler_params=params(),
    )


def stay(x):
    return pltpu.with_memory_space_constraint(x, pltpu.HBM)


def shards(state, forcing, crm_moisture, cloud_order, wave_table):
    shape = jax.ShapeDtypeStruct
    state = state.transpose(0, 2, 3, 1, 4).reshape(ROWS, 1, LONS)
    forcing = forcing.transpose(0, 2, 3, 1, 4).reshape(ROWS, 1, LONS)
    moist = crm_moisture.transpose(0, 2, 3, 4, 1, 5).reshape(LEVELS, NCRM, RUNS)
    order = cloud_order.reshape(1, COLS)
    waves = wave_table.reshape(1, MMAX)
    outgoing, cols = call(
        pack_kernel,
        (shape((TARGETS, 8, 128), F32), shape((2 * LEVELS, COLS), F32)),
        [HBM] * 3,
        [
            pltpu.VMEM((ROWS, 1, LONS), F32),
            pltpu.VMEM((ROWS, 1, LONS), F32),
            pltpu.VMEM((1, COLS), jnp.int32),
            pltpu.VMEM((COLS, COLS), BF16),
            pltpu.VMEM((TARGETS, 8, 128), F32),
            pltpu.SemaphoreType.DMA((4,)),
        ],
        (HBM, VMEM),
    )(*(stay(x) for x in (state, forcing, order)))
    outgoing, waves = lax.optimization_barrier((outgoing, waves))
    arrived = lax.all_to_all(outgoing, ("sec", "lat"), split_axis=0, concat_axis=0, tiled=True)
    trig, weights, water, tail, column = call(
        table_kernel,
        (
            shape((2 * MMAX, 384), BF16),
            shape((SLOTS_OWN, MMAX, 2 * NLAT), BF16),
            shape((LEVELS, 2, 4, 8, 128), F32),
            shape((LEVELS // 4, 4, 8, 128), F32),
            shape((COLS, 128), F32),
        ),
        [HBM] * 4,
        [
            pltpu.VMEM((1, MMAX), jnp.int32),
            pltpu.VMEM((4, 256), F32),
            pltpu.VMEM((1, COLS), jnp.int32),
            pltpu.VMEM((LEVELS, NCRM, RUNS), BF16),
            pltpu.VMEM((2, MMAX * SLOTS_OWN, 128), F32),
            pltpu.VMEM((MMAX, 128), F32),
            pltpu.VMEM((LEVELS, 3, NCRM, 128), F32),
            pltpu.SemaphoreType.DMA((4,)),
        ],
    )(*(stay(x) for x in (waves, jnp.asarray(geometry()), order, moist)))
    arrived, trig = lax.optimization_barrier((arrived, trig))
    rain = call(
        cloud_kernel,
        shape((TARGETS, 4, 128), F32),
        [VMEM] * 3,
        [
            pltpu.VMEM((3, 32, 128), F32),
            pltpu.VMEM((3, 64, 128), F32),
            pltpu.VMEM((2, 32, 128), F32),
            pltpu.VMEM((2, 32, 128), F32),
            pltpu.VMEM((2, 32, 128), F32),
            pltpu.VMEM((3, 32, 128), F32),
            pltpu.VMEM((5, 8, 128), F32),
        ],
    )(arrived, water, tail)
    returned = lax.all_to_all(rain, ("sec", "lat"), split_axis=0, concat_axis=0, tiled=True)
    updated, fourier = call(
        update_kernel,
        (shape((ROWS, 1, LONS), F32), shape((NC, NL, 4, 384), F32)),
        [VMEM] * 4,
        [
            pltpu.VMEM((32, COLS), F32),
            pltpu.VMEM((ROWS, 128), F32),
            pltpu.VMEM((COLS, COLS), BF16),
        ],
    )(returned, column, cols, trig)
    bands = lax.all_to_all(
        fourier.reshape(NL * NC, 4, 384), ("col", "lat"), split_axis=0, concat_axis=0, tiled=True
    )
    spectral, updated = call(
        legendre_kernel,
        (shape((LEV_OWN, SLOTS_OWN, 2, MMAX), F32), shape((ROWS, 1, LONS), F32)),
        [VMEM] * 3,
        [
            pltpu.VMEM((2, LEV_OWN * 16, 128), F32),
            pltpu.VMEM((LEV_OWN, SLOTS_OWN, 2, MMAX), F32),
            pltpu.SemaphoreType.DMA((3,)),
        ],
        (HBM, HBM),
    )(bands.reshape(NC, NL, 4, 384), weights, updated)
    new_state = updated.reshape(1, LEVELS, BAND, 1, LONS).transpose(0, 3, 1, 2, 4)
    return new_state, spectral[None, None]


def solution(mesh):
    placed = (
        P(None, "sec", None, "lat", "col"),
        P(None, "sec", None, "lat", "col"),
        P(None, None, None, ("sec", "lat"), "col", None),
        P("col", "lat", None),
        P(),
    )
    return jax.shard_map(
        shards,
        mesh=mesh,
        in_specs=placed,
        out_specs=(P(None, "sec", None, "lat", "col"), P("sec", None, "col", "lat", None, None)),
        check_vma=False,
    )
```

```python
import math

import jax
import jax.numpy as jnp
import numpy as np
from jax import lax
from jax.experimental import pallas as pl
from jax.experimental.pallas import tpu as pltpu
from jax.sharding import PartitionSpec as P

NLON = 384
NLAT = 192
MMAX = 128
NSUB = 4
NCRM = 32
LEVELS = 28
BAND = 12
LONS = 96
COLS = BAND * LONS
ROWS = LEVELS * BAND
TARGETS = 64
PER = 18
NL = 16
NS = 4
NC = 4
RUNS = NL * PER
HALF = 4 * PER
TAIL = RUNS - 256
LEV_OWN = LEVELS // NC
SLOTS_OWN = MMAX // NL

F32 = jnp.float32
BF16 = jnp.bfloat16
VMEM = pl.BlockSpec(memory_space=pltpu.VMEM)
HBM = pl.BlockSpec(memory_space=pltpu.HBM)


def split2(x):
    hi = x.astype(BF16)
    lo = (x - hi.astype(F32)).astype(BF16)
    return hi, lo


def params(mib=16):
    return pltpu.CompilerParams(vmem_limit_bytes=mib << 20)


def lanes_of(shape):
    return lax.broadcasted_iota(jnp.int32, shape, 1)


def place(t):
    return t % NL * NS + t // NL


def fill_one_hot(order_ref, hot_ref):
    order = order_ref[...]
    step = 96
    for c in range(0, COLS, step):
        ids = lax.broadcasted_iota(jnp.int32, (step, COLS), 0) + c
        hot_ref[c : c + step, :] = jnp.where(ids == order, 1.0, 0.0).astype(BF16)


def trig_rows(orders, trig_ref):
    first = (lax.axis_index("col") * LONS).astype(F32)
    y = lax.broadcasted_iota(jnp.int32, (MMAX, 128), 1).astype(F32) + first
    product = y * orders
    phase = product - NLON * jnp.floor((product + 0.5) * (1.0 / NLON))
    turn = jnp.floor((phase + 48.5) * (1.0 / 96.0))
    x = (phase - 96.0 * turn) * (2.0 * math.pi / NLON)
    z = x * x
    sin = x * (1.0 + z * (-1.0 / 6 + z * (1.0 / 120 + z * (-1.0 / 5040 + z * (1.0 / 362880)))))
    cos = 1.0 + z * (-0.5 + z * (1.0 / 24 + z * (-1.0 / 720 + z * (1.0 / 40320))))
    odd = (turn == 1.0) | (turn == 3.0)
    cos_out = jnp.where(odd, sin, cos)
    sin_out = jnp.where(odd, cos, sin)
    cos_out = jnp.where((turn == 1.0) | (turn == 2.0), -cos_out, cos_out)
    sin_out = jnp.where((turn == 2.0) | (turn == 3.0), -sin_out, sin_out)
    norm = 1.0 / math.sqrt(NLON)
    halves = [
        part.reshape(NL, 2, 4, 128)[:, h].reshape(NL * 4, 128)
        for part in (cos_out * norm, sin_out * norm)
        for h in range(2)
    ]
    hi, lo = split2(jnp.concatenate(halves, axis=0))
    trig_ref[:, 0:128] = hi
    trig_ref[:, 128:256] = hi
    trig_ref[:, 256:384] = lo


def legendre_rows(order, geom_ref, poly_ref, weight_ref):
    lane = lanes_of((SLOTS_OWN, 128)).astype(F32)
    head = jnp.sum(jnp.where(lane == order, geom_ref[3:4, 0:128], 0.0), axis=1, keepdims=True)
    degree = lax.broadcasted_iota(jnp.int32, (SLOTS_OWN, 128), 1).astype(F32)
    active = degree > order
    numer = jnp.where(active, 4.0 * degree * degree - 1.0, 0.0)
    denom = jnp.where(active, degree * degree - order * order, 1.0)
    grow = jnp.sqrt(numer / denom)
    lower = degree - 1.0
    retreat = jnp.sqrt(
        jnp.maximum(lower * lower - order * order, 0.0) / (4.0 * lower * lower - 1.0)
    )
    retreat = grow * retreat
    begin = jnp.where(degree == order, 1.0, 0.0)
    diagonal = jnp.exp(head + order[:, 0:1] * geom_ref[1:2, :]) * geom_ref[2:3, :]
    cosine = jnp.broadcast_to(geom_ref[0:1, :], (SLOTS_OWN, 256))
    previous = jnp.zeros((SLOTS_OWN, 256), F32)
    current = previous
    for n in range(MMAX):
        fresh = (grow[:, n : n + 1] * cosine) * current + (
            begin[:, n : n + 1] * diagonal - retreat[:, n : n + 1] * previous
        )
        poly_ref[0, n * 8 : n * 8 + 8, :] = fresh[:, :128]
        poly_ref[1, n * 8 : n * 8 + 8, :] = fresh[:, 128:]
        previous, current = current, fresh
    for s in range(SLOTS_OWN):
        for h in range(2):
            hi, lo = split2(poly_ref[h, pl.ds(s, MMAX, stride=8), :])
            size = min(128, NLAT - h * 128)
            for part, base in ((hi, 0), (lo, NLAT)):
                at = base + h * 128
                weight_ref[s, :, at : at + size] = part[:, :size]


def arrange_moisture(moist_ref, level_ref, water_ref, tail_ref):
    lane = lanes_of((8, 128))
    blank = jnp.zeros((NCRM, 384 - RUNS), F32)
    for k in range(LEVELS):
        level = jnp.concatenate((moist_ref[k].astype(F32), blank), axis=1)
        for v in range(3):
            level_ref[k, v] = level[:, v * 128 : v * 128 + 128]
    for k in range(LEVELS):
        for v in range(2):
            for n in range(4):
                water_ref[k, v, n] = level_ref[k, v, pl.ds(n, 8, stride=4), :]
    for g in range(LEVELS // 4):
        for n in range(4):
            tile = level_ref[4 * g, 2, pl.ds(n, 8, stride=4), :]
            for kk in range(1, 4):
                more = pltpu.roll(level_ref[4 * g + kk, 2, pl.ds(n, 8, stride=4), :], kk * TAIL, 1)
                tile = jnp.where(lane >= kk * TAIL, more, tile)
            tail_ref[g, n] = tile


def table_kernel(
    wave_hbm,
    geom_hbm,
    order_hbm,
    moist_hbm,
    trig_ref,
    weight_ref,
    water_ref,
    tail_ref,
    column_ref,
    wave_ref,
    geom_ref,
    order_ref,
    moist_ref,
    poly_ref,
    orders_ref,
    level_ref,
    sems,
):
    pairs = (
        (wave_hbm, wave_ref),
        (geom_hbm, geom_ref),
        (order_hbm, order_ref),
        (moist_hbm, moist_ref),
    )
    loads = [pltpu.make_async_copy(src, dst, sems.at[n]) for n, (src, dst) in enumerate(pairs)]
    for load in loads:
        load.start()
    for load in loads[:3]:
        load.wait()
    orders = jnp.broadcast_to(wave_ref[...].astype(F32), (MMAX, MMAX)).T
    orders_ref[...] = orders
    trig_rows(orders, trig_ref)
    first = pl.multiple_of(lax.axis_index("lat") * SLOTS_OWN, SLOTS_OWN)
    legendre_rows(orders_ref[pl.ds(first, SLOTS_OWN), :], geom_ref, poly_ref, weight_ref)
    order = order_ref[...].astype(F32)
    for v in range(COLS // 128):
        at = slice(v * 128, v * 128 + 128)
        column_ref[at, :] = jnp.broadcast_to(order[:, at], (128, 128)).T
    loads[3].wait()
    arrange_moisture(moist_ref, level_ref, water_ref, tail_ref)


def pack_kernel(
    state_hbm,
    force_hbm,
    order_hbm,
    out_hbm,
    cols_ref,
    state_ref,
    force_ref,
    order_ref,
    hot_ref,
    out_ref,
    sems,
):
    pairs = ((order_hbm, order_ref), (state_hbm, state_ref), (force_hbm, force_ref))
    loads = [pltpu.make_async_copy(src, dst, sems.at[n]) for n, (src, dst) in enumerate(pairs)]
    for load in loads:
        load.start()
    loads[0].wait()
    fill_one_hot(order_ref, hot_ref)
    loads[1].wait()
    loads[2].wait()
    for ref, base in ((state_ref, 0), (force_ref, LEVELS)):
        rows = ref[...].reshape(LEVELS, BAND, LONS)
        for b in range(BAND):
            cols_ref[base : base + LEVELS, b * LONS : (b + 1) * LONS] = rows[:, b, :]
    hi, lo = split2(cols_ref[...])
    both = jnp.concatenate((hi, lo), axis=0)
    got = jnp.dot(both, hot_ref[...], preferred_element_type=F32)
    got = got[: 2 * LEVELS] + got[2 * LEVELS :]
    lane = lanes_of((8, 128))
    groups = 2 * LEVELS // 8
    for t in range(TARGETS):
        v, off = divmod(t * PER, 128)
        tile = None
        for q in range(groups):
            src = got[q * 8 : q * 8 + 8, v * 128 : v * 128 + 128]
            if off + PER > 128:
                nxt = got[q * 8 : q * 8 + 8, v * 128 + 128 : v * 128 + 256]
                src = jnp.where(lane < off, nxt, src)
            shift = (q * PER - off) % 128
            if shift:
                src = pltpu.roll(src, shift, 1)
            tile = src if tile is None else jnp.where(lane >= q * PER, src, tile)
        out_ref[place(t)] = tile
    save = pltpu.make_async_copy(out_ref, out_hbm, sems.at[3])
    save.start()
    save.wait()


def gather_lanes(tile_of, q_list, first, count, width, store):
    lane = lanes_of((8, 128))
    for q in q_list:
        for v in range(pl.cdiv(width, 128)):
            acc = None
            for i in range(count):
                start = i * PER - v * 128
                if start >= 128 or start + PER <= 0:
                    continue
                src = tile_of(first + i)
                shift = (i * PER - q * PER) % 128
                if shift:
                    src = pltpu.roll(src, shift, 1)
                acc = src if acc is None else jnp.where(lane >= start, src, acc)
            store(q, v, acc)


def coefficients(wind):
    courant = 0.4 * jnp.tanh(wind)
    mixing = 0.2 + 0.5 * jnp.abs(courant)
    return mixing - 0.5 * courant, mixing + 0.5 * courant


def cloud_tile(start, push, ahead, behind, water):
    keep = 1.0 - (ahead + behind)
    gap = [start + w for w in water]
    wet = [jnp.maximum(g, 0.0) for g in gap]
    total = (wet[0] + wet[1]) + (wet[2] + wet[3])
    for _ in range(NSUB - 1):
        up = gap[1:] + [pltpu.roll(gap[0], 7, 0)]
        down = [pltpu.roll(gap[3], 1, 0)] + gap[:3]
        gap = [
            ((keep * gap[n] - wet[n]) + push) + (ahead * up[n] + behind * down[n]) for n in range(4)
        ]
        wet = [jnp.maximum(g, 0.0) for g in gap]
        total = total + ((wet[0] + wet[1]) + (wet[2] + wet[3]))
    return jnp.sum(total, axis=0, keepdims=True) * (0.5 / NCRM)


def cloud_kernel(
    got_ref,
    water_ref,
    tail_ref,
    out_ref,
    wind_ref,
    diff_ref,
    push_ref,
    left_ref,
    right_ref,
    rain_ref,
    last_ref,
):
    def store_wind(q, v, x):
        wind_ref[v, q * 8 : q * 8 + 8, :] = x

    def store_diff(q, v, x):
        diff_ref[v, q * 8 : q * 8 + 8, :] = x

    gather_lanes(lambda i: got_ref[place(i)], range(4), 0, NL, RUNS, store_wind)
    cache = {}

    def diff(i):
        if i not in cache:
            cache[i] = got_ref[place(3 * NL + i)] - got_ref[place(2 * NL + i)]
        return cache[i]

    gather_lanes(diff, range(7), 0, NL, RUNS, store_diff)
    lane = lanes_of((8, 128))
    groups = LEVELS // 4

    def tails(ref, base):
        tile = ref[2, pl.ds(base, 8, stride=4), :]
        for kk in range(1, 4):
            more = pltpu.roll(ref[2, pl.ds(base + kk, 8, stride=4), :], kk * TAIL, 1)
            tile = jnp.where(lane >= kk * TAIL, more, tile)
        return tile

    wind_tail = tails(wind_ref, 0)
    diff_tail = tails(diff_ref, 0)
    push_tail = tails(diff_ref, LEVELS) * (1.0 / NSUB)
    for v in range(2):
        left_ref[v], right_ref[v] = coefficients(wind_ref[v])
        push_ref[v] = diff_ref[v, LEVELS : LEVELS + 32, :] * (1.0 / NSUB)
    last_ref[4] = jnp.zeros_like(diff_tail)
    last_ref[0] = diff_tail
    last_ref[1] = push_tail
    last_ref[2], last_ref[3] = coefficients(wind_tail)
    rain_ref[...] = jnp.zeros_like(rain_ref)

    def level(g, carry):
        for kk in range(4):
            k = 4 * g + kk
            for v in range(2):

                def row(ref):
                    return jnp.broadcast_to(ref[v, pl.ds(k, 1), :], (8, 128))

                rain_ref[v, pl.ds(k, 1), :] = cloud_tile(
                    row(diff_ref),
                    row(push_ref),
                    row(left_ref),
                    row(right_ref),
                    [water_ref[k, v, n] for n in range(4)],
                )
        rows = [jnp.broadcast_to(last_ref[c, pl.ds(g, 1), :], (8, 128)) for c in range(4)]
        last_ref[4, pl.ds(g, 1), :] = cloud_tile(*rows, [tail_ref[g, n] for n in range(4)])
        return carry

    lax.fori_loop(0, groups, level, 0)
    rain_tail = last_ref[4]
    for kk in range(4):
        piece = rain_tail if kk == 0 else pltpu.roll(rain_tail, 128 - kk * TAIL, 1)
        rain_ref[2, pl.ds(kk, 8, stride=4), :] = piece
    for i in range(NL):
        v, off = divmod(i * PER, 128)
        tile = None
        for q in range(4):
            src = rain_ref[v, q * 8 : q * 8 + 8, :]
            if off + PER > 128:
                nxt = rain_ref[v + 1, q * 8 : q * 8 + 8, :]
                src = jnp.where(lane < off, nxt, src)
            shift = (q * PER - off) % 128
            if shift:
                src = pltpu.roll(src, shift, 1)
            tile = src if tile is None else jnp.where(lane >= q * PER, src, tile)
        low = tile[0:4]
        high = pltpu.roll(tile, HALF, 1)[4:8]
        tile = jnp.where(lane[0:4] < HALF, low, high)
        for s in range(NS):
            out_ref[place(s * NL + i)] = tile


def update_kernel(
    got_ref,
    column_ref,
    cols_ref,
    trig_ref,
    out_ref,
    four_ref,
    slots_ref,
    rows_ref,
    hot_ref,
):
    lane = lanes_of((128, 128)).astype(F32)
    for v in range(COLS // 128):
        rows = slice(v * 128, v * 128 + 128)
        column = column_ref[rows, :]
        for c in range(COLS // 128):
            hot = jnp.where(lane + float(c * 128) == column, 1.0, 0.0)
            hot_ref[rows, c * 128 : c * 128 + 128] = hot.astype(BF16)

    def store(q, v, x):
        slots_ref[q * 8 : q * 8 + 8, v * 128 : v * 128 + 128] = x

    cache = {}

    def tile_of(t):
        if t not in cache:
            tile = got_ref[place(t)]
            cache[t] = jnp.concatenate((tile, pltpu.roll(tile, 128 - HALF, 1)), axis=0)
        return cache[t]

    gather_lanes(tile_of, range(4), 0, TARGETS, COLS, store)
    hi, lo = split2(slots_ref[...])
    both = jnp.concatenate((hi, lo), axis=0)
    back = jnp.dot(both, hot_ref[...], preferred_element_type=F32)
    rain = back[:LEVELS] + back[32 : 32 + LEVELS]
    sec = lax.axis_index("sec")
    add = jnp.where(sec == 2, 1.0, jnp.where(sec == 3, -1.0, 0.0)).astype(F32)
    scale = jnp.where(sec < 2, -1.0 / NSUB, 0.0).astype(F32)
    now = cols_ref[0:LEVELS]
    now = now + (cols_ref[LEVELS : 2 * LEVELS] + rain * (add + scale * now))
    blank = jnp.zeros((LEVELS, 128 - LONS), F32)
    for b in range(BAND):
        piece = jnp.concatenate((now[:, b * LONS : (b + 1) * LONS], blank), axis=1)
        rows_ref[pl.ds(b, LEVELS, stride=BAND), :] = piece
    rows = rows_ref[...]
    out_ref[...] = rows[:, :LONS].reshape(ROWS, 1, LONS)
    hi, lo = split2(rows)
    dims = (((1,), (1,)), ((), ()))
    parts = jnp.concatenate((hi, lo, hi), axis=1)
    out = lax.dot_general(trig_ref[...], parts, dims, preferred_element_type=F32)
    width = LEV_OWN * BAND
    blank = jnp.zeros((NL * 4, 384 - 4 * width), F32)
    for j in range(NC):
        pieces = [out[g * 64 : g * 64 + 64, j * width : (j + 1) * width] for g in range(4)]
        four_ref[j] = jnp.concatenate(pieces + [blank], axis=1).reshape(NL, 4, 384)


def legendre_kernel(
    got_ref, weight_ref, state_ref, out_hbm, state_hbm, band_ref, out_ref, sems
):
    saves = [pltpu.make_async_copy(state_ref, state_hbm, sems.at[2])]
    saves[0].start()
    width = LEV_OWN * BAND
    band_ref[1] = jnp.zeros_like(band_ref[1])
    for i in range(NL):
        part = (got_ref[0, i] + got_ref[1, i]) + (got_ref[2, i] + got_ref[3, i])
        bands = jnp.concatenate([part[:, g * width : (g + 1) * width] for g in range(4)], axis=0)
        h, at = divmod(i * BAND, 128)
        first = min(BAND, 128 - at)
        for k in range(LEV_OWN):
            row = slice(k * 16, k * 16 + 16)
            piece = bands[:, k * BAND : (k + 1) * BAND]
            band_ref[h, row, at : at + first] = piece[:, :first]
            if first < BAND:
                band_ref[h + 1, row, 0 : BAND - first] = piece[:, first:]
    dims = (((1,), (1,)), ((), ()))
    for s in range(SLOTS_OWN):
        rows = [band_ref[h, pl.ds(s, 2 * LEV_OWN, stride=8), :] for h in range(2)]
        hi, lo = split2(jnp.concatenate(rows, axis=1)[:, :NLAT])
        parts = jnp.concatenate((hi, hi), axis=1)
        out = lax.dot_general(parts, weight_ref[s], dims, preferred_element_type=F32)
        out = out + lax.dot_general(lo, weight_ref[s, :, 0:NLAT], dims, preferred_element_type=F32)
        out_ref[:, s, :, :] = out.reshape(LEV_OWN, 2, MMAX)
        if s % 4 == 3:
            part = pl.ds(s - 3, 4)
            save = pltpu.make_async_copy(out_ref.at[:, part], out_hbm.at[:, part], sems.at[s // 4])
            save.start()
            saves.append(save)
    for save in saves:
        save.wait()


def geometry():
    theta = (np.arange(NLAT) + 0.5) * (math.pi / NLAT)
    sine = np.sin(theta)
    rows = np.zeros((4, 256))
    rows[0, :NLAT] = np.cos(theta)
    rows[1, :NLAT] = np.log(sine)
    rows[2, :NLAT] = sine / math.sqrt(NLAT)
    for m in range(MMAX):
        logs = math.lgamma(m + 1.5) - math.lgamma(1.5) - math.lgamma(m + 1.0)
        rows[3, m] = 0.5 * logs - 0.5 * math.log(2.0)
    return rows.astype(np.float32)


def call(kernel, out, specs, scratch=(), out_specs=None):
    return pl.pallas_call(
        kernel,
        out_shape=out,
        in_specs=specs,
        out_specs=out_specs or jax.tree.map(lambda _: VMEM, out),
        scratch_shapes=list(scratch),
        compiler_params=params(),
    )


def stay(x):
    return pltpu.with_memory_space_constraint(x, pltpu.HBM)


def shards(state, forcing, crm_moisture, cloud_order, wave_table):
    shape = jax.ShapeDtypeStruct
    state = state.transpose(0, 2, 3, 1, 4).reshape(ROWS, 1, LONS)
    forcing = forcing.transpose(0, 2, 3, 1, 4).reshape(ROWS, 1, LONS)
    moist = crm_moisture.transpose(0, 2, 3, 4, 1, 5).reshape(LEVELS, NCRM, RUNS)
    order = cloud_order.reshape(1, COLS)
    waves = wave_table.reshape(1, MMAX)
    outgoing, cols = call(
        pack_kernel,
        (shape((TARGETS, 8, 128), F32), shape((2 * LEVELS, COLS), F32)),
        [HBM] * 3,
        [
            pltpu.VMEM((ROWS, 1, LONS), F32),
            pltpu.VMEM((ROWS, 1, LONS), F32),
            pltpu.VMEM((1, COLS), jnp.int32),
            pltpu.VMEM((COLS, COLS), BF16),
            pltpu.VMEM((TARGETS, 8, 128), F32),
            pltpu.SemaphoreType.DMA((4,)),
        ],
        (HBM, VMEM),
    )(*(stay(x) for x in (state, forcing, order)))
    outgoing, waves = lax.optimization_barrier((outgoing, waves))
    arrived = lax.all_to_all(outgoing, ("lat", "sec"), split_axis=0, concat_axis=0, tiled=True)
    trig, weights, water, tail, column = call(
        table_kernel,
        (
            shape((2 * MMAX, 384), BF16),
            shape((SLOTS_OWN, MMAX, 2 * NLAT), BF16),
            shape((LEVELS, 2, 4, 8, 128), F32),
            shape((LEVELS // 4, 4, 8, 128), F32),
            shape((COLS, 128), F32),
        ),
        [HBM] * 4,
        [
            pltpu.VMEM((1, MMAX), jnp.int32),
            pltpu.VMEM((4, 256), F32),
            pltpu.VMEM((1, COLS), jnp.int32),
            pltpu.VMEM((LEVELS, NCRM, RUNS), BF16),
            pltpu.VMEM((2, MMAX * SLOTS_OWN, 128), F32),
            pltpu.VMEM((MMAX, 128), F32),
            pltpu.VMEM((LEVELS, 3, NCRM, 128), F32),
            pltpu.SemaphoreType.DMA((4,)),
        ],
    )(*(stay(x) for x in (waves, jnp.asarray(geometry()), order, moist)))
    arrived, trig = lax.optimization_barrier((arrived, trig))
    rain = call(
        cloud_kernel,
        shape((TARGETS, 4, 128), F32),
        [VMEM] * 3,
        [
            pltpu.VMEM((3, 32, 128), F32),
            pltpu.VMEM((3, 64, 128), F32),
            pltpu.VMEM((2, 32, 128), F32),
            pltpu.VMEM((2, 32, 128), F32),
            pltpu.VMEM((2, 32, 128), F32),
            pltpu.VMEM((3, 32, 128), F32),
            pltpu.VMEM((5, 8, 128), F32),
        ],
    )(arrived, water, tail)
    returned = lax.all_to_all(rain, ("lat", "sec"), split_axis=0, concat_axis=0, tiled=True)
    updated, fourier = call(
        update_kernel,
        (shape((ROWS, 1, LONS), F32), shape((NC, NL, 4, 384), F32)),
        [VMEM] * 4,
        [
            pltpu.VMEM((32, COLS), F32),
            pltpu.VMEM((ROWS, 128), F32),
            pltpu.VMEM((COLS, COLS), BF16),
        ],
    )(returned, column, cols, trig)
    bands = lax.all_to_all(
        fourier.reshape(NL * NC, 4, 384), ("col", "lat"), split_axis=0, concat_axis=0, tiled=True
    )
    spectral, updated = call(
        legendre_kernel,
        (shape((LEV_OWN, SLOTS_OWN, 2, MMAX), F32), shape((ROWS, 1, LONS), F32)),
        [VMEM] * 3,
        [
            pltpu.VMEM((2, LEV_OWN * 16, 128), F32),
            pltpu.VMEM((LEV_OWN, SLOTS_OWN, 2, MMAX), F32),
            pltpu.SemaphoreType.DMA((3,)),
        ],
        (HBM, HBM),
    )(bands.reshape(NC, NL, 4, 384), weights, updated)
    new_state = updated.reshape(1, LEVELS, BAND, 1, LONS).transpose(0, 3, 1, 2, 4)
    return new_state, spectral[None, None]


def solution(mesh):
    placed = (
        P(None, "sec", None, "lat", "col"),
        P(None, "sec", None, "lat", "col"),
        P(None, None, None, ("sec", "lat"), "col", None),
        P("col", "lat", None),
        P(),
    )
    return jax.shard_map(
        shards,
        mesh=mesh,
        in_specs=placed,
        out_specs=(P(None, "sec", None, "lat", "col"), P("sec", None, "col", "lat", None, None)),
        check_vma=False,
    )
```

```python
import math

import jax
import jax.numpy as jnp
import numpy as np
from jax import lax
from jax.experimental import pallas as pl
from jax.experimental.pallas import tpu as pltpu
from jax.sharding import PartitionSpec as P

NLON = 384
NLAT = 192
MMAX = 128
NSUB = 4
NCRM = 32
LEVELS = 28
BAND = 12
LONS = 96
COLS = BAND * LONS
ROWS = LEVELS * BAND
TARGETS = 64
PER = 18
NL = 16
NS = 4
NC = 4
RUNS = NL * PER
HALF = 4 * PER
TAIL = RUNS - 256
LEV_OWN = LEVELS // NC
SLOTS_OWN = MMAX // NL

F32 = jnp.float32
BF16 = jnp.bfloat16
VMEM = pl.BlockSpec(memory_space=pltpu.VMEM)
HBM = pl.BlockSpec(memory_space=pltpu.HBM)


def split2(x):
    hi = x.astype(BF16)
    lo = (x - hi.astype(F32)).astype(BF16)
    return hi, lo


def params(mib=16):
    return pltpu.CompilerParams(vmem_limit_bytes=mib << 20)


def lanes_of(shape):
    return lax.broadcasted_iota(jnp.int32, shape, 1)


def fill_one_hot(order_ref, hot_ref):
    order = order_ref[...]
    step = 96
    for c in range(0, COLS, step):
        ids = lax.broadcasted_iota(jnp.int32, (step, COLS), 0) + c
        hot_ref[c : c + step, :] = jnp.where(ids == order, 1.0, 0.0).astype(BF16)


def trig_rows(orders, trig_ref):
    first = (lax.axis_index("col") * LONS).astype(F32)
    y = lax.broadcasted_iota(jnp.int32, (MMAX, 128), 1).astype(F32) + first
    product = y * orders
    phase = product - NLON * jnp.floor((product + 0.5) * (1.0 / NLON))
    turn = jnp.floor((phase + 48.5) * (1.0 / 96.0))
    x = (phase - 96.0 * turn) * (2.0 * math.pi / NLON)
    z = x * x
    sin = x * (1.0 + z * (-1.0 / 6 + z * (1.0 / 120 + z * (-1.0 / 5040 + z * (1.0 / 362880)))))
    cos = 1.0 + z * (-0.5 + z * (1.0 / 24 + z * (-1.0 / 720 + z * (1.0 / 40320))))
    odd = (turn == 1.0) | (turn == 3.0)
    cos_out = jnp.where(odd, sin, cos)
    sin_out = jnp.where(odd, cos, sin)
    cos_out = jnp.where((turn == 1.0) | (turn == 2.0), -cos_out, cos_out)
    sin_out = jnp.where((turn == 2.0) | (turn == 3.0), -sin_out, sin_out)
    norm = 1.0 / math.sqrt(NLON)
    halves = [
        part.reshape(NL, 2, 4, 128)[:, h].reshape(NL * 4, 128)
        for part in (cos_out * norm, sin_out * norm)
        for h in range(2)
    ]
    hi, lo = split2(jnp.concatenate(halves, axis=0))
    trig_ref[:, 0:128] = hi
    trig_ref[:, 128:256] = hi
    trig_ref[:, 256:384] = lo


def legendre_rows(order, geom_ref, poly_ref, weight_ref):
    lane = lanes_of((SLOTS_OWN, 128)).astype(F32)
    head = jnp.sum(jnp.where(lane == order, geom_ref[3:4, 0:128], 0.0), axis=1, keepdims=True)
    degree = lax.broadcasted_iota(jnp.int32, (SLOTS_OWN, 128), 1).astype(F32)
    active = degree > order
    numer = jnp.where(active, 4.0 * degree * degree - 1.0, 0.0)
    denom = jnp.where(active, degree * degree - order * order, 1.0)
    grow = jnp.sqrt(numer / denom)
    lower = degree - 1.0
    retreat = jnp.sqrt(
        jnp.maximum(lower * lower - order * order, 0.0) / (4.0 * lower * lower - 1.0)
    )
    retreat = grow * retreat
    begin = jnp.where(degree == order, 1.0, 0.0)
    diagonal = jnp.exp(head + order[:, 0:1] * geom_ref[1:2, :])
    weight = geom_ref[2:3, :]
    cosine = jnp.broadcast_to(geom_ref[0:1, :], (SLOTS_OWN, 256))
    previous = jnp.zeros((SLOTS_OWN, 256), F32)
    current = previous
    for n in range(MMAX):
        fresh = (grow[:, n : n + 1] * cosine) * current + (
            begin[:, n : n + 1] * diagonal - retreat[:, n : n + 1] * previous
        )
        poly_ref[0, n * 8 : n * 8 + 8, :] = fresh[:, :128] * weight[:, :128]
        poly_ref[1, n * 8 : n * 8 + 8, :] = fresh[:, 128:] * weight[:, 128:]
        previous, current = current, fresh
    for s in range(SLOTS_OWN):
        for h in range(2):
            hi, lo = split2(poly_ref[h, pl.ds(s, MMAX, stride=8), :])
            size = min(128, NLAT - h * 128)
            for part, base in ((hi, 0), (lo, NLAT)):
                at = base + h * 128
                weight_ref[s, :, at : at + size] = part[:, :size]


def arrange_moisture(moist_ref, level_ref, water_ref, tail_ref):
    lane = lanes_of((8, 128))
    blank = jnp.zeros((NCRM, 384 - RUNS), F32)
    for k in range(LEVELS):
        level = jnp.concatenate((moist_ref[k].astype(F32), blank), axis=1)
        for v in range(3):
            level_ref[k, v] = level[:, v * 128 : v * 128 + 128]
    for k in range(LEVELS):
        for v in range(2):
            for n in range(4):
                water_ref[k, v, n] = level_ref[k, v, pl.ds(n, 8, stride=4), :]
    for g in range(LEVELS // 4):
        for n in range(4):
            tile = level_ref[4 * g, 2, pl.ds(n, 8, stride=4), :]
            for kk in range(1, 4):
                more = pltpu.roll(level_ref[4 * g + kk, 2, pl.ds(n, 8, stride=4), :], kk * TAIL, 1)
                tile = jnp.where(lane >= kk * TAIL, more, tile)
            tail_ref[g, n] = tile


def table_kernel(
    wave_hbm,
    geom_hbm,
    order_hbm,
    moist_hbm,
    trig_ref,
    weight_ref,
    water_ref,
    tail_ref,
    column_ref,
    wave_ref,
    geom_ref,
    order_ref,
    moist_ref,
    poly_ref,
    orders_ref,
    level_ref,
    sems,
):
    pairs = (
        (wave_hbm, wave_ref),
        (geom_hbm, geom_ref),
        (order_hbm, order_ref),
        (moist_hbm, moist_ref),
    )
    loads = [pltpu.make_async_copy(src, dst, sems.at[n]) for n, (src, dst) in enumerate(pairs)]
    for load in loads:
        load.start()
    for load in loads[:3]:
        load.wait()
    orders = jnp.broadcast_to(wave_ref[...].astype(F32), (MMAX, MMAX)).T
    orders_ref[...] = orders
    trig_rows(orders, trig_ref)
    first = pl.multiple_of(lax.axis_index("lat") * SLOTS_OWN, SLOTS_OWN)
    legendre_rows(orders_ref[pl.ds(first, SLOTS_OWN), :], geom_ref, poly_ref, weight_ref)
    order = order_ref[...].astype(F32)
    for v in range(COLS // 128):
        at = slice(v * 128, v * 128 + 128)
        column_ref[at, :] = jnp.broadcast_to(order[:, at], (128, 128)).T
    loads[3].wait()
    arrange_moisture(moist_ref, level_ref, water_ref, tail_ref)


def pack_kernel(
    state_hbm,
    force_hbm,
    order_hbm,
    out_hbm,
    cols_ref,
    state_ref,
    force_ref,
    order_ref,
    hot_ref,
    out_ref,
    sems,
):
    pairs = ((order_hbm, order_ref), (state_hbm, state_ref), (force_hbm, force_ref))
    loads = [pltpu.make_async_copy(src, dst, sems.at[n]) for n, (src, dst) in enumerate(pairs)]
    for load in loads:
        load.start()
    loads[0].wait()
    fill_one_hot(order_ref, hot_ref)
    loads[1].wait()
    loads[2].wait()
    for ref, base in ((state_ref, 0), (force_ref, LEVELS)):
        rows = ref[...].reshape(LEVELS, BAND, LONS)
        for b in range(BAND):
            cols_ref[base : base + LEVELS, b * LONS : (b + 1) * LONS] = rows[:, b, :]
    hi, lo = split2(cols_ref[...])
    both = jnp.concatenate((hi, lo), axis=0)
    got = jnp.dot(both, hot_ref[...], preferred_element_type=F32)
    got = got[: 2 * LEVELS] + got[2 * LEVELS :]
    lane = lanes_of((8, 128))
    groups = 2 * LEVELS // 8
    for t in range(TARGETS):
        v, off = divmod(t * PER, 128)
        tile = None
        for q in range(groups):
            src = got[q * 8 : q * 8 + 8, v * 128 : v * 128 + 128]
            if off + PER > 128:
                nxt = got[q * 8 : q * 8 + 8, v * 128 + 128 : v * 128 + 256]
                src = jnp.where(lane < off, nxt, src)
            shift = (q * PER - off) % 128
            if shift:
                src = pltpu.roll(src, shift, 1)
            tile = src if tile is None else jnp.where(lane >= q * PER, src, tile)
        out_ref[t] = tile
    save = pltpu.make_async_copy(out_ref, out_hbm, sems.at[3])
    save.start()
    save.wait()


def gather_lanes(tile_of, q_list, first, count, width, store):
    lane = lanes_of((8, 128))
    for q in q_list:
        for v in range(pl.cdiv(width, 128)):
            acc = None
            for i in range(count):
                start = i * PER - v * 128
                if start >= 128 or start + PER <= 0:
                    continue
                src = tile_of(first + i)
                shift = (i * PER - q * PER) % 128
                if shift:
                    src = pltpu.roll(src, shift, 1)
                acc = src if acc is None else jnp.where(lane >= start, src, acc)
            store(q, v, acc)


def coefficients(wind):
    courant = 0.4 * jnp.tanh(wind)
    mixing = 0.2 + 0.5 * jnp.abs(courant)
    return mixing - 0.5 * courant, mixing + 0.5 * courant


def cloud_tile(start, push, ahead, behind, water):
    keep = 1.0 - (ahead + behind)
    gap = [start + w for w in water]
    wet = [jnp.maximum(g, 0.0) for g in gap]
    total = (wet[0] + wet[1]) + (wet[2] + wet[3])
    for _ in range(NSUB - 1):
        up = gap[1:] + [pltpu.roll(gap[0], 7, 0)]
        down = [pltpu.roll(gap[3], 1, 0)] + gap[:3]
        gap = [
            ((keep * gap[n] - wet[n]) + push) + (ahead * up[n] + behind * down[n]) for n in range(4)
        ]
        wet = [jnp.maximum(g, 0.0) for g in gap]
        total = total + ((wet[0] + wet[1]) + (wet[2] + wet[3]))
    return jnp.sum(total, axis=0, keepdims=True) * (0.5 / NCRM)


def cloud_kernel(
    got_ref,
    water_ref,
    tail_ref,
    out_ref,
    wind_ref,
    diff_ref,
    push_ref,
    left_ref,
    right_ref,
    rain_ref,
    last_ref,
):
    def store_wind(q, v, x):
        wind_ref[v, q * 8 : q * 8 + 8, :] = x

    def store_diff(q, v, x):
        diff_ref[v, q * 8 : q * 8 + 8, :] = x

    gather_lanes(lambda i: got_ref[i], range(4), 0, NL, RUNS, store_wind)
    cache = {}

    def diff(i):
        if i not in cache:
            cache[i] = got_ref[3 * NL + i] - got_ref[2 * NL + i]
        return cache[i]

    gather_lanes(diff, range(7), 0, NL, RUNS, store_diff)
    lane = lanes_of((8, 128))
    groups = LEVELS // 4

    def tails(ref, base):
        tile = ref[2, pl.ds(base, 8, stride=4), :]
        for kk in range(1, 4):
            more = pltpu.roll(ref[2, pl.ds(base + kk, 8, stride=4), :], kk * TAIL, 1)
            tile = jnp.where(lane >= kk * TAIL, more, tile)
        return tile

    wind_tail = tails(wind_ref, 0)
    diff_tail = tails(diff_ref, 0)
    push_tail = tails(diff_ref, LEVELS) * (1.0 / NSUB)
    for v in range(2):
        left_ref[v], right_ref[v] = coefficients(wind_ref[v])
        push_ref[v] = diff_ref[v, LEVELS : LEVELS + 32, :] * (1.0 / NSUB)
    last_ref[4] = jnp.zeros_like(diff_tail)
    last_ref[0] = diff_tail
    last_ref[1] = push_tail
    last_ref[2], last_ref[3] = coefficients(wind_tail)
    rain_ref[...] = jnp.zeros_like(rain_ref)

    def level(g, carry):
        for kk in range(4):
            k = 4 * g + kk
            for v in range(2):

                def row(ref):
                    return jnp.broadcast_to(ref[v, pl.ds(k, 1), :], (8, 128))

                rain_ref[v, pl.ds(k, 1), :] = cloud_tile(
                    row(diff_ref),
                    row(push_ref),
                    row(left_ref),
                    row(right_ref),
                    [water_ref[k, v, n] for n in range(4)],
                )
        rows = [jnp.broadcast_to(last_ref[c, pl.ds(g, 1), :], (8, 128)) for c in range(4)]
        last_ref[4, pl.ds(g, 1), :] = cloud_tile(*rows, [tail_ref[g, n] for n in range(4)])
        return carry

    lax.fori_loop(0, groups, level, 0)
    rain_tail = last_ref[4]
    for kk in range(4):
        piece = rain_tail if kk == 0 else pltpu.roll(rain_tail, 128 - kk * TAIL, 1)
        rain_ref[2, pl.ds(kk, 8, stride=4), :] = piece
    for i in range(NL):
        v, off = divmod(i * PER, 128)
        tile = None
        for q in range(4):
            src = rain_ref[v, q * 8 : q * 8 + 8, :]
            if off + PER > 128:
                nxt = rain_ref[v + 1, q * 8 : q * 8 + 8, :]
                src = jnp.where(lane < off, nxt, src)
            shift = (q * PER - off) % 128
            if shift:
                src = pltpu.roll(src, shift, 1)
            tile = src if tile is None else jnp.where(lane >= q * PER, src, tile)
        low = tile[0:4]
        high = pltpu.roll(tile, HALF, 1)[4:8]
        tile = jnp.where(lane[0:4] < HALF, low, high)
        for s in range(NS):
            out_ref[s * NL + i] = tile


def update_kernel(
    got_ref,
    column_ref,
    cols_ref,
    trig_ref,
    out_ref,
    four_ref,
    slots_ref,
    rows_ref,
    hot_ref,
):
    lane = lanes_of((128, 128)).astype(F32)
    for v in range(COLS // 128):
        rows = slice(v * 128, v * 128 + 128)
        column = column_ref[rows, :]
        for c in range(COLS // 128):
            hot = jnp.where(lane + float(c * 128) == column, 1.0, 0.0)
            hot_ref[rows, c * 128 : c * 128 + 128] = hot.astype(BF16)

    def store(q, v, x):
        slots_ref[q * 8 : q * 8 + 8, v * 128 : v * 128 + 128] = x

    cache = {}

    def tile_of(t):
        if t not in cache:
            tile = got_ref[t]
            cache[t] = jnp.concatenate((tile, pltpu.roll(tile, 128 - HALF, 1)), axis=0)
        return cache[t]

    gather_lanes(tile_of, range(4), 0, TARGETS, COLS, store)
    hi, lo = split2(slots_ref[...])
    both = jnp.concatenate((hi, lo), axis=0)
    back = jnp.dot(both, hot_ref[...], preferred_element_type=F32)
    rain = back[:LEVELS] + back[32 : 32 + LEVELS]
    sec = lax.axis_index("sec")
    add = jnp.where(sec == 2, 1.0, jnp.where(sec == 3, -1.0, 0.0)).astype(F32)
    scale = jnp.where(sec < 2, -1.0 / NSUB, 0.0).astype(F32)
    now = cols_ref[0:LEVELS]
    now = now + (cols_ref[LEVELS : 2 * LEVELS] + rain * (add + scale * now))
    blank = jnp.zeros((LEVELS, 128 - LONS), F32)
    for b in range(BAND):
        piece = jnp.concatenate((now[:, b * LONS : (b + 1) * LONS], blank), axis=1)
        rows_ref[pl.ds(b, LEVELS, stride=BAND), :] = piece
    rows = rows_ref[0:ROWS, :]
    out_ref[...] = rows[:, :LONS].reshape(ROWS, 1, LONS)
    hi, lo = split2(rows)
    dims = (((1,), (1,)), ((), ()))
    parts = jnp.concatenate((hi, lo, hi), axis=1)
    out = lax.dot_general(trig_ref[...], parts, dims, preferred_element_type=F32)
    width = LEV_OWN * BAND
    blank = jnp.zeros((NL * 4, 384 - 4 * width), F32)
    for j in range(NC):
        pieces = [out[g * 64 : g * 64 + 64, j * width : (j + 1) * width] for g in range(4)]
        four_ref[j] = jnp.concatenate(pieces + [blank], axis=1).reshape(NL, 4, 384)


def legendre_kernel(
    got_ref, weight_ref, state_ref, out_hbm, state_hbm, band_ref, out_ref, sems
):
    saves = [pltpu.make_async_copy(state_ref, state_hbm, sems.at[2])]
    saves[0].start()
    width = LEV_OWN * BAND
    band_ref[1] = jnp.zeros_like(band_ref[1])
    for i in range(NL):
        part = (got_ref[0, i] + got_ref[1, i]) + (got_ref[2, i] + got_ref[3, i])
        bands = jnp.concatenate([part[:, g * width : (g + 1) * width] for g in range(4)], axis=0)
        h, at = divmod(i * BAND, 128)
        first = min(BAND, 128 - at)
        for k in range(LEV_OWN):
            row = slice(k * 16, k * 16 + 16)
            piece = bands[:, k * BAND : (k + 1) * BAND]
            band_ref[h, row, at : at + first] = piece[:, :first]
            if first < BAND:
                band_ref[h + 1, row, 0 : BAND - first] = piece[:, first:]
    dims = (((1,), (1,)), ((), ()))
    for s in range(SLOTS_OWN):
        rows = [band_ref[h, pl.ds(s, 2 * LEV_OWN, stride=8), :] for h in range(2)]
        hi, lo = split2(jnp.concatenate(rows, axis=1)[:, :NLAT])
        parts = jnp.concatenate((hi, hi), axis=1)
        out = lax.dot_general(parts, weight_ref[s], dims, preferred_element_type=F32)
        out = out + lax.dot_general(lo, weight_ref[s, :, 0:NLAT], dims, preferred_element_type=F32)
        out_ref[:, s, :, :] = out.reshape(LEV_OWN, 2, MMAX)
        if s % 4 == 3:
            part = pl.ds(s - 3, 4)
            save = pltpu.make_async_copy(out_ref.at[:, part], out_hbm.at[:, part], sems.at[s // 4])
            save.start()
            saves.append(save)
    for save in saves:
        save.wait()


def geometry():
    theta = (np.arange(NLAT) + 0.5) * (math.pi / NLAT)
    sine = np.sin(theta)
    rows = np.zeros((4, 256))
    rows[0, :NLAT] = np.cos(theta)
    rows[1, :NLAT] = np.log(sine)
    rows[2, :NLAT] = sine / math.sqrt(NLAT)
    for m in range(MMAX):
        logs = math.lgamma(m + 1.5) - math.lgamma(1.5) - math.lgamma(m + 1.0)
        rows[3, m] = 0.5 * logs - 0.5 * math.log(2.0)
    return rows.astype(np.float32)


def call(kernel, out, specs, scratch=(), out_specs=None):
    return pl.pallas_call(
        kernel,
        out_shape=out,
        in_specs=specs,
        out_specs=out_specs or jax.tree.map(lambda _: VMEM, out),
        scratch_shapes=list(scratch),
        compiler_params=params(),
    )


def stay(x):
    return pltpu.with_memory_space_constraint(x, pltpu.HBM)


def shards(state, forcing, crm_moisture, cloud_order, wave_table):
    shape = jax.ShapeDtypeStruct
    state = state.transpose(0, 2, 3, 1, 4).reshape(ROWS, 1, LONS)
    forcing = forcing.transpose(0, 2, 3, 1, 4).reshape(ROWS, 1, LONS)
    moist = crm_moisture.transpose(0, 2, 3, 4, 1, 5).reshape(LEVELS, NCRM, RUNS)
    order = cloud_order.reshape(1, COLS)
    waves = wave_table.reshape(1, MMAX)
    outgoing, cols = call(
        pack_kernel,
        (shape((TARGETS, 8, 128), F32), shape((2 * LEVELS, COLS), F32)),
        [HBM] * 3,
        [
            pltpu.VMEM((ROWS, 1, LONS), F32),
            pltpu.VMEM((ROWS, 1, LONS), F32),
            pltpu.VMEM((1, COLS), jnp.int32),
            pltpu.VMEM((COLS, COLS), BF16),
            pltpu.VMEM((TARGETS, 8, 128), F32),
            pltpu.SemaphoreType.DMA((4,)),
        ],
        (HBM, VMEM),
    )(*(stay(x) for x in (state, forcing, order)))
    outgoing, waves = lax.optimization_barrier((outgoing, waves))
    arrived = lax.all_to_all(outgoing, ("sec", "lat"), split_axis=0, concat_axis=0, tiled=True)
    trig, weights, water, tail, column = call(
        table_kernel,
        (
            shape((2 * MMAX, 384), BF16),
            shape((SLOTS_OWN, MMAX, 2 * NLAT), BF16),
            shape((LEVELS, 2, 4, 8, 128), F32),
            shape((LEVELS // 4, 4, 8, 128), F32),
            shape((COLS, 128), F32),
        ),
        [HBM] * 4,
        [
            pltpu.VMEM((1, MMAX), jnp.int32),
            pltpu.VMEM((4, 256), F32),
            pltpu.VMEM((1, COLS), jnp.int32),
            pltpu.VMEM((LEVELS, NCRM, RUNS), BF16),
            pltpu.VMEM((2, MMAX * SLOTS_OWN, 128), F32),
            pltpu.VMEM((MMAX, 128), F32),
            pltpu.VMEM((LEVELS, 3, NCRM, 128), F32),
            pltpu.SemaphoreType.DMA((4,)),
        ],
    )(*(stay(x) for x in (waves, jnp.asarray(geometry()), order, moist)))
    arrived, trig = lax.optimization_barrier((arrived, trig))
    rain = call(
        cloud_kernel,
        shape((TARGETS, 4, 128), F32),
        [VMEM] * 3,
        [
            pltpu.VMEM((3, 32, 128), F32),
            pltpu.VMEM((3, 64, 128), F32),
            pltpu.VMEM((2, 32, 128), F32),
            pltpu.VMEM((2, 32, 128), F32),
            pltpu.VMEM((2, 32, 128), F32),
            pltpu.VMEM((3, 32, 128), F32),
            pltpu.VMEM((5, 8, 128), F32),
        ],
    )(arrived, water, tail)
    returned = lax.all_to_all(rain, ("sec", "lat"), split_axis=0, concat_axis=0, tiled=True)
    updated, fourier = call(
        update_kernel,
        (shape((ROWS, 1, LONS), F32), shape((NC, NL, 4, 384), F32)),
        [VMEM] * 4,
        [
            pltpu.VMEM((32, COLS), F32),
            pltpu.VMEM((32 * BAND, 128), F32),
            pltpu.VMEM((COLS, COLS), BF16),
        ],
    )(returned, column, cols, trig)
    bands = lax.all_to_all(
        fourier.reshape(NL * NC, 4, 384), ("col", "lat"), split_axis=0, concat_axis=0, tiled=True
    )
    spectral, updated = call(
        legendre_kernel,
        (shape((LEV_OWN, SLOTS_OWN, 2, MMAX), F32), shape((ROWS, 1, LONS), F32)),
        [VMEM] * 3,
        [
            pltpu.VMEM((2, 128, 128), F32),
            pltpu.VMEM((LEV_OWN, SLOTS_OWN, 2, MMAX), F32),
            pltpu.SemaphoreType.DMA((3,)),
        ],
        (HBM, HBM),
    )(bands.reshape(NC, NL, 4, 384), weights, updated)
    new_state = updated.reshape(1, LEVELS, BAND, 1, LONS).transpose(0, 3, 1, 2, 4)
    return new_state, spectral[None, None]


def solution(mesh):
    placed = (
        P(None, "sec", None, "lat", "col"),
        P(None, "sec", None, "lat", "col"),
        P(None, None, None, ("sec", "lat"), "col", None),
        P("col", "lat", None),
        P(),
    )
    return jax.shard_map(
        shards,
        mesh=mesh,
        in_specs=placed,
        out_specs=(P(None, "sec", None, "lat", "col"), P("sec", None, "col", "lat", None, None)),
        check_vma=False,
    )
```

```python
import math

import jax
import jax.numpy as jnp
import numpy as np
from jax import lax
from jax.experimental import pallas as pl
from jax.experimental.pallas import tpu as pltpu
from jax.sharding import PartitionSpec as P

NLON = 384
NLAT = 192
MMAX = 128
NSUB = 4
NCRM = 32
LEVELS = 28
BAND = 12
LONS = 96
COLS = BAND * LONS
ROWS = LEVELS * BAND
TARGETS = 64
PER = 18
NL = 16
NS = 4
NC = 4
RUNS = NL * PER
HALF = 4 * PER
TAIL = RUNS - 256
LEV_OWN = LEVELS // NC
SLOTS_OWN = MMAX // NL

F32 = jnp.float32
BF16 = jnp.bfloat16
VMEM = pl.BlockSpec(memory_space=pltpu.VMEM)
HBM = pl.BlockSpec(memory_space=pltpu.HBM)


def split2(x):
    hi = x.astype(BF16)
    lo = (x - hi.astype(F32)).astype(BF16)
    return hi, lo


def params(mib=16):
    return pltpu.CompilerParams(vmem_limit_bytes=mib << 20)


def lanes_of(shape):
    return lax.broadcasted_iota(jnp.int32, shape, 1)


def fill_one_hot(order_ref, hot_ref):
    order = order_ref[...]
    step = 96
    for c in range(0, COLS, step):
        ids = lax.broadcasted_iota(jnp.int32, (step, COLS), 0) + c
        hot_ref[c : c + step, :] = jnp.where(ids == order, 1.0, 0.0).astype(BF16)


def trig_rows(orders, trig_ref):
    first = (lax.axis_index("col") * LONS).astype(F32)
    y = lax.broadcasted_iota(jnp.int32, (MMAX, 128), 1).astype(F32) + first
    product = y * orders
    phase = product - NLON * jnp.floor((product + 0.5) * (1.0 / NLON))
    turn = jnp.floor((phase + 48.5) * (1.0 / 96.0))
    x = (phase - 96.0 * turn) * (2.0 * math.pi / NLON)
    z = x * x
    sin = x * (1.0 + z * (-1.0 / 6 + z * (1.0 / 120 + z * (-1.0 / 5040 + z * (1.0 / 362880)))))
    cos = 1.0 + z * (-0.5 + z * (1.0 / 24 + z * (-1.0 / 720 + z * (1.0 / 40320))))
    odd = (turn == 1.0) | (turn == 3.0)
    cos_out = jnp.where(odd, sin, cos)
    sin_out = jnp.where(odd, cos, sin)
    cos_out = jnp.where((turn == 1.0) | (turn == 2.0), -cos_out, cos_out)
    sin_out = jnp.where((turn == 2.0) | (turn == 3.0), -sin_out, sin_out)
    norm = 1.0 / math.sqrt(NLON)
    halves = [
        part.reshape(NL, 2, 4, 128)[:, h].reshape(NL * 4, 128)
        for part in (cos_out * norm, sin_out * norm)
        for h in range(2)
    ]
    hi, lo = split2(jnp.concatenate(halves, axis=0))
    trig_ref[:, 0:128] = hi
    trig_ref[:, 128:256] = hi
    trig_ref[:, 256:384] = lo


def legendre_rows(order, geom_ref, poly_ref, weight_ref):
    lane = lanes_of((SLOTS_OWN, 128)).astype(F32)
    head = jnp.sum(jnp.where(lane == order, geom_ref[3:4, 0:128], 0.0), axis=1, keepdims=True)
    degree = lax.broadcasted_iota(jnp.int32, (SLOTS_OWN, 128), 1).astype(F32)
    active = degree > order
    numer = jnp.where(active, 4.0 * degree * degree - 1.0, 0.0)
    denom = jnp.where(active, degree * degree - order * order, 1.0)
    grow = jnp.sqrt(numer / denom)
    lower = degree - 1.0
    retreat = jnp.sqrt(
        jnp.maximum(lower * lower - order * order, 0.0) / (4.0 * lower * lower - 1.0)
    )
    retreat = grow * retreat
    begin = jnp.where(degree == order, 1.0, 0.0)
    diagonal = jnp.exp(head + order[:, 0:1] * geom_ref[1:2, :])
    weight = geom_ref[2:3, :]
    cosine = jnp.broadcast_to(geom_ref[0:1, :], (SLOTS_OWN, 256))
    previous = jnp.zeros((SLOTS_OWN, 256), F32)
    current = previous
    for n in range(MMAX):
        fresh = (grow[:, n : n + 1] * cosine) * current + (
            begin[:, n : n + 1] * diagonal - retreat[:, n : n + 1] * previous
        )
        poly_ref[0, n * 8 : n * 8 + 8, :] = fresh[:, :128] * weight[:, :128]
        poly_ref[1, n * 8 : n * 8 + 8, :] = fresh[:, 128:] * weight[:, 128:]
        previous, current = current, fresh
    for s in range(SLOTS_OWN):
        for h in range(2):
            hi, lo = split2(poly_ref[h, pl.ds(s, MMAX, stride=8), :])
            size = min(128, NLAT - h * 128)
            for part, base in ((hi, 0), (lo, NLAT)):
                at = base + h * 128
                weight_ref[s, :, at : at + size] = part[:, :size]


def arrange_moisture(moist_ref, level_ref, water_ref, tail_ref):
    lane = lanes_of((8, 128))
    blank = jnp.zeros((NCRM, 384 - RUNS), F32)
    for k in range(LEVELS):
        level = jnp.concatenate((moist_ref[k].astype(F32), blank), axis=1)
        for v in range(3):
            level_ref[k, v] = level[:, v * 128 : v * 128 + 128]
    for k in range(LEVELS):
        for v in range(2):
            for n in range(4):
                water_ref[k, v, n] = level_ref[k, v, pl.ds(n, 8, stride=4), :]
    for g in range(LEVELS // 4):
        for n in range(4):
            tile = level_ref[4 * g, 2, pl.ds(n, 8, stride=4), :]
            for kk in range(1, 4):
                more = pltpu.roll(level_ref[4 * g + kk, 2, pl.ds(n, 8, stride=4), :], kk * TAIL, 1)
                tile = jnp.where(lane >= kk * TAIL, more, tile)
            tail_ref[g, n] = tile


def table_kernel(
    wave_hbm,
    geom_hbm,
    order_hbm,
    moist_hbm,
    trig_ref,
    weight_ref,
    water_ref,
    tail_ref,
    column_ref,
    wave_ref,
    geom_ref,
    order_ref,
    moist_ref,
    poly_ref,
    orders_ref,
    level_ref,
    sems,
):
    pairs = (
        (wave_hbm, wave_ref),
        (geom_hbm, geom_ref),
        (order_hbm, order_ref),
        (moist_hbm, moist_ref),
    )
    loads = [pltpu.make_async_copy(src, dst, sems.at[n]) for n, (src, dst) in enumerate(pairs)]
    for load in loads:
        load.start()
    for load in loads[:3]:
        load.wait()
    orders = jnp.broadcast_to(wave_ref[...].astype(F32), (MMAX, MMAX)).T
    orders_ref[...] = orders
    trig_rows(orders, trig_ref)
    first = pl.multiple_of(lax.axis_index("lat") * SLOTS_OWN, SLOTS_OWN)
    legendre_rows(orders_ref[pl.ds(first, SLOTS_OWN), :], geom_ref, poly_ref, weight_ref)
    order = order_ref[...].astype(F32)
    for v in range(COLS // 128):
        at = slice(v * 128, v * 128 + 128)
        column_ref[at, :] = jnp.broadcast_to(order[:, at], (128, 128)).T
    loads[3].wait()
    arrange_moisture(moist_ref, level_ref, water_ref, tail_ref)


def pack_kernel(
    state_hbm,
    force_hbm,
    order_hbm,
    out_hbm,
    cols_ref,
    state_ref,
    force_ref,
    order_ref,
    hot_ref,
    out_ref,
    sems,
):
    pairs = ((order_hbm, order_ref), (state_hbm, state_ref), (force_hbm, force_ref))
    loads = [pltpu.make_async_copy(src, dst, sems.at[n]) for n, (src, dst) in enumerate(pairs)]
    for load in loads:
        load.start()
    loads[0].wait()
    fill_one_hot(order_ref, hot_ref)
    loads[1].wait()
    loads[2].wait()
    for ref, base in ((state_ref, 0), (force_ref, LEVELS)):
        rows = ref[...].reshape(LEVELS, BAND, LONS)
        for b in range(BAND):
            cols_ref[base : base + LEVELS, b * LONS : (b + 1) * LONS] = rows[:, b, :]
    hi, lo = split2(cols_ref[...])
    both = jnp.concatenate((hi, lo), axis=0)
    got = jnp.dot(both, hot_ref[...], preferred_element_type=F32)
    got = got[: 2 * LEVELS] + got[2 * LEVELS :]
    lane = lanes_of((8, 128))
    wide = lanes_of((8, COLS)).astype(F32)
    window = jnp.floor((wide + 0.5) * (1.0 / PER))
    even = window - 2.0 * jnp.floor(window * 0.5) == 0.0
    groups = [got[q * 8 : q * 8 + 8] for q in range(2 * LEVELS // 8)]
    paired = []
    for parity in range(2):
        here = even if parity == 0 else ~even
        rows = [
            jnp.where(here, groups[q], pltpu.roll(groups[q + 1], PER, 1)) for q in range(0, 6, 2)
        ]
        paired.append(rows + [groups[6]])
    for t in range(TARGETS):
        v, off = divmod(t * PER, 128)
        tile = None
        for p, row in enumerate(paired[t % 2]):
            span = PER if p == 3 else 2 * PER
            src = row[:, v * 128 : v * 128 + 128]
            if off + span > 128:
                w = (v + 1) % (COLS // 128)
                src = jnp.where(lane < off, row[:, w * 128 : w * 128 + 128], src)
            shift = (2 * p * PER - off) % 128
            if shift:
                src = pltpu.roll(src, shift, 1)
            tile = src if tile is None else jnp.where(lane >= 2 * p * PER, src, tile)
        out_ref[t] = tile
    save = pltpu.make_async_copy(out_ref, out_hbm, sems.at[3])
    save.start()
    save.wait()


def gather_lanes(tile_of, q_list, first, count, width, store):
    lane = lanes_of((8, 128))
    for q in q_list:
        for v in range(pl.cdiv(width, 128)):
            acc = None
            for i in range(count):
                start = i * PER - v * 128
                if start >= 128 or start + PER <= 0:
                    continue
                src = tile_of(first + i)
                shift = (i * PER - q * PER) % 128
                if shift:
                    src = pltpu.roll(src, shift, 1)
                acc = src if acc is None else jnp.where(lane >= start, src, acc)
            store(q, v, acc)


def coefficients(wind):
    courant = 0.4 * jnp.tanh(wind)
    mixing = 0.2 + 0.5 * jnp.abs(courant)
    return mixing - 0.5 * courant, mixing + 0.5 * courant


def cloud_tile(start, push, ahead, behind, water):
    keep = 1.0 - (ahead + behind)
    gap = [start + w for w in water]
    wet = [jnp.maximum(g, 0.0) for g in gap]
    total = (wet[0] + wet[1]) + (wet[2] + wet[3])
    for _ in range(NSUB - 1):
        up = gap[1:] + [pltpu.roll(gap[0], 7, 0)]
        down = [pltpu.roll(gap[3], 1, 0)] + gap[:3]
        gap = [
            ((keep * gap[n] - wet[n]) + push) + (ahead * up[n] + behind * down[n]) for n in range(4)
        ]
        wet = [jnp.maximum(g, 0.0) for g in gap]
        total = total + ((wet[0] + wet[1]) + (wet[2] + wet[3]))
    return jnp.sum(total, axis=0, keepdims=True) * (0.5 / NCRM)


def cloud_kernel(
    got_ref,
    water_ref,
    tail_ref,
    out_ref,
    wind_ref,
    diff_ref,
    push_ref,
    left_ref,
    right_ref,
    rain_ref,
    last_ref,
):
    def store_wind(q, v, x):
        wind_ref[v, q * 8 : q * 8 + 8, :] = x

    def store_diff(q, v, x):
        diff_ref[v, q * 8 : q * 8 + 8, :] = x

    gather_lanes(lambda i: got_ref[i], range(4), 0, NL, RUNS, store_wind)
    cache = {}

    def diff(i):
        if i not in cache:
            cache[i] = got_ref[3 * NL + i] - got_ref[2 * NL + i]
        return cache[i]

    gather_lanes(diff, range(7), 0, NL, RUNS, store_diff)
    lane = lanes_of((8, 128))
    groups = LEVELS // 4

    def tails(ref, base):
        tile = ref[2, pl.ds(base, 8, stride=4), :]
        for kk in range(1, 4):
            more = pltpu.roll(ref[2, pl.ds(base + kk, 8, stride=4), :], kk * TAIL, 1)
            tile = jnp.where(lane >= kk * TAIL, more, tile)
        return tile

    wind_tail = tails(wind_ref, 0)
    diff_tail = tails(diff_ref, 0)
    push_tail = tails(diff_ref, LEVELS) * (1.0 / NSUB)
    for v in range(2):
        left_ref[v], right_ref[v] = coefficients(wind_ref[v])
        push_ref[v] = diff_ref[v, LEVELS : LEVELS + 32, :] * (1.0 / NSUB)
    last_ref[4] = jnp.zeros_like(diff_tail)
    last_ref[0] = diff_tail
    last_ref[1] = push_tail
    last_ref[2], last_ref[3] = coefficients(wind_tail)
    rain_ref[...] = jnp.zeros_like(rain_ref)

    def level(g, carry):
        for kk in range(4):
            k = 4 * g + kk
            for v in range(2):

                def row(ref):
                    return jnp.broadcast_to(ref[v, pl.ds(k, 1), :], (8, 128))

                rain_ref[v, pl.ds(k, 1), :] = cloud_tile(
                    row(diff_ref),
                    row(push_ref),
                    row(left_ref),
                    row(right_ref),
                    [water_ref[k, v, n] for n in range(4)],
                )
        rows = [jnp.broadcast_to(last_ref[c, pl.ds(g, 1), :], (8, 128)) for c in range(4)]
        last_ref[4, pl.ds(g, 1), :] = cloud_tile(*rows, [tail_ref[g, n] for n in range(4)])
        return carry

    lax.fori_loop(0, groups, level, 0)
    rain_tail = last_ref[4]
    for kk in range(4):
        piece = rain_tail if kk == 0 else pltpu.roll(rain_tail, 128 - kk * TAIL, 1)
        rain_ref[2, pl.ds(kk, 8, stride=4), :] = piece
    for i in range(NL):
        v, off = divmod(i * PER, 128)
        tile = None
        for q in range(4):
            src = rain_ref[v, q * 8 : q * 8 + 8, :]
            if off + PER > 128:
                nxt = rain_ref[v + 1, q * 8 : q * 8 + 8, :]
                src = jnp.where(lane < off, nxt, src)
            shift = (q * PER - off) % 128
            if shift:
                src = pltpu.roll(src, shift, 1)
            tile = src if tile is None else jnp.where(lane >= q * PER, src, tile)
        low = tile[0:4]
        high = pltpu.roll(tile, HALF, 1)[4:8]
        tile = jnp.where(lane[0:4] < HALF, low, high)
        for s in range(NS):
            out_ref[s * NL + i] = tile


def update_kernel(
    got_ref,
    column_ref,
    cols_ref,
    trig_ref,
    out_ref,
    four_ref,
    slots_ref,
    rows_ref,
    hot_ref,
):
    lane = lanes_of((128, 128)).astype(F32)
    for v in range(COLS // 128):
        rows = slice(v * 128, v * 128 + 128)
        column = column_ref[rows, :]
        block = jnp.floor((column + 0.5) * (1.0 / 128.0))
        same = jnp.where(column - 128.0 * block == lane, 1.0, 0.0).astype(BF16)
        block = block.astype(BF16)
        for c in range(COLS // 128):
            hot_ref[rows, c * 128 : c * 128 + 128] = jnp.where(block == c, same, jnp.zeros_like(same))

    def store(q, v, x):
        slots_ref[q * 8 : q * 8 + 8, v * 128 : v * 128 + 128] = x

    cache = {}

    def tile_of(t):
        if t not in cache:
            tile = got_ref[t]
            cache[t] = jnp.concatenate((tile, pltpu.roll(tile, 128 - HALF, 1)), axis=0)
        return cache[t]

    gather_lanes(tile_of, range(4), 0, TARGETS, COLS, store)
    hi, lo = split2(slots_ref[...])
    both = jnp.concatenate((hi, lo), axis=0)
    back = jnp.dot(both, hot_ref[...], preferred_element_type=F32)
    rain = back[:LEVELS] + back[32 : 32 + LEVELS]
    sec = lax.axis_index("sec")
    add = jnp.where(sec == 2, 1.0, jnp.where(sec == 3, -1.0, 0.0)).astype(F32)
    scale = jnp.where(sec < 2, -1.0 / NSUB, 0.0).astype(F32)
    now = cols_ref[0:LEVELS]
    now = now + (cols_ref[LEVELS : 2 * LEVELS] + rain * (add + scale * now))
    blank = jnp.zeros((LEVELS, 128 - LONS), F32)
    for b in range(BAND):
        piece = jnp.concatenate((now[:, b * LONS : (b + 1) * LONS], blank), axis=1)
        rows_ref[pl.ds(b, LEVELS, stride=BAND), :] = piece
    rows = rows_ref[0:ROWS, :]
    out_ref[...] = rows[:, :LONS].reshape(ROWS, 1, LONS)
    hi, lo = split2(rows)
    dims = (((1,), (1,)), ((), ()))
    parts = jnp.concatenate((hi, lo, hi), axis=1)
    out = lax.dot_general(trig_ref[...], parts, dims, preferred_element_type=F32)
    width = LEV_OWN * BAND
    blank = jnp.zeros((NL * 4, 384 - 4 * width), F32)
    for j in range(NC):
        pieces = [out[g * 64 : g * 64 + 64, j * width : (j + 1) * width] for g in range(4)]
        four_ref[j] = jnp.concatenate(pieces + [blank], axis=1).reshape(NL, 4, 384)


def legendre_kernel(
    got_ref, weight_ref, state_ref, out_hbm, state_hbm, band_ref, out_ref, sems
):
    saves = [pltpu.make_async_copy(state_ref, state_hbm, sems.at[2])]
    saves[0].start()
    width = LEV_OWN * BAND
    band_ref[1] = jnp.zeros_like(band_ref[1])
    for i in range(NL):
        part = (got_ref[0, i] + got_ref[1, i]) + (got_ref[2, i] + got_ref[3, i])
        bands = jnp.concatenate([part[:, g * width : (g + 1) * width] for g in range(4)], axis=0)
        h, at = divmod(i * BAND, 128)
        first = min(BAND, 128 - at)
        for k in range(LEV_OWN):
            row = slice(k * 16, k * 16 + 16)
            piece = bands[:, k * BAND : (k + 1) * BAND]
            band_ref[h, row, at : at + first] = piece[:, :first]
            if first < BAND:
                band_ref[h + 1, row, 0 : BAND - first] = piece[:, first:]
    dims = (((1,), (1,)), ((), ()))
    for s in range(SLOTS_OWN):
        rows = [band_ref[h, pl.ds(s, 2 * LEV_OWN, stride=8), :] for h in range(2)]
        hi, lo = split2(jnp.concatenate(rows, axis=1)[:, :NLAT])
        parts = jnp.concatenate((hi, hi), axis=1)
        out = lax.dot_general(parts, weight_ref[s], dims, preferred_element_type=F32)
        out = out + lax.dot_general(lo, weight_ref[s, :, 0:NLAT], dims, preferred_element_type=F32)
        out_ref[:, s, :, :] = out.reshape(LEV_OWN, 2, MMAX)
    saves.append(pltpu.make_async_copy(out_ref, out_hbm, sems.at[0]))
    saves[1].start()
    for save in saves:
        save.wait()


def geometry():
    theta = (np.arange(NLAT) + 0.5) * (math.pi / NLAT)
    sine = np.sin(theta)
    rows = np.zeros((4, 256))
    rows[0, :NLAT] = np.cos(theta)
    rows[1, :NLAT] = np.log(sine)
    rows[2, :NLAT] = sine / math.sqrt(NLAT)
    for m in range(MMAX):
        logs = math.lgamma(m + 1.5) - math.lgamma(1.5) - math.lgamma(m + 1.0)
        rows[3, m] = 0.5 * logs - 0.5 * math.log(2.0)
    return rows.astype(np.float32)


def call(kernel, out, specs, scratch=(), out_specs=None):
    return pl.pallas_call(
        kernel,
        out_shape=out,
        in_specs=specs,
        out_specs=out_specs or jax.tree.map(lambda _: VMEM, out),
        scratch_shapes=list(scratch),
        compiler_params=params(),
    )


def stay(x):
    return pltpu.with_memory_space_constraint(x, pltpu.HBM)


def shards(state, forcing, crm_moisture, cloud_order, wave_table):
    shape = jax.ShapeDtypeStruct
    state = state.transpose(0, 2, 3, 1, 4).reshape(ROWS, 1, LONS)
    forcing = forcing.transpose(0, 2, 3, 1, 4).reshape(ROWS, 1, LONS)
    moist = crm_moisture.transpose(0, 2, 3, 4, 1, 5).reshape(LEVELS, NCRM, RUNS)
    order = cloud_order.reshape(1, COLS)
    waves = wave_table.reshape(1, MMAX)
    outgoing, cols = call(
        pack_kernel,
        (shape((TARGETS, 8, 128), F32), shape((2 * LEVELS, COLS), F32)),
        [HBM] * 3,
        [
            pltpu.VMEM((ROWS, 1, LONS), F32),
            pltpu.VMEM((ROWS, 1, LONS), F32),
            pltpu.VMEM((1, COLS), jnp.int32),
            pltpu.VMEM((COLS, COLS), BF16),
            pltpu.VMEM((TARGETS, 8, 128), F32),
            pltpu.SemaphoreType.DMA((4,)),
        ],
        (HBM, VMEM),
    )(*(stay(x) for x in (state, forcing, order)))
    outgoing, waves = lax.optimization_barrier((outgoing, waves))
    arrived = lax.all_to_all(outgoing, ("sec", "lat"), split_axis=0, concat_axis=0, tiled=True)
    trig, weights, water, tail, column = call(
        table_kernel,
        (
            shape((2 * MMAX, 384), BF16),
            shape((SLOTS_OWN, MMAX, 2 * NLAT), BF16),
            shape((LEVELS, 2, 4, 8, 128), F32),
            shape((LEVELS // 4, 4, 8, 128), F32),
            shape((COLS, 128), F32),
        ),
        [HBM] * 4,
        [
            pltpu.VMEM((1, MMAX), jnp.int32),
            pltpu.VMEM((4, 256), F32),
            pltpu.VMEM((1, COLS), jnp.int32),
            pltpu.VMEM((LEVELS, NCRM, RUNS), BF16),
            pltpu.VMEM((2, MMAX * SLOTS_OWN, 128), F32),
            pltpu.VMEM((MMAX, 128), F32),
            pltpu.VMEM((LEVELS, 3, NCRM, 128), F32),
            pltpu.SemaphoreType.DMA((4,)),
        ],
    )(*(stay(x) for x in (waves, jnp.asarray(geometry()), order, moist)))
    arrived, trig = lax.optimization_barrier((arrived, trig))
    rain = call(
        cloud_kernel,
        shape((TARGETS, 4, 128), F32),
        [VMEM] * 3,
        [
            pltpu.VMEM((3, 32, 128), F32),
            pltpu.VMEM((3, 64, 128), F32),
            pltpu.VMEM((2, 32, 128), F32),
            pltpu.VMEM((2, 32, 128), F32),
            pltpu.VMEM((2, 32, 128), F32),
            pltpu.VMEM((3, 32, 128), F32),
            pltpu.VMEM((5, 8, 128), F32),
        ],
    )(arrived, water, tail)
    returned = lax.all_to_all(rain, ("sec", "lat"), split_axis=0, concat_axis=0, tiled=True)
    updated, fourier = call(
        update_kernel,
        (shape((ROWS, 1, LONS), F32), shape((NC, NL, 4, 384), F32)),
        [VMEM] * 4,
        [
            pltpu.VMEM((32, COLS), F32),
            pltpu.VMEM((32 * BAND, 128), F32),
            pltpu.VMEM((COLS, COLS), BF16),
        ],
    )(returned, column, cols, trig)
    bands = lax.all_to_all(
        fourier.reshape(NL * NC, 4, 384), ("col", "lat"), split_axis=0, concat_axis=0, tiled=True
    )
    spectral, updated = call(
        legendre_kernel,
        (shape((LEV_OWN, SLOTS_OWN, 2, MMAX), F32), shape((ROWS, 1, LONS), F32)),
        [VMEM] * 3,
        [
            pltpu.VMEM((2, 128, 128), F32),
            pltpu.VMEM((LEV_OWN, SLOTS_OWN, 2, MMAX), F32),
            pltpu.SemaphoreType.DMA((3,)),
        ],
        (HBM, HBM),
    )(bands.reshape(NC, NL, 4, 384), weights, updated)
    new_state = updated.reshape(1, LEVELS, BAND, 1, LONS).transpose(0, 3, 1, 2, 4)
    return new_state, spectral[None, None]


def solution(mesh):
    placed = (
        P(None, "sec", None, "lat", "col"),
        P(None, "sec", None, "lat", "col"),
        P(None, None, None, ("sec", "lat"), "col", None),
        P("col", "lat", None),
        P(),
    )
    return jax.shard_map(
        shards,
        mesh=mesh,
        in_specs=placed,
        out_specs=(P(None, "sec", None, "lat", "col"), P("sec", None, "col", "lat", None, None)),
        check_vma=False,
    )
```

```python
import math

import jax
import jax.numpy as jnp
import numpy as np
from jax import lax
from jax.experimental import pallas as pl
from jax.experimental.pallas import tpu as pltpu
from jax.sharding import PartitionSpec as P

NLON = 384
NLAT = 192
MMAX = 128
NSUB = 4
NCRM = 32
LEVELS = 28
BAND = 12
LONS = 96
COLS = BAND * LONS
ROWS = LEVELS * BAND
TARGETS = 64
PER = 18
NL = 16
NS = 4
NC = 4
RUNS = NL * PER
HALF = 4 * PER
TAIL = RUNS - 256
LEV_OWN = LEVELS // NC
SLOTS_OWN = MMAX // NL

F32 = jnp.float32
BF16 = jnp.bfloat16
VMEM = pl.BlockSpec(memory_space=pltpu.VMEM)
HBM = pl.BlockSpec(memory_space=pltpu.HBM)


def split2(x):
    hi = x.astype(BF16)
    lo = (x - hi.astype(F32)).astype(BF16)
    return hi, lo


def params(mib=16):
    return pltpu.CompilerParams(vmem_limit_bytes=mib << 20)


def lanes_of(shape):
    return lax.broadcasted_iota(jnp.int32, shape, 1)


def fill_one_hot(order_ref, hot_ref):
    order = order_ref[...]
    step = 96
    for c in range(0, COLS, step):
        ids = lax.broadcasted_iota(jnp.int32, (step, COLS), 0) + c
        hot_ref[c : c + step, :] = jnp.where(ids == order, 1.0, 0.0).astype(BF16)


def trig_rows(orders, trig_ref):
    first = (lax.axis_index("col") * LONS).astype(F32)
    y = lax.broadcasted_iota(jnp.int32, (MMAX, 128), 1).astype(F32) + first
    product = y * orders
    phase = product - NLON * jnp.floor((product + 0.5) * (1.0 / NLON))
    turn = jnp.floor((phase + 48.5) * (1.0 / 96.0))
    x = (phase - 96.0 * turn) * (2.0 * math.pi / NLON)
    z = x * x
    sin = x * (1.0 + z * (-1.0 / 6 + z * (1.0 / 120 + z * (-1.0 / 5040 + z * (1.0 / 362880)))))
    cos = 1.0 + z * (-0.5 + z * (1.0 / 24 + z * (-1.0 / 720 + z * (1.0 / 40320))))
    odd = (turn == 1.0) | (turn == 3.0)
    cos_out = jnp.where(odd, sin, cos)
    sin_out = jnp.where(odd, cos, sin)
    cos_out = jnp.where((turn == 1.0) | (turn == 2.0), -cos_out, cos_out)
    sin_out = jnp.where((turn == 2.0) | (turn == 3.0), -sin_out, sin_out)
    norm = 1.0 / math.sqrt(NLON)
    halves = [
        part.reshape(NL, 2, 4, 128)[:, h].reshape(NL * 4, 128)
        for part in (cos_out * norm, sin_out * norm)
        for h in range(2)
    ]
    hi, lo = split2(jnp.concatenate(halves, axis=0))
    trig_ref[:, 0:128] = hi
    trig_ref[:, 128:256] = hi
    trig_ref[:, 256:384] = lo


def legendre_rows(order, geom_ref, poly_ref, weight_ref):
    lane = lanes_of((SLOTS_OWN, 128)).astype(F32)
    head = jnp.sum(jnp.where(lane == order, geom_ref[3:4, 0:128], 0.0), axis=1, keepdims=True)
    degree = lax.broadcasted_iota(jnp.int32, (SLOTS_OWN, 128), 1).astype(F32)
    active = degree > order
    numer = jnp.where(active, 4.0 * degree * degree - 1.0, 0.0)
    denom = jnp.where(active, degree * degree - order * order, 1.0)
    grow = jnp.sqrt(numer / denom)
    lower = degree - 1.0
    retreat = jnp.sqrt(
        jnp.maximum(lower * lower - order * order, 0.0) / (4.0 * lower * lower - 1.0)
    )
    retreat = grow * retreat
    begin = jnp.where(degree == order, 1.0, 0.0)
    diagonal = jnp.exp(head + order[:, 0:1] * geom_ref[1:2, :])
    weight = geom_ref[2:3, :]
    cosine = jnp.broadcast_to(geom_ref[0:1, :], (SLOTS_OWN, 256))
    previous = jnp.zeros((SLOTS_OWN, 256), F32)
    current = previous
    for n in range(MMAX):
        fresh = (grow[:, n : n + 1] * cosine) * current + (
            begin[:, n : n + 1] * diagonal - retreat[:, n : n + 1] * previous
        )
        poly_ref[0, n * 8 : n * 8 + 8, :] = fresh[:, :128] * weight[:, :128]
        poly_ref[1, n * 8 : n * 8 + 8, :] = fresh[:, 128:] * weight[:, 128:]
        previous, current = current, fresh
    for s in range(SLOTS_OWN):
        for h in range(2):
            hi, lo = split2(poly_ref[h, pl.ds(s, MMAX, stride=8), :])
            size = min(128, NLAT - h * 128)
            for part, base in ((hi, 0), (lo, NLAT)):
                at = base + h * 128
                weight_ref[s, :, at : at + size] = part[:, :size]


def arrange_moisture(moist_ref, level_ref, water_ref, tail_ref):
    lane = lanes_of((8, 128))
    blank = jnp.zeros((NCRM, 384 - RUNS), F32)
    for k in range(LEVELS):
        level = jnp.concatenate((moist_ref[k].astype(F32), blank), axis=1)
        for v in range(3):
            level_ref[k, v] = level[:, v * 128 : v * 128 + 128]
    for k in range(LEVELS):
        for v in range(2):
            for n in range(4):
                water_ref[k, v, n] = level_ref[k, v, pl.ds(n, 8, stride=4), :]
    for g in range(LEVELS // 4):
        for n in range(4):
            tile = level_ref[4 * g, 2, pl.ds(n, 8, stride=4), :]
            for kk in range(1, 4):
                more = pltpu.roll(level_ref[4 * g + kk, 2, pl.ds(n, 8, stride=4), :], kk * TAIL, 1)
                tile = jnp.where(lane >= kk * TAIL, more, tile)
            tail_ref[g, n] = tile


def table_kernel(
    wave_hbm,
    geom_hbm,
    order_hbm,
    moist_hbm,
    trig_ref,
    weight_ref,
    water_ref,
    tail_ref,
    column_ref,
    wave_ref,
    geom_ref,
    order_ref,
    moist_ref,
    poly_ref,
    orders_ref,
    level_ref,
    sems,
):
    pairs = (
        (wave_hbm, wave_ref),
        (geom_hbm, geom_ref),
        (order_hbm, order_ref),
        (moist_hbm, moist_ref),
    )
    loads = [pltpu.make_async_copy(src, dst, sems.at[n]) for n, (src, dst) in enumerate(pairs)]
    for load in loads:
        load.start()
    for load in loads[:3]:
        load.wait()
    orders = jnp.broadcast_to(wave_ref[...].astype(F32), (MMAX, MMAX)).T
    orders_ref[...] = orders
    trig_rows(orders, trig_ref)
    first = pl.multiple_of(lax.axis_index("lat") * SLOTS_OWN, SLOTS_OWN)
    legendre_rows(orders_ref[pl.ds(first, SLOTS_OWN), :], geom_ref, poly_ref, weight_ref)
    order = order_ref[...].astype(F32)
    for v in range(COLS // 128):
        at = slice(v * 128, v * 128 + 128)
        column_ref[at, :] = jnp.broadcast_to(order[:, at], (128, 128)).T
    loads[3].wait()
    arrange_moisture(moist_ref, level_ref, water_ref, tail_ref)


def pack_kernel(
    state_hbm,
    force_hbm,
    order_hbm,
    out_hbm,
    cols_ref,
    state_ref,
    force_ref,
    order_ref,
    hot_ref,
    out_ref,
    sems,
):
    pairs = ((order_hbm, order_ref), (state_hbm, state_ref), (force_hbm, force_ref))
    loads = [pltpu.make_async_copy(src, dst, sems.at[n]) for n, (src, dst) in enumerate(pairs)]
    for load in loads:
        load.start()
    loads[0].wait()
    fill_one_hot(order_ref, hot_ref)
    loads[1].wait()
    loads[2].wait()
    for ref, base in ((state_ref, 0), (force_ref, LEVELS)):
        rows = ref[...].reshape(LEVELS, BAND, LONS)
        for b in range(BAND):
            cols_ref[base : base + LEVELS, b * LONS : (b + 1) * LONS] = rows[:, b, :]
    hi, lo = split2(cols_ref[...])
    both = jnp.concatenate((hi, lo), axis=0)
    got = jnp.dot(both, hot_ref[...], preferred_element_type=F32)
    got = got[: 2 * LEVELS] + got[2 * LEVELS :]
    lane = lanes_of((8, 128))
    wide = lanes_of((8, COLS)).astype(F32)
    window = jnp.floor((wide + 0.5) * (1.0 / PER))
    even = window - 2.0 * jnp.floor(window * 0.5) == 0.0
    groups = [got[q * 8 : q * 8 + 8] for q in range(2 * LEVELS // 8)]
    paired = []
    for parity in range(2):
        here = even if parity == 0 else ~even
        rows = [
            jnp.where(here, groups[q], pltpu.roll(groups[q + 1], PER, 1)) for q in range(0, 6, 2)
        ]
        paired.append(rows + [groups[6]])
    for t in range(TARGETS):
        v, off = divmod(t * PER, 128)
        tile = None
        for p, row in enumerate(paired[t % 2]):
            span = PER if p == 3 else 2 * PER
            src = row[:, v * 128 : v * 128 + 128]
            if off + span > 128:
                w = (v + 1) % (COLS // 128)
                src = jnp.where(lane < off, row[:, w * 128 : w * 128 + 128], src)
            shift = (2 * p * PER - off) % 128
            if shift:
                src = pltpu.roll(src, shift, 1)
            tile = src if tile is None else jnp.where(lane >= 2 * p * PER, src, tile)
        out_ref[t] = tile
    save = pltpu.make_async_copy(out_ref, out_hbm, sems.at[3])
    save.start()
    save.wait()


def gather_lanes(tile_of, q_list, first, count, width, store):
    lane = lanes_of((8, 128))
    for q in q_list:
        for v in range(pl.cdiv(width, 128)):
            acc = None
            for i in range(count):
                start = i * PER - v * 128
                if start >= 128 or start + PER <= 0:
                    continue
                src = tile_of(first + i)
                shift = (i * PER - q * PER) % 128
                if shift:
                    src = pltpu.roll(src, shift, 1)
                acc = src if acc is None else jnp.where(lane >= start, src, acc)
            store(q, v, acc)


def coefficients(wind):
    courant = 0.4 * jnp.tanh(wind)
    mixing = 0.2 + 0.5 * jnp.abs(courant)
    return mixing - 0.5 * courant, mixing + 0.5 * courant


def cloud_tile(start, push, ahead, behind, water):
    keep = 1.0 - (ahead + behind)
    gap = [start + w for w in water]
    wet = [jnp.maximum(g, 0.0) for g in gap]
    total = (wet[0] + wet[1]) + (wet[2] + wet[3])
    for _ in range(NSUB - 1):
        up = gap[1:] + [pltpu.roll(gap[0], 7, 0)]
        down = [pltpu.roll(gap[3], 1, 0)] + gap[:3]
        gap = [
            ((keep * gap[n] - wet[n]) + push) + (ahead * up[n] + behind * down[n]) for n in range(4)
        ]
        wet = [jnp.maximum(g, 0.0) for g in gap]
        total = total + ((wet[0] + wet[1]) + (wet[2] + wet[3]))
    return jnp.sum(total, axis=0, keepdims=True) * (0.5 / NCRM)


def cloud_kernel(
    got_ref,
    water_ref,
    tail_ref,
    out_ref,
    wind_ref,
    diff_ref,
    push_ref,
    left_ref,
    right_ref,
    rain_ref,
    last_ref,
):
    def store_wind(q, v, x):
        wind_ref[v, q * 8 : q * 8 + 8, :] = x

    def store_diff(q, v, x):
        diff_ref[v, q * 8 : q * 8 + 8, :] = x

    gather_lanes(lambda i: got_ref[i], range(4), 0, NL, RUNS, store_wind)
    cache = {}

    def diff(i):
        if i not in cache:
            cache[i] = got_ref[3 * NL + i] - got_ref[2 * NL + i]
        return cache[i]

    gather_lanes(diff, range(7), 0, NL, RUNS, store_diff)
    lane = lanes_of((8, 128))
    groups = LEVELS // 4

    def tails(ref, base):
        tile = ref[2, pl.ds(base, 8, stride=4), :]
        for kk in range(1, 4):
            more = pltpu.roll(ref[2, pl.ds(base + kk, 8, stride=4), :], kk * TAIL, 1)
            tile = jnp.where(lane >= kk * TAIL, more, tile)
        return tile

    wind_tail = tails(wind_ref, 0)
    diff_tail = tails(diff_ref, 0)
    push_tail = tails(diff_ref, LEVELS) * (1.0 / NSUB)
    for v in range(2):
        left_ref[v], right_ref[v] = coefficients(wind_ref[v])
        push_ref[v] = diff_ref[v, LEVELS : LEVELS + 32, :] * (1.0 / NSUB)
    last_ref[4] = jnp.zeros_like(diff_tail)
    last_ref[0] = diff_tail
    last_ref[1] = push_tail
    last_ref[2], last_ref[3] = coefficients(wind_tail)
    rain_ref[...] = jnp.zeros_like(rain_ref)

    def level(g, carry):
        for kk in range(4):
            k = 4 * g + kk
            for v in range(2):

                def row(ref):
                    return jnp.broadcast_to(ref[v, pl.ds(k, 1), :], (8, 128))

                rain_ref[v, pl.ds(k, 1), :] = cloud_tile(
                    row(diff_ref),
                    row(push_ref),
                    row(left_ref),
                    row(right_ref),
                    [water_ref[k, v, n] for n in range(4)],
                )
        rows = [jnp.broadcast_to(last_ref[c, pl.ds(g, 1), :], (8, 128)) for c in range(4)]
        last_ref[4, pl.ds(g, 1), :] = cloud_tile(*rows, [tail_ref[g, n] for n in range(4)])
        return carry

    for g in range(groups):
        level(g, 0)
    rain_tail = last_ref[4]
    for kk in range(4):
        piece = rain_tail if kk == 0 else pltpu.roll(rain_tail, 128 - kk * TAIL, 1)
        rain_ref[2, pl.ds(kk, 8, stride=4), :] = piece
    for i in range(NL):
        v, off = divmod(i * PER, 128)
        tile = None
        for q in range(4):
            src = rain_ref[v, q * 8 : q * 8 + 8, :]
            if off + PER > 128:
                nxt = rain_ref[v + 1, q * 8 : q * 8 + 8, :]
                src = jnp.where(lane < off, nxt, src)
            shift = (q * PER - off) % 128
            if shift:
                src = pltpu.roll(src, shift, 1)
            tile = src if tile is None else jnp.where(lane >= q * PER, src, tile)
        low = tile[0:4]
        high = pltpu.roll(tile, HALF, 1)[4:8]
        tile = jnp.where(lane[0:4] < HALF, low, high)
        for s in range(NS):
            out_ref[s * NL + i] = tile


def update_kernel(
    got_ref,
    column_ref,
    cols_ref,
    trig_ref,
    out_ref,
    four_ref,
    slots_ref,
    rows_ref,
    hot_ref,
):
    lane = lanes_of((128, 128)).astype(F32)
    for v in range(COLS // 128):
        rows = slice(v * 128, v * 128 + 128)
        column = column_ref[rows, :]
        block = jnp.floor((column + 0.5) * (1.0 / 128.0))
        same = jnp.where(column - 128.0 * block == lane, 1.0, 0.0).astype(BF16)
        block = block.astype(BF16)
        for c in range(COLS // 128):
            hot_ref[rows, c * 128 : c * 128 + 128] = jnp.where(block == c, same, jnp.zeros_like(same))

    def store(q, v, x):
        slots_ref[q * 8 : q * 8 + 8, v * 128 : v * 128 + 128] = x

    cache = {}

    def tile_of(t):
        if t not in cache:
            tile = got_ref[t]
            cache[t] = jnp.concatenate((tile, pltpu.roll(tile, 128 - HALF, 1)), axis=0)
        return cache[t]

    gather_lanes(tile_of, range(4), 0, TARGETS, COLS, store)
    hi, lo = split2(slots_ref[...])
    both = jnp.concatenate((hi, lo), axis=0)
    back = jnp.dot(both, hot_ref[...], preferred_element_type=F32)
    rain = back[:LEVELS] + back[32 : 32 + LEVELS]
    sec = lax.axis_index("sec")
    add = jnp.where(sec == 2, 1.0, jnp.where(sec == 3, -1.0, 0.0)).astype(F32)
    scale = jnp.where(sec < 2, -1.0 / NSUB, 0.0).astype(F32)
    now = cols_ref[0:LEVELS]
    now = now + (cols_ref[LEVELS : 2 * LEVELS] + rain * (add + scale * now))
    blank = jnp.zeros((LEVELS, 128 - LONS), F32)
    for b in range(BAND):
        piece = jnp.concatenate((now[:, b * LONS : (b + 1) * LONS], blank), axis=1)
        rows_ref[pl.ds(b, LEVELS, stride=BAND), :] = piece
    rows = rows_ref[0:ROWS, :]
    out_ref[...] = rows[:, :LONS].reshape(ROWS, 1, LONS)
    hi, lo = split2(rows)
    dims = (((1,), (1,)), ((), ()))
    parts = jnp.concatenate((hi, lo, hi), axis=1)
    out = lax.dot_general(trig_ref[...], parts, dims, preferred_element_type=F32)
    width = LEV_OWN * BAND
    blank = jnp.zeros((NL * 4, 384 - 4 * width), F32)
    for j in range(NC):
        pieces = [out[g * 64 : g * 64 + 64, j * width : (j + 1) * width] for g in range(4)]
        four_ref[j] = jnp.concatenate(pieces + [blank], axis=1).reshape(NL, 4, 384)


def legendre_kernel(
    got_ref, weight_ref, state_ref, out_hbm, state_hbm, band_ref, out_ref, sems
):
    saves = [pltpu.make_async_copy(state_ref, state_hbm, sems.at[2])]
    saves[0].start()
    width = LEV_OWN * BAND
    band_ref[1] = jnp.zeros_like(band_ref[1])
    for i in range(NL):
        part = (got_ref[0, i] + got_ref[1, i]) + (got_ref[2, i] + got_ref[3, i])
        bands = jnp.concatenate([part[:, g * width : (g + 1) * width] for g in range(4)], axis=0)
        h, at = divmod(i * BAND, 128)
        first = min(BAND, 128 - at)
        for k in range(LEV_OWN):
            row = slice(k * 16, k * 16 + 16)
            piece = bands[:, k * BAND : (k + 1) * BAND]
            band_ref[h, row, at : at + first] = piece[:, :first]
            if first < BAND:
                band_ref[h + 1, row, 0 : BAND - first] = piece[:, first:]
    dims = (((1,), (1,)), ((), ()))
    for s in range(SLOTS_OWN):
        rows = [band_ref[h, pl.ds(s, 2 * LEV_OWN, stride=8), :] for h in range(2)]
        hi, lo = split2(jnp.concatenate(rows, axis=1)[:, :NLAT])
        parts = jnp.concatenate((hi, hi), axis=1)
        out = lax.dot_general(parts, weight_ref[s], dims, preferred_element_type=F32)
        out = out + lax.dot_general(lo, weight_ref[s, :, 0:NLAT], dims, preferred_element_type=F32)
        out_ref[:, s, :, :] = out.reshape(LEV_OWN, 2, MMAX)
    saves.append(pltpu.make_async_copy(out_ref, out_hbm, sems.at[0]))
    saves[1].start()
    for save in saves:
        save.wait()


def geometry():
    theta = (np.arange(NLAT) + 0.5) * (math.pi / NLAT)
    sine = np.sin(theta)
    rows = np.zeros((4, 256))
    rows[0, :NLAT] = np.cos(theta)
    rows[1, :NLAT] = np.log(sine)
    rows[2, :NLAT] = sine / math.sqrt(NLAT)
    for m in range(MMAX):
        logs = math.lgamma(m + 1.5) - math.lgamma(1.5) - math.lgamma(m + 1.0)
        rows[3, m] = 0.5 * logs - 0.5 * math.log(2.0)
    return rows.astype(np.float32)


def call(kernel, out, specs, scratch=(), out_specs=None):
    return pl.pallas_call(
        kernel,
        out_shape=out,
        in_specs=specs,
        out_specs=out_specs or jax.tree.map(lambda _: VMEM, out),
        scratch_shapes=list(scratch),
        compiler_params=params(),
    )


def stay(x):
    return pltpu.with_memory_space_constraint(x, pltpu.HBM)


def shards(state, forcing, crm_moisture, cloud_order, wave_table):
    shape = jax.ShapeDtypeStruct
    state = state.transpose(0, 2, 3, 1, 4).reshape(ROWS, 1, LONS)
    forcing = forcing.transpose(0, 2, 3, 1, 4).reshape(ROWS, 1, LONS)
    moist = crm_moisture.transpose(0, 2, 3, 4, 1, 5).reshape(LEVELS, NCRM, RUNS)
    order = cloud_order.reshape(1, COLS)
    waves = wave_table.reshape(1, MMAX)
    outgoing, cols = call(
        pack_kernel,
        (shape((TARGETS, 8, 128), F32), shape((2 * LEVELS, COLS), F32)),
        [HBM] * 3,
        [
            pltpu.VMEM((ROWS, 1, LONS), F32),
            pltpu.VMEM((ROWS, 1, LONS), F32),
            pltpu.VMEM((1, COLS), jnp.int32),
            pltpu.VMEM((COLS, COLS), BF16),
            pltpu.VMEM((TARGETS, 8, 128), F32),
            pltpu.SemaphoreType.DMA((4,)),
        ],
        (HBM, VMEM),
    )(*(stay(x) for x in (state, forcing, order)))
    outgoing, waves = lax.optimization_barrier((outgoing, waves))
    arrived = lax.all_to_all(outgoing, ("sec", "lat"), split_axis=0, concat_axis=0, tiled=True)
    trig, weights, water, tail, column = call(
        table_kernel,
        (
            shape((2 * MMAX, 384), BF16),
            shape((SLOTS_OWN, MMAX, 2 * NLAT), BF16),
            shape((LEVELS, 2, 4, 8, 128), F32),
            shape((LEVELS // 4, 4, 8, 128), F32),
            shape((COLS, 128), F32),
        ),
        [HBM] * 4,
        [
            pltpu.VMEM((1, MMAX), jnp.int32),
            pltpu.VMEM((4, 256), F32),
            pltpu.VMEM((1, COLS), jnp.int32),
            pltpu.VMEM((LEVELS, NCRM, RUNS), BF16),
            pltpu.VMEM((2, MMAX * SLOTS_OWN, 128), F32),
            pltpu.VMEM((MMAX, 128), F32),
            pltpu.VMEM((LEVELS, 3, NCRM, 128), F32),
            pltpu.SemaphoreType.DMA((4,)),
        ],
    )(*(stay(x) for x in (waves, jnp.asarray(geometry()), order, moist)))
    arrived, trig = lax.optimization_barrier((arrived, trig))
    rain = call(
        cloud_kernel,
        shape((TARGETS, 4, 128), F32),
        [VMEM] * 3,
        [
            pltpu.VMEM((3, 32, 128), F32),
            pltpu.VMEM((3, 64, 128), F32),
            pltpu.VMEM((2, 32, 128), F32),
            pltpu.VMEM((2, 32, 128), F32),
            pltpu.VMEM((2, 32, 128), F32),
            pltpu.VMEM((3, 32, 128), F32),
            pltpu.VMEM((5, 8, 128), F32),
        ],
    )(arrived, water, tail)
    returned = lax.all_to_all(rain, ("sec", "lat"), split_axis=0, concat_axis=0, tiled=True)
    updated, fourier = call(
        update_kernel,
        (shape((ROWS, 1, LONS), F32), shape((NC, NL, 4, 384), F32)),
        [VMEM] * 4,
        [
            pltpu.VMEM((32, COLS), F32),
            pltpu.VMEM((32 * BAND, 128), F32),
            pltpu.VMEM((COLS, COLS), BF16),
        ],
    )(returned, column, cols, trig)
    bands = lax.all_to_all(
        fourier.reshape(NL * NC, 4, 384), ("col", "lat"), split_axis=0, concat_axis=0, tiled=True
    )
    spectral, updated = call(
        legendre_kernel,
        (shape((LEV_OWN, SLOTS_OWN, 2, MMAX), F32), shape((ROWS, 1, LONS), F32)),
        [VMEM] * 3,
        [
            pltpu.VMEM((2, 128, 128), F32),
            pltpu.VMEM((LEV_OWN, SLOTS_OWN, 2, MMAX), F32),
            pltpu.SemaphoreType.DMA((3,)),
        ],
        (HBM, HBM),
    )(bands.reshape(NC, NL, 4, 384), weights, updated)
    new_state = updated.reshape(1, LEVELS, BAND, 1, LONS).transpose(0, 3, 1, 2, 4)
    return new_state, spectral[None, None]


def solution(mesh):
    placed = (
        P(None, "sec", None, "lat", "col"),
        P(None, "sec", None, "lat", "col"),
        P(None, None, None, ("sec", "lat"), "col", None),
        P("col", "lat", None),
        P(),
    )
    return jax.shard_map(
        shards,
        mesh=mesh,
        in_specs=placed,
        out_specs=(P(None, "sec", None, "lat", "col"), P("sec", None, "col", "lat", None, None)),
        check_vma=False,
    )
```
